256 devices in a mesh: row: 64 (over y, z, core), col: 4 (over x).
Axes of the slice: x: 4, y: 4, z: 8, core: 2. Of those that a mesh axis runs over, the one named last changes fastest.
Arguments:
- features: bfloat16 [65536, 256], P('row', 'col'), may hold values from -600 to 600
- tile_vals: bfloat16 [10240, 128, 128], P('row'), may hold values from -0.125 to 0.125
- tile_rows: int32 [64, 160], P('row'), may hold values from 0 to 7
- tile_srcs: int32 [64, 160], P('row'), may hold values from 0 to 135, as said below
- tile_count: int32 [64], P('row'), may hold values from 20 to 160, as said below
- needed: int32 [64, 64, 2], P('row'), may hold values from 0 to 7, as said below
- hop_noise: float32 [2, 65536, 256], P(None, 'row', 'col'), may hold values from -0.24 to 0.24
- enc_weight: bfloat16 [3, 256, 256], replicated, may hold values from -3.59375 to 3.59375
Outputs:
- encoded: bfloat16 [65536, 256], P('row', 'col')
The draws below stay inside these ranges and needn't reach their ends.
Inputs may be any that keep to these rules, and one draw needn't show every extreme that they name: `tile_count`: some row index has exactly 160 live slots; slots at or beyond a row index's count are ignored. `tile_srcs`: A value s below 8 names the row index's own block s; otherwise s = 8 + o * 2 + c names entry c of needed for owner o, and o is never the row index itself. needed[d, o, :] are 2 distinct block indices among owner o's 8 blocks.
All inputs are finite; a program needn't handle non-finite values.
Results may differ from the reference program's by a relative error of at most 0.0053.
Values may be sent and summed in bfloat16 or wider, within the bound.
No kernel may reach another device: no remote copies, remote signals or barrier semaphores. Data moves between devices by JAX's collectives and lax.ppermute only.
A program may use at most 64 MiB of HBM per device.

```python
import jax
import jax.numpy as jnp
from jax import lax

F = 256
BLK = 128
BPD = 8
TPD = 160
CAP = 2
HOPS = 2
NODES = 65536
TILES = 10240
N_ROW = 64


def draw_features(key, part):
    first, second, third = jax.random.split(key, 3)
    columns = jnp.arange(F, dtype=jnp.float32)
    column_scale = 10.0 ** (columns / (F - 1)) * jnp.exp(jax.random.uniform(second, (F,), minval=-0.35, maxval=0.35))
    base = jnp.clip(jax.random.normal(first, (NODES, F)), -4.0, 4.0)
    row_scale = 10.0 ** jax.random.uniform(third, (NODES, 1))
    return (base * column_scale[None, :] * row_scale).astype(jnp.bfloat16)


def draw_tile_count(key, part):
    first, second = jax.random.split(jax.random.fold_in(key, 11))
    shifts = jax.random.randint(first, (N_ROW,), 0, 4)
    counts = TPD // 2 ** shifts
    busiest = jax.random.randint(second, (), 0, N_ROW)
    return jnp.where(jnp.arange(N_ROW) == busiest, TPD, counts).astype(jnp.int32)


def draw_tile_rows(key, part):
    return jax.random.randint(jax.random.fold_in(key, 12), (N_ROW, TPD), 0, BPD).astype(jnp.int32)


def draw_tile_srcs(key, part):
    first, second, third, fourth = jax.random.split(jax.random.fold_in(key, 13), 4)
    local = jax.random.randint(first, (N_ROW, TPD), 0, 3) == 0
    own_block = jax.random.randint(second, (N_ROW, TPD), 0, BPD)
    offset = jax.random.randint(third, (N_ROW, TPD), 1, N_ROW)
    owner = (jnp.arange(N_ROW)[:, None] + offset) % N_ROW
    slot = jax.random.randint(fourth, (N_ROW, TPD), 0, CAP)
    return jnp.where(local, own_block, BPD + owner * CAP + slot).astype(jnp.int32)


def draw_needed(key, part):
    scores = jax.random.randint(jax.random.fold_in(key, 14), (N_ROW, N_ROW, BPD), 0, 2 ** 20)
    scores = scores * BPD + jnp.arange(BPD)[None, None, :]
    order = jnp.argsort(scores, axis=-1, stable=True)
    return order[:, :, :CAP].astype(jnp.int32)


def steps_of(stream_key, shape, pieces, low, largest):
    def one(dim, blocks):
        draws = jax.random.uniform(jax.random.fold_in(jax.random.fold_in(stream_key, 6), dim), (blocks,), jnp.float32, low / len(pieces), largest / len(pieces))
        return jnp.repeat(jnp.exp(draws), shape[dim] // blocks).reshape((-1,) + (1,) * (len(shape) - dim - 1))

    level = one(*pieces[0])
    for cut in pieces[1:]:
        level = level * one(*cut)
    return level


def noise(rng, dims, deviation, most, cuts=(), kind=jnp.bfloat16):
    drawn = deviation * jax.random.normal(rng, dims, jnp.float32)
    if cuts:
        drawn = drawn * steps_of(rng, dims, cuts, -0.22, 0.18)
    return jnp.clip(drawn, -most, most).astype(kind)


def setup_inputs(seed: int = 0) -> dict:
    arg_keys = jax.random.split(jax.random.key(seed), 9)
    features = draw_features(jax.random.fold_in(arg_keys[8], 71), 0)
    tile_vals = noise(arg_keys[1], (TILES, BLK, BLK), (BLK * TPD // BPD) ** -0.5, 0.125, ((0, 64),))
    tile_rows = draw_tile_rows(jax.random.fold_in(arg_keys[8], 71), 0)
    tile_srcs = draw_tile_srcs(jax.random.fold_in(arg_keys[8], 71), 0)
    tile_count = draw_tile_count(jax.random.fold_in(arg_keys[8], 71), 0)
    needed = draw_needed(jax.random.fold_in(arg_keys[8], 71), 0)
    hop_noise = noise(arg_keys[6], (HOPS, NODES, F), 0.04, 0.24, ((1, 64), (2, 4)), jnp.float32)
    enc_weight = noise(arg_keys[7], (HOPS + 1, F, F), 0.6, 3.59375)
    return dict(features=features, tile_vals=tile_vals, tile_rows=tile_rows, tile_srcs=tile_srcs, tile_count=tile_count, needed=needed, hop_noise=hop_noise, enc_weight=enc_weight)


epsilon = 1e-06

def normalize(values):
    squares = lax.optimization_barrier(jnp.sum(values * values, axis=1, keepdims=True))
    return (values / jnp.sqrt(squares + epsilon)).astype(jnp.bfloat16)

def aggregate(previous, tile_vals, tile_rows, tile_srcs, tile_count, needed):
    blocks = previous.astype(jnp.float32).reshape(N_ROW * BPD, BLK, F)
    values = tile_vals.reshape(N_ROW, TPD, BLK, BLK)

    def one_device(device):
        sources = tile_srcs[device]
        remote = jnp.maximum(sources - BPD, 0)
        owner = (remote // CAP).astype(jnp.int32)
        slot = (remote % CAP).astype(jnp.int32)
        far_block = owner * BPD + needed[device][owner, slot]
        near_block = device * BPD + sources
        index = jnp.where(sources < BPD, near_block, far_block).astype(jnp.int32)
        picked = blocks[index]
        products = jnp.einsum('tij,tjf->tif', values[device].astype(jnp.float32), picked, precision=lax.Precision.HIGHEST)
        live = jnp.arange(TPD, dtype=jnp.int32) < tile_count[device]
        onehot = ((tile_rows[device][:, None] == jnp.arange(BPD, dtype=jnp.int32)[None, :]) & live[:, None]).astype(jnp.float32)
        return jnp.einsum('tr,tif->rif', onehot, products, precision=lax.Precision.HIGHEST)
    summed = lax.map(one_device, jnp.arange(N_ROW, dtype=jnp.int32))
    return summed.reshape(N_ROW * BPD * BLK, F)

def reference(features, tile_vals, tile_rows, tile_srcs, tile_count, needed, hop_noise, enc_weight):
    current = normalize(features.astype(jnp.float32))
    layers = [current]
    for hop_index in range(HOPS):
        gathered = aggregate(current, tile_vals, tile_rows, tile_srcs, tile_count, needed)
        current = normalize(gathered + hop_noise[hop_index])
        layers.append(current)
    stacked = jnp.stack(layers).astype(jnp.float32)
    encoded = jnp.einsum('kri,kio->ro', stacked, enc_weight.astype(jnp.float32), precision=lax.Precision.HIGHEST)
    return encoded.astype(jnp.bfloat16)
```

```python
import functools

import jax
import jax.numpy as jnp
import numpy as np
from jax import lax
from jax.experimental import pallas as pl
from jax.experimental.pallas import tpu as pltpu
from jax.sharding import Mesh, PartitionSpec as P

BLK = 128
BPD = 8
TPD = 160
PAIRS = BPD // 2
HOPS = 2
NY, NZ, NC, NX = 4, 8, 2, 4
WIDTH = 64
CHUNK = 16
GROUP = 4
EPS = 1e-06
bf16 = jnp.bfloat16
f32 = jnp.float32
VMEM = pltpu.VMEM
SMEM = pltpu.SMEM


def lane_low(shape):
    return lax.broadcasted_iota(jnp.int32, shape, len(shape) - 1) < WIDTH


def pair_squares(pair_values):
    total = jnp.zeros((BPD, BLK), f32)
    row = lax.broadcasted_iota(jnp.int32, (BPD, BLK), 0)
    half = lax.broadcasted_iota(jnp.int32, (BPD, BLK), 1) // WIDTH
    for p in range(PAIRS):
        v = pair_values[p]
        pick = jnp.where(row == 2 * p + half, 1.0, 0.0).astype(f32)
        total = total + lax.dot_general(
            pick, v * v, (((1,), (1,)), ((), ())),
            precision=lax.Precision.HIGHEST, preferred_element_type=f32,
        )
    return total


def row_scale(total):
    return (1.0 / jnp.sqrt(total + EPS)).T


def pair_scale(columns, p):
    return jnp.where(
        lane_low((BLK, BLK)),
        jnp.broadcast_to(columns[:, 2 * p : 2 * p + 1], (BLK, BLK)),
        jnp.broadcast_to(columns[:, 2 * p + 1 : 2 * p + 2], (BLK, BLK)),
    )


def swap_halves(v):
    return pltpu.roll(v, WIDTH, 1)


def join(low, high):
    return jnp.concatenate([low, high], axis=1)


def pack_kernel(feat_ref, out_ref, sq_ref):
    pairs = []
    for p in range(PAIRS):
        low = feat_ref[(2 * p) * BLK : (2 * p + 1) * BLK, :].astype(f32)
        high = feat_ref[(2 * p + 1) * BLK : (2 * p + 2) * BLK, :].astype(f32)
        pair = join(low, high)
        pairs.append(pair)
        for z in range(NZ):
            out_ref[z, p] = pair.astype(bf16)
    total = pair_squares(pairs)
    for i in range(NX * NZ):
        sq_ref[i] = total


def pick_kernel(me_ref, idx_ref, z_ref, sq_ref, out_ref, own_ref, norm):
    for z in range(NZ):
        total = sq_ref[z]
        for x in range(1, NX):
            total = total + sq_ref[x * NZ + z]
        columns = row_scale(total)
        for p in range(PAIRS):
            v = z_ref[z, p].astype(f32) * pair_scale(columns, p)
            norm[z, p] = v.astype(bf16)
            norm[z, PAIRS + p] = swap_halves(v).astype(bf16)
    own_ref[...] = norm[me_ref[0], 0:PAIRS]
    mask = lane_low((BLK, BLK))

    def body(i, carry):
        z = i % NZ
        first = idx_ref[2 * i]
        second = idx_ref[2 * i + 1]
        low = norm[z, first // 2 + PAIRS * (first % 2)]
        high = norm[z, second // 2 + PAIRS * (1 - second % 2)]
        out_ref[i] = jnp.where(mask, low, high)
        return carry

    lax.fori_loop(0, NY * NC * NZ, body, 0, unroll=2)


def tile_kernel(hop, rows_ref, srcs_ref, count_ref, tiles_ref, got_ref, own_ref, noise_ref, *rest):
    last = hop == HOPS - 1
    if last:
        out_ref, acc, tile_buf, src_buf, noise_buf, tile_sem, src_sem = rest
    else:
        out_ref, sq_ref, acc, tile_buf, src_buf, noise_buf, tile_sem, src_sem = rest
    count = count_ref[0]
    chunks = (count + CHUNK - 1) // CHUNK

    def tile_copy(c):
        return pltpu.make_async_copy(
            tiles_ref.at[pl.ds(c * CHUNK, CHUNK)], tile_buf.at[pl.ds(c * CHUNK, CHUNK)], tile_sem.at[c]
        )

    got_copy = pltpu.make_async_copy(got_ref, src_buf.at[pl.ds(0, NY * NC * NZ)], src_sem.at[0])
    own_copy = pltpu.make_async_copy(own_ref, src_buf.at[pl.ds(NY * NC * NZ, PAIRS)], src_sem.at[1])
    noise_copy = pltpu.make_async_copy(noise_ref.at[hop], noise_buf, src_sem.at[2])
    got_copy.start()
    own_copy.start()

    @pl.loop(0, chunks)
    def _(c):
        tile_copy(c).start()

    noise_copy.start()
    acc[...] = jnp.zeros_like(acc)
    got_copy.wait()
    own_copy.wait()

    def group(g, carry):
        @pl.when(g % (CHUNK // GROUP) == 0)
        def _():
            tile_copy(g // (CHUNK // GROUP)).wait()

        for j in range(GROUP):
            t = g * GROUP + j
            s = srcs_ref[t]
            o = (s - BPD) // 2
            y = o // (NZ * NC)
            z = (o // NC) % NZ
            k = o % NC
            slab = jnp.where(s < BPD, NY * NC * NZ + s // 2, (y * NC + k) * NZ + z)
            target = jnp.where(t < count, rows_ref[t] * 2 + s % 2, 2 * BPD)
            acc[target] += jnp.dot(tile_buf[t], src_buf[slab], preferred_element_type=f32)
        return carry

    lax.fori_loop(0, (count + GROUP - 1) // GROUP, group, 0)

    noise_copy.wait()
    mask = lane_low((BLK, BLK))
    pairs = []
    for p in range(PAIRS):
        noise = join(noise_buf[(2 * p) * BLK : (2 * p + 1) * BLK, :], noise_buf[(2 * p + 1) * BLK : (2 * p + 2) * BLK, :])
        u = noise + jnp.where(
            mask,
            acc[4 * p] + swap_halves(acc[4 * p + 1]),
            swap_halves(acc[4 * p + 2]) + acc[4 * p + 3],
        )
        pairs.append(u)
    total = pair_squares(pairs)
    if last:
        hi = total.astype(bf16).astype(f32)
        mid = (total - hi).astype(bf16).astype(f32)
        lo = total - hi - mid
        for x in range(NX):
            for p in range(PAIRS):
                out_ref[x, p * BLK : (p + 1) * BLK] = pairs[p].astype(bf16)
            out_ref[x, PAIRS * BLK : PAIRS * BLK + 16] = jnp.concatenate([hi, mid], axis=0).astype(bf16)
            out_ref[x, PAIRS * BLK + 16 : PAIRS * BLK + 32] = jnp.concatenate([lo, jnp.zeros_like(lo)], axis=0).astype(bf16)
    else:
        for p in range(PAIRS):
            for z in range(NZ):
                out_ref[z, p] = pairs[p].astype(bf16)
        for i in range(NX * NZ):
            sq_ref[i] = total


def early_kernel(h_ref, w_ref, out_ref):
    for p in range(PAIRS):
        total = jnp.zeros((BLK, BLK), f32)
        for k in range(HOPS):
            for x in range(NX):
                total = total + jnp.dot(h_ref[x, k, p], w_ref[k, x], preferred_element_type=f32)
        out_ref[p] = total


def final_kernel(got_ref, w_ref, early_ref, out_ref):
    total = jnp.zeros((BPD, BLK), f32)
    for x in range(NX):
        a = got_ref[x, PAIRS * BLK : PAIRS * BLK + 16].astype(f32)
        b = got_ref[x, PAIRS * BLK + 16 : PAIRS * BLK + 32].astype(f32)
        total = total + (a[:BPD] + a[BPD:] + b[:BPD])
    columns = row_scale(total)
    for p in range(PAIRS):
        raw = jnp.zeros((BLK, BLK), f32)
        for x in range(NX):
            raw = raw + jnp.dot(got_ref[x, p * BLK : (p + 1) * BLK], w_ref[HOPS, x], preferred_element_type=f32)
        v = early_ref[p] + raw * pair_scale(columns, p)
        out_ref[(2 * p) * BLK : (2 * p + 1) * BLK, :] = v[:, :WIDTH].astype(bf16)
        out_ref[(2 * p + 1) * BLK : (2 * p + 2) * BLK, :] = swap_halves(v)[:, :WIDTH].astype(bf16)


def whole(space=VMEM):
    return pl.BlockSpec(memory_space=space)


def call(kernel, name, in_specs, out_shape, scratch=(), limit=24 << 20, flops=1 << 20, moved=1 << 20, **kw):
    outs = jax.tree.map(lambda _: whole(), out_shape)
    return pl.pallas_call(
        kernel,
        name=name,
        out_shape=out_shape,
        in_specs=in_specs,
        out_specs=outs,
        scratch_shapes=list(scratch),
        compiler_params=pltpu.CompilerParams(vmem_limit_bytes=limit),
        cost_estimate=pl.CostEstimate(flops=flops, bytes_accessed=moved, transcendentals=0),
        **kw,
    )


def shape(dims, kind):
    return jax.ShapeDtypeStruct(dims, kind)


def shards(features, tile_vals, tile_rows, tile_srcs, tile_count, needed, hop_noise, enc_weight):
    z_index = lax.axis_index("z").astype(jnp.int32).reshape(1)
    x_index = lax.axis_index("x")

    packed, squares = call(
        pack_kernel, "pack", [whole()],
        (shape((NZ, PAIRS, BLK, BLK), bf16), shape((NX * NZ, BPD, BLK), f32)),
    )(features)
    wanted = needed.reshape(NY, NZ, NC, 2).transpose(0, 2, 1, 3).reshape(NY * NC, NZ * 2)
    wanted, packed = lax.optimization_barrier((wanted, packed))

    weights = lax.dynamic_slice_in_dim(enc_weight, x_index * WIDTH, WIDTH, axis=2).reshape(HOPS + 1, NX, WIDTH, WIDTH)
    nothing = jnp.zeros_like(weights)
    weights = jnp.concatenate(
        [jnp.concatenate([weights, nothing], axis=-1), jnp.concatenate([nothing, weights], axis=-1)], axis=-2
    )

    owned = []
    asked = None
    for hop in range(HOPS):
        last = hop == HOPS - 1
        along = lax.all_to_all(packed, "z", 0, 0, tiled=True)
        sums = lax.all_to_all(squares, ("x", "z"), 0, 0, tiled=True)
        if asked is None:
            asked = lax.all_to_all(wanted, ("y", "core"), 0, 0, tiled=True).reshape(-1)
        picked, own = call(
            pick_kernel, "pick", [whole(SMEM), whole(SMEM), whole(), whole()],
            (shape((NY * NC * NZ, BLK, BLK), bf16), shape((PAIRS, BLK, BLK), bf16)),
            [pltpu.VMEM((NZ, BPD, BLK, BLK), bf16)],
        )(z_index, asked, along, sums)
        owned.append(own)
        got = lax.all_to_all(picked, ("y", "core"), 0, 0, tiled=True)
        if last:
            both = jnp.stack(owned)
            spread = lax.all_to_all(
                jnp.broadcast_to(both[None], (NX,) + both.shape), "x", 0, 0, tiled=True
            )
            early = call(early_kernel, "early", [whole(), whole()], shape((PAIRS, BLK, BLK), f32))(spread, weights)
        scratch = [
            pltpu.VMEM((2 * BPD + 1, BLK, BLK), f32),
            pltpu.VMEM((TPD, BLK, BLK), bf16),
            pltpu.VMEM((NY * NC * NZ + PAIRS, BLK, BLK), bf16),
            pltpu.VMEM((BPD * BLK, WIDTH), f32),
            pltpu.SemaphoreType.DMA((TPD // CHUNK,)),
            pltpu.SemaphoreType.DMA((3,)),
        ]
        if last:
            outs = shape((NX, PAIRS * BLK + 32, BLK), bf16)
        else:
            outs = (
                shape((NZ, PAIRS, BLK, BLK), bf16),
                shape((NX * NZ, BPD, BLK), f32),
            )
        specs = [whole(SMEM)] * 3 + [whole(pl.ANY)] * 4
        result = call(
            functools.partial(tile_kernel, hop), "tiles", specs, outs, scratch, flops=TPD * 2 * BLK**3, moved=8 << 20,
        )(tile_rows.reshape(-1), tile_srcs.reshape(-1), tile_count, tile_vals, got, own, hop_noise)
        if last:
            tail = result
        else:
            packed, squares = result
    tail = lax.all_to_all(tail, "x", 0, 0, tiled=True)
    return call(final_kernel, "final", [whole(), whole(), whole()], shape((BPD * BLK, WIDTH), bf16))(tail, weights, early)


def solution(mesh):
    grid = Mesh(np.array(mesh.devices).reshape(NY, NZ, NC, NX), ("y", "z", "core", "x"))
    row = ("y", "z", "core")
    in_specs = (
        P(row, "x"),
        P(row, None, None),
        P(row, None),
        P(row, None),
        P(row),
        P(row, None, None),
        P(None, row, "x"),
        P(),
    )
    return jax.shard_map(shards, mesh=grid, in_specs=in_specs, out_specs=P(row, "x"), check_vma=False)
```

```python
import functools

import jax
import jax.numpy as jnp
import numpy as np
from jax import lax
from jax.experimental import pallas as pl
from jax.experimental.pallas import tpu as pltpu
from jax.sharding import Mesh, PartitionSpec as P

BLK = 128
BPD = 8
TPD = 160
PAIRS = BPD // 2
HOPS = 2
NY, NZ, NC, NX = 4, 8, 2, 4
WIDTH = 64
GROUP = 4
BUCKETS = 2 * BPD
MAXG = TPD // GROUP + BUCKETS
SLOTS = MAXG * GROUP
SHIFTS = (0, 1, 2, 3)
EPS = 1e-06
bf16 = jnp.bfloat16
f32 = jnp.float32
VMEM = pltpu.VMEM
SMEM = pltpu.SMEM
HBM = pltpu.HBM
DMA = pltpu.SemaphoreType.DMA


def lane_low(shape):
    return lax.broadcasted_iota(jnp.int32, shape, len(shape) - 1) < WIDTH


def pair_squares(pair_values):
    total = jnp.zeros((BPD, BLK), f32)
    row = lax.broadcasted_iota(jnp.int32, (BPD, BLK), 0)
    half = lax.broadcasted_iota(jnp.int32, (BPD, BLK), 1) // WIDTH
    for p in range(PAIRS):
        v = pair_values[p]
        pick = jnp.where(row == 2 * p + half, 1.0, 0.0).astype(f32)
        total = total + lax.dot_general(
            pick, v * v, (((1,), (1,)), ((), ())),
            precision=lax.Precision.HIGHEST, preferred_element_type=f32,
        )
    return total


def row_scale(total):
    return (1.0 / jnp.sqrt(total + EPS)).T


def pair_scale(columns, p):
    return jnp.where(
        lane_low((BLK, BLK)),
        jnp.broadcast_to(columns[:, 2 * p : 2 * p + 1], (BLK, BLK)),
        jnp.broadcast_to(columns[:, 2 * p + 1 : 2 * p + 2], (BLK, BLK)),
    )


def swap_halves(v):
    return pltpu.roll(v, WIDTH, 1)


def stacked_pair(ref, p):
    first = ref[:, (2 * p) * BLK : (2 * p + 1) * BLK].astype(f32)
    second = ref[:, (2 * p + 1) * BLK : (2 * p + 2) * BLK].astype(f32)
    return jnp.concatenate([first, second], axis=0)


def pack_kernel(feat_ref, out_ref, sq_ref, buf, sem):
    rows = []
    for p in range(PAIRS):
        stacked = stacked_pair(feat_ref, p)
        buf[p] = stacked.T.astype(bf16)
        squares = stacked * stacked
        rows.append(jnp.sum(squares[:WIDTH], axis=0, keepdims=True))
        rows.append(jnp.sum(squares[WIDTH:], axis=0, keepdims=True))
    sq_ref[...] = jnp.concatenate(rows, axis=0)
    copies = [pltpu.make_async_copy(buf, out_ref.at[z], sem.at[z]) for z in range(NZ)]
    for copy in copies:
        copy.start()
    for copy in copies:
        copy.wait()


def pick_kernel(me_ref, idx_ref, z_ref, sq_ref, out_ref, own_ref, norm, buf, sem):
    for z in range(NZ):
        columns = row_scale(sq_ref[z])
        for p in range(PAIRS):
            v = z_ref[z, p].astype(f32) * pair_scale(columns, p)
            norm[z, p] = v.astype(bf16)
            norm[z, PAIRS + p] = swap_halves(v).astype(bf16)
    own_ref[...] = norm[me_ref[1], 0:PAIRS]
    mask = lane_low((BLK, BLK))
    base = (me_ref[0] * NZ * NC + me_ref[2]) * 2
    copies = []
    for dest in range(NY * NC):
        for z in range(NZ):
            at = base + dest * (NY * NZ * NC * 2) + z * NC * 2
            first = idx_ref[at]
            second = idx_ref[at + 1]
            low = norm[z, first // 2 + PAIRS * (first % 2)]
            high = norm[z, second // 2 + PAIRS * (1 - second % 2)]
            buf[dest * NZ + z] = jnp.where(mask, low, high)
        copy = pltpu.make_async_copy(
            buf.at[pl.ds(dest * NZ, NZ)], out_ref.at[pl.ds(dest * NZ, NZ)], sem.at[dest]
        )
        copy.start()
        copies.append(copy)
    for copy in copies:
        copy.wait()


def order_kernel(rows_ref, srcs_ref, count_ref, tile_ref, slab_ref, into_ref, groups_ref, fill, begin):
    count = count_ref[0]

    @pl.loop(0, 2 * SLOTS)
    def _(i):
        tile_ref[i] = TPD
        slab_ref[i] = 0

    for b in range(2 * BUCKETS):
        fill[b] = 0

    def bucket_of(t):
        s = srcs_ref[t]
        return jnp.where(s < BPD, 0, BUCKETS) + rows_ref[t] * 2 + s % 2

    @pl.loop(0, count)
    def _(t):
        b = bucket_of(t)
        fill[b] = fill[b] + 1

    for kind in range(2):
        def place(b, group):
            size = (fill[kind * BUCKETS + b] + GROUP - 1) // GROUP
            begin[kind * BUCKETS + b] = (kind * MAXG + group) * GROUP

            @pl.loop(0, size)
            def _(i):
                into_ref[kind * MAXG + group + i] = b

            return group + size

        groups_ref[kind] = lax.fori_loop(0, BUCKETS, place, jnp.int32(0))

    @pl.loop(0, count)
    def _(t):
        b = bucket_of(t)
        at = begin[b]
        begin[b] = at + 1
        s = srcs_ref[t]
        o = (s - BPD) // 2
        y = o // (NZ * NC)
        z = (o // NC) % NZ
        k = o % NC
        tile_ref[at] = t
        slab_ref[at] = jnp.where(s < BPD, s // 2, (y * NC + k) * NZ + z)


def stage_kernel(tiles_ref, out_ref, sem):
    copy = pltpu.make_async_copy(tiles_ref, out_ref.at[pl.ds(0, TPD)], sem)
    copy.start()
    out_ref[TPD] = jnp.zeros((BLK, BLK), bf16)
    copy.wait()


def add_groups(kind, tile_ref, slab_ref, into_ref, groups_ref, tiles_ref, src_ref, acc):
    def group(g, carry):
        at = (kind * MAXG + g) * GROUP
        left = jnp.concatenate([tiles_ref[tile_ref[at + j]] for j in range(GROUP)], axis=1)
        right = jnp.concatenate([src_ref[slab_ref[at + j]] for j in range(GROUP)], axis=0)
        acc[into_ref[kind * MAXG + g]] += jnp.dot(left, right, preferred_element_type=f32)
        return carry

    lax.fori_loop(0, groups_ref[kind], group, 0)


def own_kernel(tile_ref, slab_ref, into_ref, groups_ref, tiles_ref, src_ref, acc_ref):
    acc_ref[...] = jnp.zeros_like(acc_ref)
    add_groups(0, tile_ref, slab_ref, into_ref, groups_ref, tiles_ref, src_ref, acc_ref)


def far_kernel(hop, tile_ref, slab_ref, into_ref, groups_ref, tiles_ref, src_ref, part_ref, noise_ref, *rest):
    last = hop == HOPS - 1
    if last:
        out_ref, acc, buf, sem = rest
    else:
        out_ref, sq_ref, acc, buf, sem = rest
    acc[...] = part_ref[...]
    add_groups(1, tile_ref, slab_ref, into_ref, groups_ref, tiles_ref, src_ref, acc)
    mask = lane_low((BLK, BLK))
    pairs = []
    for p in range(PAIRS):
        u = stacked_pair(noise_ref.at[hop], p).T + jnp.where(
            mask,
            acc[4 * p] + swap_halves(acc[4 * p + 1]),
            swap_halves(acc[4 * p + 2]) + acc[4 * p + 3],
        )
        pairs.append(u)
        buf[p * BLK : (p + 1) * BLK] = u.astype(bf16)
    total = pair_squares(pairs)
    if last:
        hi = total.astype(bf16).astype(f32)
        mid = (total - hi).astype(bf16).astype(f32)
        lo = total - hi - mid
        buf[PAIRS * BLK : PAIRS * BLK + 16] = jnp.concatenate([hi, mid], axis=0).astype(bf16)
        buf[PAIRS * BLK + 16 : PAIRS * BLK + 32] = jnp.concatenate([lo, jnp.zeros_like(lo)], axis=0).astype(bf16)
        copies = [pltpu.make_async_copy(buf, out_ref, sem.at[0])]
    else:
        sq_ref[...] = total
        copies = [pltpu.make_async_copy(buf, out_ref.at[z], sem.at[z]) for z in range(NZ)]
    for copy in copies:
        copy.start()
    for copy in copies:
        copy.wait()


def early_kernel(x_ref, w_ref, *refs):
    h_refs, out_ref = refs[:-1], refs[-1]
    for p in range(PAIRS):
        total = jnp.zeros((BLK, BLK), f32)
        for k in range(HOPS):
            for j, shift in enumerate(SHIFTS):
                source = (x_ref[0] + NX - shift) % NX
                total = total + jnp.dot(h_refs[k * NX + j][p], w_ref[k, source], preferred_element_type=f32)
        out_ref[p] = total


def final_kernel(x_ref, w_ref, early_ref, *refs):
    got_refs, out_ref = refs[:-1], refs[-1]
    total = jnp.zeros((BPD, BLK), f32)
    for got_ref in got_refs:
        a = got_ref[PAIRS * BLK : PAIRS * BLK + 16].astype(f32)
        b = got_ref[PAIRS * BLK + 16 : PAIRS * BLK + 32].astype(f32)
        total = total + (a[:BPD] + a[BPD:] + b[:BPD])
    columns = row_scale(total)
    for p in range(PAIRS):
        raw = jnp.zeros((BLK, BLK), f32)
        for j, shift in enumerate(SHIFTS):
            source = (x_ref[0] + NX - shift) % NX
            raw = raw + jnp.dot(got_refs[j][p * BLK : (p + 1) * BLK], w_ref[HOPS, source], preferred_element_type=f32)
        v = (early_ref[p] + raw * pair_scale(columns, p)).T
        out_ref[:, (2 * p) * BLK : (2 * p + 1) * BLK] = v[:WIDTH].astype(bf16)
        out_ref[:, (2 * p + 1) * BLK : (2 * p + 2) * BLK] = v[WIDTH:].astype(bf16)


def whole(space=VMEM):
    return pl.BlockSpec(memory_space=space)


def call(kernel, name, in_specs, outs, scratch=(), limit=24 << 20, flops=1 << 20, moved=1 << 20):
    shapes = [jax.ShapeDtypeStruct(dims, kind) for dims, kind, _ in outs]
    specs = [whole(space) for _, _, space in outs]
    single = len(outs) == 1
    return pl.pallas_call(
        kernel,
        name=name,
        out_shape=shapes[0] if single else shapes,
        in_specs=in_specs,
        out_specs=specs[0] if single else specs,
        scratch_shapes=list(scratch),
        compiler_params=pltpu.CompilerParams(vmem_limit_bytes=limit),
        cost_estimate=pl.CostEstimate(flops=flops, bytes_accessed=moved, transcendentals=0),
    )


def shift_x(value, shift):
    return lax.ppermute(value, "x", [(i, (i + shift) % NX) for i in range(NX)])


def shards(features, tile_vals, tile_rows, tile_srcs, tile_count, needed, hop_noise, enc_weight):
    me = jnp.stack([lax.axis_index("y"), lax.axis_index("z"), lax.axis_index("core")]).astype(jnp.int32)
    x_index = lax.axis_index("x").astype(jnp.int32)
    x_only = x_index.reshape(1)
    noise = hop_noise.transpose(0, 2, 1)

    packed, squares = call(
        pack_kernel, "pack", [whole()],
        [((NZ, PAIRS, BLK, BLK), bf16, HBM), ((BPD, BLK), f32, VMEM)],
        [VMEM((PAIRS, BLK, BLK), bf16), DMA((NZ,))],
    )(features.T)
    packed, squares, needed, rows, srcs, count, enc_weight, tile_vals = lax.optimization_barrier(
        (packed, squares, needed.reshape(-1), tile_rows.reshape(-1), tile_srcs.reshape(-1), tile_count, enc_weight, tile_vals)
    )

    weights = lax.dynamic_slice_in_dim(enc_weight, x_index * WIDTH, WIDTH, axis=2).reshape(HOPS + 1, NX, WIDTH, WIDTH)
    nothing = jnp.zeros_like(weights)
    weights = jnp.concatenate(
        [jnp.concatenate([weights, nothing], axis=-1), jnp.concatenate([nothing, weights], axis=-1)], axis=-2
    )
    lists = call(
        order_kernel, "order", [whole(SMEM)] * 3,
        [((2 * SLOTS,), jnp.int32, SMEM), ((2 * SLOTS,), jnp.int32, SMEM), ((2 * MAXG,), jnp.int32, SMEM), ((2,), jnp.int32, SMEM)],
        [SMEM((2 * BUCKETS,), jnp.int32), SMEM((2 * BUCKETS,), jnp.int32)],
    )(rows, srcs, count)
    staged = call(
        stage_kernel, "stage", [whole(HBM)], [((TPD + 1, BLK, BLK), bf16, VMEM)], [DMA(())], moved=10 << 20,
    )(tile_vals)

    spread = []
    asked = None
    for hop in range(HOPS):
        last = hop == HOPS - 1
        along = lax.all_to_all(packed.reshape(NZ, PAIRS, BLK, BLK), "z", 0, 0, tiled=True)
        sums = lax.all_gather(lax.psum(squares, "x"), "z", axis=0)
        if asked is None:
            asked = lax.all_gather(needed, ("y", "core"), axis=0).reshape(-1)
        picked, own = call(
            pick_kernel, "pick", [whole(SMEM), whole(SMEM), whole(), whole()],
            [((NY * NC * NZ, BLK, BLK), bf16, HBM), ((PAIRS, BLK, BLK), bf16, VMEM)],
            [VMEM((NZ, BPD, BLK, BLK), bf16), VMEM((NY * NC * NZ, BLK, BLK), bf16), DMA((NY * NC,))],
        )(me, asked, along, sums)
        got = lax.all_to_all(picked, ("y", "core"), 0, 0, tiled=True)
        part = call(
            own_kernel, "own", [whole(SMEM)] * 4 + [whole()] * 2, [((BUCKETS, BLK, BLK), f32, VMEM)],
            flops=TPD * 2 * BLK**3, moved=4 << 20,
        )(*lists, staged, own)
        spread += [own] + [shift_x(own, shift) for shift in SHIFTS[1:]]
        if last:
            early = call(
                early_kernel, "early", [whole(SMEM)] + [whole()] * (1 + 2 * NX), [((PAIRS, BLK, BLK), f32, VMEM)]
            )(x_only, weights, *spread)
        if last:
            outs = [((PAIRS * BLK + 32, BLK), bf16, HBM)]
            buf = VMEM((PAIRS * BLK + 32, BLK), bf16)
        else:
            outs = [((NZ, PAIRS * BLK, BLK), bf16, HBM), ((BPD, BLK), f32, VMEM)]
            buf = VMEM((PAIRS * BLK, BLK), bf16)
        result = call(
            functools.partial(far_kernel, hop), "far", [whole(SMEM)] * 4 + [whole()] * 4, outs,
            [VMEM((BUCKETS, BLK, BLK), f32), buf, DMA((NZ,))],
            flops=TPD * 2 * BLK**3, moved=8 << 20,
        )(*lists, staged, got, part, noise)
        if not last:
            packed, squares = result
    tails = [result] + [shift_x(result, shift) for shift in SHIFTS[1:]]
    return call(
        final_kernel, "final", [whole(SMEM)] + [whole()] * (2 + NX), [((WIDTH, BPD * BLK), bf16, VMEM)]
    )(x_only, weights, early, *tails).T


def solution(mesh):
    grid = Mesh(np.array(mesh.devices).reshape(NY, NZ, NC, NX), ("y", "z", "core", "x"))
    row = ("y", "z", "core")
    in_specs = (
        P(row, "x"),
        P(row, None, None),
        P(row, None),
        P(row, None),
        P(row),
        P(row, None, None),
        P(None, row, "x"),
        P(),
    )
    return jax.shard_map(shards, mesh=grid, in_specs=in_specs, out_specs=P(row, "x"), check_vma=False)
```

```python
import functools

import jax
import jax.numpy as jnp
import numpy as np
from jax import lax
from jax.experimental import pallas as pl
from jax.experimental.pallas import tpu as pltpu
from jax.sharding import Mesh, PartitionSpec as P

BLK = 128
BPD = 8
TPD = 160
PAIRS = BPD // 2
HOPS = 2
NY, NZ, NC, NX = 4, 8, 2, 4
WIDTH = 64
GROUP = 4
BUCKETS = 2 * BPD
MAXG = TPD // GROUP + BUCKETS
SLOTS = MAXG * GROUP
SHIFTS = (0, 1, 2, 3)
ZSHIFTS = (0, 1, 7, 2, 6, 3, 5, 4)
DEPTH = 4
FULL = 63 << 20
MOST = 65_300_000
EPS = 1e-06
bf16 = jnp.bfloat16
f32 = jnp.float32
VMEM = pltpu.VMEM
SMEM = pltpu.SMEM
HBM = pltpu.HBM
DMA = pltpu.SemaphoreType.DMA


def lane_low(shape):
    return lax.broadcasted_iota(jnp.int32, shape, len(shape) - 1) < WIDTH


def pair_squares(pair_values):
    total = jnp.zeros((BPD, BLK), f32)
    row = lax.broadcasted_iota(jnp.int32, (BPD, BLK), 0)
    half = lax.broadcasted_iota(jnp.int32, (BPD, BLK), 1) // WIDTH
    for p in range(PAIRS):
        v = pair_values[p]
        pick = jnp.where(row == 2 * p + half, 1.0, 0.0).astype(f32)
        total = total + lax.dot_general(
            pick, v * v, (((1,), (1,)), ((), ())),
            precision=lax.Precision.HIGHEST, preferred_element_type=f32,
        )
    return total


def row_scale(total):
    return (1.0 / jnp.sqrt(total + EPS)).T


def pair_scale(columns, p):
    return jnp.where(
        lane_low((BLK, BLK)),
        jnp.broadcast_to(columns[:, 2 * p : 2 * p + 1], (BLK, BLK)),
        jnp.broadcast_to(columns[:, 2 * p + 1 : 2 * p + 2], (BLK, BLK)),
    )


def swap_halves(v):
    return pltpu.roll(v, WIDTH, 1)


def stacked_pair(ref, p):
    first = ref[:, (2 * p) * BLK : (2 * p + 1) * BLK].astype(f32)
    second = ref[:, (2 * p + 1) * BLK : (2 * p + 2) * BLK].astype(f32)
    return jnp.concatenate([first, second], axis=0)


def pack_kernel(feat_ref, out_ref, sq_ref):
    rows = []
    for p in range(PAIRS):
        stacked = stacked_pair(feat_ref, p)
        out_ref[p] = stacked.T.astype(bf16)
        squares = stacked * stacked
        rows.append(jnp.sum(squares[:WIDTH], axis=0, keepdims=True))
        rows.append(jnp.sum(squares[WIDTH:], axis=0, keepdims=True))
    total = jnp.concatenate(rows, axis=0)
    for i in range(NX * NZ):
        sq_ref[i] = total


def pick_kernel(me_ref, idx_ref, sq_ref, *refs):
    z_refs = refs[:NZ]
    out_ref, own_ref, norm, buf, sem = refs[NZ:]
    for j, shift in enumerate(ZSHIFTS):
        z = (me_ref[1] + NZ - shift) % NZ
        total = sq_ref[z]
        for x in range(1, NX):
            total = total + sq_ref[x * NZ + z]
        columns = row_scale(total)
        for p in range(PAIRS):
            v = z_refs[j][p].astype(f32) * pair_scale(columns, p)
            if j == 0:
                own_ref[p] = v.astype(bf16)
            norm[j, p] = v.astype(bf16)
            norm[j, PAIRS + p] = swap_halves(v).astype(bf16)
    mask = lane_low((BLK, BLK))
    base = (me_ref[0] * NZ * NC + me_ref[2]) * 2
    copies = []
    for dest in range(NY * NC):
        for j, shift in enumerate(ZSHIFTS):
            z = (me_ref[1] + NZ - shift) % NZ
            at = base + dest * (NY * NZ * NC * 2) + z * NC * 2
            first = idx_ref[at]
            second = idx_ref[at + 1]
            low = norm[j, first // 2 + PAIRS * (first % 2)]
            high = norm[j, second // 2 + PAIRS * (1 - second % 2)]
            buf[dest * NZ + z] = jnp.where(mask, low, high)
        copy = pltpu.make_async_copy(
            buf.at[pl.ds(dest * NZ, NZ)], out_ref.at[pl.ds(dest * NZ, NZ)], sem.at[dest]
        )
        copy.start()
        copies.append(copy)
    for copy in copies:
        copy.wait()


def order_kernel(rows_ref, srcs_ref, count_ref, tile_ref, slab_ref, into_ref, groups_ref, fill, begin):
    count = count_ref[0]

    @pl.loop(0, SLOTS // 8)
    def _(i):
        for j in range(8):
            tile_ref[i * 8 + j] = 0
            tile_ref[SLOTS + i * 8 + j] = 0
            slab_ref[i * 8 + j] = PAIRS
            slab_ref[SLOTS + i * 8 + j] = NY * NC * NZ

    @pl.loop(0, 2 * MAXG)
    def _(i):
        into_ref[i] = 0

    for b in range(2 * BUCKETS):
        fill[b] = 0

    def bucket_of(t):
        s = srcs_ref[t]
        return jnp.where(s < BPD, 0, BUCKETS) + rows_ref[t] * 2 + s % 2

    @pl.loop(0, count)
    def _(t):
        b = bucket_of(t)
        fill[b] = fill[b] + 1

    for kind in range(2):
        def place(b, group):
            size = (fill[kind * BUCKETS + b] + GROUP - 1) // GROUP
            begin[kind * BUCKETS + b] = (kind * MAXG + group) * GROUP

            @pl.loop(0, size)
            def _(i):
                into_ref[kind * MAXG + group + i] = b

            return group + size

        groups_ref[kind] = lax.fori_loop(0, BUCKETS, place, jnp.int32(0))

    @pl.loop(0, count)
    def _(t):
        b = bucket_of(t)
        at = begin[b]
        begin[b] = at + 1
        s = srcs_ref[t]
        o = (s - BPD) // 2
        y = o // (NZ * NC)
        z = (o // NC) % NZ
        k = o % NC
        tile_ref[at] = t
        slab_ref[at] = jnp.where(s < BPD, s // 2, (y * NC + k) * NZ + z)


def add_groups(kind, tile_ref, slab_ref, into_ref, groups_ref, tiles_ref, src, acc, ring, sem):
    steps = (groups_ref[kind] + 1) // 2

    def copies(step):
        slot = step % DEPTH
        first = (kind * MAXG + 2 * step) * GROUP
        return [
            pltpu.make_async_copy(tiles_ref.at[tile_ref[first + j]], ring.at[slot, j], sem.at[slot, j])
            for j in range(2 * GROUP)
        ]

    def begin(step):
        @pl.when(step < steps)
        def _():
            for copy in copies(step):
                copy.start()

    def run(step, carry):
        slot = step % DEPTH
        group = kind * MAXG + 2 * step
        for copy in copies(step):
            copy.wait()
        parts = []
        for h in range(2):
            left = jnp.concatenate([ring[slot, h * GROUP + j] for j in range(GROUP)], axis=1)
            right = jnp.concatenate([src[slab_ref[(group + h) * GROUP + j]] for j in range(GROUP)], axis=0)
            parts.append(jnp.dot(left, right, preferred_element_type=f32))
        for h in range(2):
            acc[into_ref[group + h]] += parts[h]
        begin(step + DEPTH)
        return carry

    return begin, lambda: lax.fori_loop(0, steps, run, 0)


def own_kernel(tile_ref, slab_ref, into_ref, groups_ref, tiles_ref, own_ref, acc_ref, src, ring, sem):
    begin, run = add_groups(0, tile_ref, slab_ref, into_ref, groups_ref, tiles_ref, src, acc_ref, ring, sem)
    for step in range(DEPTH):
        begin(step)
    acc_ref[...] = jnp.zeros_like(acc_ref)
    src[0:PAIRS] = own_ref[...]
    src[PAIRS] = jnp.zeros((BLK, BLK), bf16)
    run()


def far_kernel(hop, tile_ref, slab_ref, into_ref, groups_ref, tiles_ref, got_ref, part_ref, noise_ref, *rest):
    last = hop == HOPS - 1
    if last:
        out_ref, acc, src, noise, ring, sem, load = rest
    else:
        out_ref, sq_ref, acc, src, noise, ring, sem, load = rest
    got_copy = pltpu.make_async_copy(got_ref, src.at[pl.ds(0, NY * NC * NZ)], load.at[0])
    part_copy = pltpu.make_async_copy(part_ref, acc, load.at[1])
    noise_copy = pltpu.make_async_copy(noise_ref.at[hop], noise, load.at[2])
    got_copy.start()
    begin, run = add_groups(1, tile_ref, slab_ref, into_ref, groups_ref, tiles_ref, src, acc, ring, sem)
    begin(0)
    part_copy.start()
    for step in range(1, DEPTH):
        begin(step)
    noise_copy.start()
    src[NY * NC * NZ] = jnp.zeros((BLK, BLK), bf16)
    got_copy.wait()
    part_copy.wait()
    run()
    noise_copy.wait()
    mask = lane_low((BLK, BLK))
    pairs = []
    for p in range(PAIRS):
        u = stacked_pair(noise, p).T + jnp.where(
            mask,
            acc[4 * p] + swap_halves(acc[4 * p + 1]),
            swap_halves(acc[4 * p + 2]) + acc[4 * p + 3],
        )
        pairs.append(u)
        if last:
            out_ref[p * BLK : (p + 1) * BLK] = u.astype(bf16)
        else:
            out_ref[p] = u.astype(bf16)
    total = pair_squares(pairs)
    if last:
        hi = total.astype(bf16).astype(f32)
        mid = (total - hi).astype(bf16).astype(f32)
        lo = total - hi - mid
        out_ref[PAIRS * BLK : PAIRS * BLK + 16] = jnp.concatenate([hi, mid], axis=0).astype(bf16)
        out_ref[PAIRS * BLK + 16 : PAIRS * BLK + 32] = jnp.concatenate([lo, jnp.zeros_like(lo)], axis=0).astype(bf16)
    else:
        for i in range(NX * NZ):
            sq_ref[i] = total


def early_kernel(x_ref, w_ref, *refs):
    h_refs, out_ref = refs[:-1], refs[-1]
    for p in range(PAIRS):
        total = jnp.zeros((BLK, BLK), f32)
        for k in range(HOPS):
            for j, shift in enumerate(SHIFTS):
                source = (x_ref[0] + NX - shift) % NX
                total = total + jnp.dot(h_refs[k * NX + j][p], w_ref[k, source], preferred_element_type=f32)
        out_ref[p] = total


def final_kernel(x_ref, w_ref, early_ref, *refs):
    got_refs, out_ref = refs[:-1], refs[-1]
    total = jnp.zeros((BPD, BLK), f32)
    for got_ref in got_refs:
        a = got_ref[PAIRS * BLK : PAIRS * BLK + 16].astype(f32)
        b = got_ref[PAIRS * BLK + 16 : PAIRS * BLK + 32].astype(f32)
        total = total + (a[:BPD] + a[BPD:] + b[:BPD])
    columns = row_scale(total)
    for p in range(PAIRS):
        raw = jnp.zeros((BLK, BLK), f32)
        for j, shift in enumerate(SHIFTS):
            source = (x_ref[0] + NX - shift) % NX
            raw = raw + jnp.dot(got_refs[j][p * BLK : (p + 1) * BLK], w_ref[HOPS, source], preferred_element_type=f32)
        v = (early_ref[p] + raw * pair_scale(columns, p)).T
        out_ref[:, (2 * p) * BLK : (2 * p + 1) * BLK] = v[:WIDTH].astype(bf16)
        out_ref[:, (2 * p + 1) * BLK : (2 * p + 2) * BLK] = v[WIDTH:].astype(bf16)


def whole(space=VMEM):
    return pl.BlockSpec(memory_space=space)


def call(kernel, name, in_specs, outs, scratch=(), limit=24 << 20, flops=1 << 20, moved=1 << 20):
    shapes = [jax.ShapeDtypeStruct(dims, kind) for dims, kind, _ in outs]
    specs = [whole(space) for _, _, space in outs]
    single = len(outs) == 1
    return pl.pallas_call(
        kernel,
        name=name,
        out_shape=shapes[0] if single else shapes,
        in_specs=in_specs,
        out_specs=specs[0] if single else specs,
        scratch_shapes=list(scratch),
        compiler_params=pltpu.CompilerParams(vmem_limit_bytes=limit),
        cost_estimate=pl.CostEstimate(flops=flops, bytes_accessed=moved, transcendentals=0),
    )


def shift_by(value, axis, shift):
    size = lax.axis_size(axis)
    return lax.ppermute(value, axis, [(i, (i + shift) % size) for i in range(size)])


def shards(features, tile_vals, tile_rows, tile_srcs, tile_count, needed, hop_noise, enc_weight):
    me = jnp.stack([lax.axis_index("y"), lax.axis_index("z"), lax.axis_index("core")]).astype(jnp.int32)
    x_index = lax.axis_index("x").astype(jnp.int32)
    x_only = x_index.reshape(1)
    noise = hop_noise.transpose(0, 2, 1)

    packed, squares = call(
        pack_kernel, "pack", [whole()],
        [((PAIRS, BLK, BLK), bf16, VMEM), ((NX * NZ, BPD, BLK), f32, VMEM)],
    )(features.T)
    packed, squares, needed, rows, srcs, count, enc_weight, tile_vals = lax.optimization_barrier(
        (packed, squares, needed.reshape(-1), tile_rows.reshape(-1), tile_srcs.reshape(-1), tile_count, enc_weight, tile_vals)
    )

    weights = lax.dynamic_slice_in_dim(enc_weight, x_index * WIDTH, WIDTH, axis=2).reshape(HOPS + 1, NX, WIDTH, WIDTH)
    nothing = jnp.zeros_like(weights)
    weights = jnp.concatenate(
        [jnp.concatenate([weights, nothing], axis=-1), jnp.concatenate([nothing, weights], axis=-1)], axis=-2
    )
    lists = call(
        order_kernel, "order", [whole(SMEM)] * 3,
        [((2 * SLOTS,), jnp.int32, SMEM), ((2 * SLOTS,), jnp.int32, SMEM), ((2 * MAXG,), jnp.int32, SMEM), ((2,), jnp.int32, SMEM)],
        [SMEM((2 * BUCKETS,), jnp.int32), SMEM((2 * BUCKETS,), jnp.int32)],
    )(rows, srcs, count)
    spread = []
    asked = None
    for hop in range(HOPS):
        last = hop == HOPS - 1
        along = [packed] + [shift_by(packed, "z", shift) for shift in ZSHIFTS[1:]]
        sums = lax.all_to_all(squares, ("x", "z"), 0, 0, tiled=True)
        if asked is None:
            asked = lax.all_gather(needed, ("y", "core"), axis=0).reshape(-1)
        picked, own = call(
            pick_kernel, "pick", [whole(SMEM)] * 2 + [whole()] * (1 + NZ),
            [((NY * NC * NZ, BLK, BLK), bf16, HBM), ((PAIRS, BLK, BLK), bf16, VMEM)],
            [VMEM((NZ, BPD, BLK, BLK), bf16), VMEM((NY * NC * NZ, BLK, BLK), bf16), DMA((NY * NC,))],
            limit=MOST,
        )(me, asked, sums, *along)
        got = lax.all_to_all(picked, ("y", "core"), 0, 0, tiled=True)
        ring = [VMEM((DEPTH, 2 * GROUP, BLK, BLK), bf16), DMA((DEPTH, 2 * GROUP))]
        part = call(
            own_kernel, "own", [whole(SMEM)] * 4 + [whole(HBM), whole()], [((BUCKETS, BLK, BLK), f32, VMEM)],
            [VMEM((PAIRS + 1, BLK, BLK), bf16)] + ring,
            limit=FULL, flops=TPD * 2 * BLK**3, moved=4 << 20,
        )(*lists, tile_vals, own)
        spread += [own] + [shift_by(own, "x", shift) for shift in SHIFTS[1:]]
        if last:
            early = call(
                early_kernel, "early", [whole(SMEM)] + [whole()] * (1 + 2 * NX), [((PAIRS, BLK, BLK), f32, VMEM)]
            )(x_only, weights, *spread)
        if last:
            outs = [((PAIRS * BLK + 32, BLK), bf16, VMEM)]
        else:
            outs = [((PAIRS, BLK, BLK), bf16, VMEM), ((NX * NZ, BPD, BLK), f32, VMEM)]
        result = call(
            functools.partial(far_kernel, hop), "far", [whole(SMEM)] * 4 + [whole(HBM)] * 4, outs,
            [
                VMEM((BUCKETS, BLK, BLK), f32),
                VMEM((NY * NC * NZ + 1, BLK, BLK), bf16),
                VMEM((WIDTH, BPD * BLK), f32),
            ] + ring + [DMA((3,))],
            limit=FULL, flops=TPD * 2 * BLK**3, moved=8 << 20,
        )(*lists, tile_vals, got, part, noise)
        if not last:
            packed, squares = result
    tails = [result] + [shift_by(result, "x", shift) for shift in SHIFTS[1:]]
    return call(
        final_kernel, "final", [whole(SMEM)] + [whole()] * (2 + NX), [((WIDTH, BPD * BLK), bf16, VMEM)]
    )(x_only, weights, early, *tails).T


def solution(mesh):
    grid = Mesh(np.array(mesh.devices).reshape(NY, NZ, NC, NX), ("y", "z", "core", "x"))
    row = ("y", "z", "core")
    in_specs = (
        P(row, "x"),
        P(row, None, None),
        P(row, None),
        P(row, None),
        P(row),
        P(row, None, None),
        P(None, row, "x"),
        P(),
    )
    return jax.shard_map(shards, mesh=grid, in_specs=in_specs, out_specs=P(row, "x"), check_vma=False)
```

```python
import functools

import jax
import jax.numpy as jnp
import numpy as np
from jax import lax
from jax.experimental import pallas as pl
from jax.experimental.pallas import tpu as pltpu
from jax.sharding import Mesh, PartitionSpec as P

BLK = 128
BPD = 8
TPD = 160
PAIRS = BPD // 2
HOPS = 2
NY, NZ, NC, NX = 4, 8, 2, 4
WIDTH = 64
GROUP = 4
BUCKETS = 2 * BPD
MAXG = TPD // GROUP + BUCKETS
SLOTS = MAXG * GROUP
SHIFTS = (0, 2, 1, 3)
DEPTH = 4
FULL = 63 << 20
MOST = 65_300_000
ROOM = 63_600_000
EPS = 1e-06
bf16 = jnp.bfloat16
f32 = jnp.float32
VMEM = pltpu.VMEM
SMEM = pltpu.SMEM
HBM = pltpu.HBM
DMA = pltpu.SemaphoreType.DMA


def lane_low(shape):
    return lax.broadcasted_iota(jnp.int32, shape, len(shape) - 1) < WIDTH


def pair_squares(pair_values):
    total = jnp.zeros((BPD, BLK), f32)
    row = lax.broadcasted_iota(jnp.int32, (BPD, BLK), 0)
    half = lax.broadcasted_iota(jnp.int32, (BPD, BLK), 1) // WIDTH
    for p in range(PAIRS):
        v = pair_values[p]
        pick = jnp.where(row == 2 * p + half, 1.0, 0.0).astype(f32)
        total = total + lax.dot_general(
            pick, v * v, (((1,), (1,)), ((), ())),
            precision=lax.Precision.HIGHEST, preferred_element_type=f32,
        )
    return total


def row_scale(total):
    return (1.0 / jnp.sqrt(total + EPS)).T


def pair_scale(columns, p):
    return jnp.where(
        lane_low((BLK, BLK)),
        jnp.broadcast_to(columns[:, 2 * p : 2 * p + 1], (BLK, BLK)),
        jnp.broadcast_to(columns[:, 2 * p + 1 : 2 * p + 2], (BLK, BLK)),
    )


def swap_halves(v):
    return pltpu.roll(v, WIDTH, 1)


def stacked_pair(ref, p):
    first = ref[:, (2 * p) * BLK : (2 * p + 1) * BLK].astype(f32)
    second = ref[:, (2 * p + 1) * BLK : (2 * p + 2) * BLK].astype(f32)
    return jnp.concatenate([first, second], axis=0)


def pack_kernel(feat_ref, out_ref, sq_ref):
    rows = []
    for p in range(PAIRS):
        stacked = stacked_pair(feat_ref, p)
        out_ref[p] = stacked.T.astype(bf16)
        squares = stacked * stacked
        rows.append(jnp.sum(squares[:WIDTH], axis=0, keepdims=True))
        rows.append(jnp.sum(squares[WIDTH:], axis=0, keepdims=True))
    sq_ref[...] = jnp.concatenate(rows, axis=0)


def norm_kernel(hop, raw_ref, sq_ref, *rest):
    columns = row_scale(sq_ref[...])
    before_ref = rest[0] if hop else None
    out_ref, own_ref, buf, sem = rest[-4:]
    copies = []
    for p in range(PAIRS):
        v = (raw_ref[p].astype(f32) * pair_scale(columns, p)).astype(bf16)
        buf[p] = v
        own_ref[hop, p] = v
    for z in range(NZ):
        copy = pltpu.make_async_copy(buf, out_ref.at[z], sem.at[z])
        copy.start()
        copies.append(copy)
    if hop:
        own_ref[0:hop] = before_ref[...]
    for copy in copies:
        copy.wait()


def pick_kernel(me_ref, idx_ref, z_ref, out_ref, slots, buf, sem):
    for z in range(NZ):
        for p in range(PAIRS):
            v = z_ref[z, p]
            slots[z * BPD + p] = v
            slots[z * BPD + PAIRS + p] = jnp.concatenate([v[:, WIDTH:], v[:, :WIDTH]], axis=1)
    mask = lane_low((BLK, BLK))
    mine = me_ref[0] * NC + me_ref[2]
    copies = []
    for dest in range(NY * NC):
        for z in range(NZ):
            i = dest * NZ + z
            buf[i] = jnp.where(mask, slots[idx_ref[2 * i]], slots[idx_ref[2 * i + 1]])

        @pl.when(mine == dest)
        def _():
            buf[dest * NZ + me_ref[1]] = jnp.zeros((BLK, BLK), bf16)

        copy = pltpu.make_async_copy(
            buf.at[pl.ds(dest * NZ, NZ)], out_ref.at[pl.ds(dest * NZ, NZ)], sem.at[dest]
        )
        copy.start()
        copies.append(copy)
    for copy in copies:
        copy.wait()


def order_kernel(me_ref, rows_ref, srcs_ref, count_ref, tile_ref, slab_ref, into_ref, groups_ref, fill, begin):
    count = count_ref[0]
    empty = (me_ref[0] * NC + me_ref[2]) * NZ + me_ref[1]

    @pl.loop(0, SLOTS // 8)
    def _(i):
        for j in range(8):
            tile_ref[i * 8 + j] = 0
            tile_ref[SLOTS + i * 8 + j] = 0
            slab_ref[i * 8 + j] = PAIRS
            slab_ref[SLOTS + i * 8 + j] = empty

    @pl.loop(0, 2 * MAXG)
    def _(i):
        into_ref[i] = 0

    for b in range(2 * BUCKETS):
        fill[b] = 0

    def bucket_of(t):
        s = srcs_ref[t]
        return jnp.where(s < BPD, 0, BUCKETS) + rows_ref[t] * 2 + s % 2

    @pl.loop(0, count)
    def _(t):
        b = bucket_of(t)
        fill[b] = fill[b] + 1

    for kind in range(2):
        def place(b, group):
            size = (fill[kind * BUCKETS + b] + GROUP - 1) // GROUP
            begin[kind * BUCKETS + b] = (kind * MAXG + group) * GROUP

            @pl.loop(0, size)
            def _(i):
                into_ref[kind * MAXG + group + i] = b

            return group + size

        groups_ref[kind] = lax.fori_loop(0, BUCKETS, place, jnp.int32(0))

    @pl.loop(0, count)
    def _(t):
        b = bucket_of(t)
        at = begin[b]
        begin[b] = at + 1
        s = srcs_ref[t]
        o = (s - BPD) // 2
        y = o // (NZ * NC)
        z = (o // NC) % NZ
        k = o % NC
        tile_ref[at] = t
        slab_ref[at] = jnp.where(s < BPD, s // 2, (y * NC + k) * NZ + z)


def add_groups(kind, tile_ref, slab_ref, into_ref, groups_ref, tiles_ref, src, acc, ring, sem):
    steps = (groups_ref[kind] + 1) // 2

    def copies(step):
        slot = step % DEPTH
        first = (kind * MAXG + 2 * step) * GROUP
        return [
            pltpu.make_async_copy(tiles_ref.at[tile_ref[first + j]], ring.at[slot, j], sem.at[slot, j])
            for j in range(2 * GROUP)
        ]

    def begin(step):
        @pl.when(step < steps)
        def _():
            for copy in copies(step):
                copy.start()

    def run(step, carry):
        slot = step % DEPTH
        group = kind * MAXG + 2 * step
        for copy in copies(step):
            copy.wait()
        parts = []
        for h in range(2):
            left = jnp.concatenate([ring[slot, h * GROUP + j] for j in range(GROUP)], axis=1)
            right = jnp.concatenate([src[slab_ref[(group + h) * GROUP + j]] for j in range(GROUP)], axis=0)
            parts.append(jnp.dot(left, right, preferred_element_type=f32))
        for h in range(2):
            acc[into_ref[group + h]] += parts[h]
        begin(step + DEPTH)
        return carry

    return begin, lambda: lax.fori_loop(0, steps, run, 0)


def own_kernel(hop, tile_ref, slab_ref, into_ref, groups_ref, tiles_ref, own_ref, acc_ref, src, ring, sem):
    begin, run = add_groups(0, tile_ref, slab_ref, into_ref, groups_ref, tiles_ref, src, acc_ref, ring, sem)
    for step in range(DEPTH):
        begin(step)
    acc_ref[...] = jnp.zeros_like(acc_ref)
    src[0:PAIRS] = own_ref[hop]
    src[PAIRS] = jnp.zeros((BLK, BLK), bf16)
    run()


def far_kernel(hop, tile_ref, slab_ref, into_ref, groups_ref, tiles_ref, got_ref, part_ref, noise_ref, *rest):
    last = hop == HOPS - 1
    if last:
        out_ref, acc, noise, ring, sem, load = rest
    else:
        out_ref, sq_ref, acc, noise, ring, sem, load = rest
    begin, run = add_groups(1, tile_ref, slab_ref, into_ref, groups_ref, tiles_ref, got_ref, acc, ring, sem)
    for step in range(DEPTH):
        begin(step)
    noise_copy = pltpu.make_async_copy(noise_ref.at[hop], noise, load)
    noise_copy.start()
    acc[...] = part_ref[...]
    run()
    noise_copy.wait()
    mask = lane_low((BLK, BLK))
    pairs = []
    for p in range(PAIRS):
        u = stacked_pair(noise, p).T + jnp.where(
            mask,
            acc[4 * p] + swap_halves(acc[4 * p + 1]),
            swap_halves(acc[4 * p + 2]) + acc[4 * p + 3],
        )
        pairs.append(u)
        if last:
            out_ref[p * BLK : (p + 1) * BLK] = u.astype(bf16)
        else:
            out_ref[p] = u
    total = pair_squares(pairs)
    if last:
        hi = total.astype(bf16).astype(f32)
        mid = (total - hi).astype(bf16).astype(f32)
        lo = total - hi - mid
        out_ref[PAIRS * BLK : PAIRS * BLK + 16] = jnp.concatenate([hi, mid], axis=0).astype(bf16)
        out_ref[PAIRS * BLK + 16 : PAIRS * BLK + 32] = jnp.concatenate([lo, jnp.zeros_like(lo)], axis=0).astype(bf16)
    else:
        sq_ref[...] = total


def early_kernel(x_ref, w_ref, *refs):
    h_refs, out_ref = refs[:-1], refs[-1]
    for p in range(PAIRS):
        total = jnp.zeros((BLK, BLK), f32)
        for k in range(HOPS):
            for j, shift in enumerate(SHIFTS):
                source = (x_ref[0] + NX - shift) % NX
                total = total + jnp.dot(h_refs[j][k, p], w_ref[k, source], preferred_element_type=f32)
        out_ref[p] = total


def final_kernel(x_ref, w_ref, early_ref, *refs):
    got_refs, out_ref = refs[:-1], refs[-1]
    total = jnp.zeros((BPD, BLK), f32)
    for got_ref in got_refs:
        a = got_ref[PAIRS * BLK : PAIRS * BLK + 16].astype(f32)
        b = got_ref[PAIRS * BLK + 16 : PAIRS * BLK + 32].astype(f32)
        total = total + (a[:BPD] + a[BPD:] + b[:BPD])
    columns = row_scale(total)
    for p in range(PAIRS):
        raw = jnp.zeros((BLK, BLK), f32)
        for j, shift in enumerate(SHIFTS):
            source = (x_ref[0] + NX - shift) % NX
            raw = raw + jnp.dot(got_refs[j][p * BLK : (p + 1) * BLK], w_ref[HOPS, source], preferred_element_type=f32)
        v = (early_ref[p] + raw * pair_scale(columns, p)).T
        out_ref[:, (2 * p) * BLK : (2 * p + 1) * BLK] = v[:WIDTH].astype(bf16)
        out_ref[:, (2 * p + 1) * BLK : (2 * p + 2) * BLK] = v[WIDTH:].astype(bf16)


def whole(space=VMEM):
    return pl.BlockSpec(memory_space=space)


def call(kernel, name, in_specs, outs, scratch=(), limit=24 << 20, flops=1 << 20, moved=1 << 20):
    shapes = [jax.ShapeDtypeStruct(dims, kind) for dims, kind, _ in outs]
    specs = [whole(space) for _, _, space in outs]
    single = len(outs) == 1
    return pl.pallas_call(
        kernel,
        name=name,
        out_shape=shapes[0] if single else shapes,
        in_specs=in_specs,
        out_specs=specs[0] if single else specs,
        scratch_shapes=list(scratch),
        compiler_params=pltpu.CompilerParams(vmem_limit_bytes=limit),
        cost_estimate=pl.CostEstimate(flops=flops, bytes_accessed=moved, transcendentals=0),
    )


def shift_by(value, axis, shift):
    size = lax.axis_size(axis)
    return lax.ppermute(value, axis, [(i, (i + shift) % size) for i in range(size)])


def shards(features, tile_vals, tile_rows, tile_srcs, tile_count, needed, hop_noise, enc_weight):
    me = jnp.stack([lax.axis_index("y"), lax.axis_index("z"), lax.axis_index("core")]).astype(jnp.int32)
    x_index = lax.axis_index("x").astype(jnp.int32)
    x_only = x_index.reshape(1)
    noise = hop_noise.transpose(0, 2, 1)

    packed, squares = call(
        pack_kernel, "pack", [whole()],
        [((PAIRS, BLK, BLK), bf16, VMEM), ((BPD, BLK), f32, VMEM)],
    )(features.T)
    packed, squares, needed, rows, srcs, count, enc_weight, tile_vals = lax.optimization_barrier(
        (packed, squares, needed.reshape(-1), tile_rows.reshape(-1), tile_srcs.reshape(-1), tile_count, enc_weight, tile_vals)
    )

    weights = lax.dynamic_slice_in_dim(enc_weight, x_index * WIDTH, WIDTH, axis=2).reshape(HOPS + 1, NX, WIDTH, WIDTH)
    nothing = jnp.zeros_like(weights)
    weights = jnp.concatenate(
        [jnp.concatenate([weights, nothing], axis=-1), jnp.concatenate([nothing, weights], axis=-1)], axis=-2
    )
    lists = call(
        order_kernel, "order", [whole(SMEM)] * 4,
        [((2 * SLOTS,), jnp.int32, SMEM), ((2 * SLOTS,), jnp.int32, SMEM), ((2 * MAXG,), jnp.int32, SMEM), ((2,), jnp.int32, SMEM)],
        [SMEM((2 * BUCKETS,), jnp.int32), SMEM((2 * BUCKETS,), jnp.int32)],
    )(me, rows, srcs, count)
    table = None
    for hop in range(HOPS):
        last = hop == HOPS - 1
        total = lax.psum(squares, "x")
        before = [owned] if hop else []
        packed, owned = call(
            functools.partial(norm_kernel, hop), "norm", [whole()] * (2 + hop),
            [((NZ, PAIRS, BLK, BLK), bf16, HBM), ((hop + 1, PAIRS, BLK, BLK), bf16, VMEM)],
            [VMEM((PAIRS, BLK, BLK), bf16), DMA((NZ,))],
            limit=MOST,
        )(packed, total, *before)
        if last:
            spread = [owned] + [shift_by(owned, "x", shift) for shift in SHIFTS[1:]]
        along = lax.all_to_all(packed, "z", 0, 0, tiled=True)
        if table is None:
            needed, owned = lax.optimization_barrier((needed, owned))
            asked = lax.all_gather(needed, ("y", "core"), axis=0).reshape(NY * NC, NY, NZ, NC, 2)
            asked = lax.dynamic_slice(asked, (0, me[0], 0, me[2], 0), (NY * NC, 1, NZ, 1, 2)).reshape(NY * NC, NZ, 2)
            odd = (asked % 2) ^ jnp.arange(2, dtype=jnp.int32)
            table = (jnp.arange(NZ, dtype=jnp.int32)[:, None] * BPD + asked // 2 + PAIRS * odd).reshape(-1)
        picked = call(
            pick_kernel, "pick", [whole(SMEM)] * 2 + [whole()],
            [((NY * NC * NZ, BLK, BLK), bf16, HBM)],
            [VMEM((NZ * BPD, BLK, BLK), bf16), VMEM((NY * NC * NZ, BLK, BLK), bf16), DMA((NY * NC,))],
            limit=MOST,
        )(me, table, along)
        got = lax.all_to_all(picked, ("y", "core"), 0, 0, tiled=True)
        ring = [VMEM((DEPTH, 2 * GROUP, BLK, BLK), bf16), DMA((DEPTH, 2 * GROUP))]
        part = call(
            functools.partial(own_kernel, hop), "own", [whole(SMEM)] * 4 + [whole(HBM), whole()], [((BUCKETS, BLK, BLK), f32, VMEM)],
            [VMEM((PAIRS + 1, BLK, BLK), bf16)] + ring,
            limit=FULL, flops=TPD * 2 * BLK**3, moved=4 << 20,
        )(*lists, tile_vals, owned)
        if last:
            early = call(
                early_kernel, "early", [whole(SMEM)] + [whole()] * (1 + NX), [((PAIRS, BLK, BLK), f32, VMEM)]
            )(x_only, weights, *spread)
        if last:
            outs = [((PAIRS * BLK + 32, BLK), bf16, VMEM)]
        else:
            outs = [((PAIRS, BLK, BLK), f32, VMEM), ((BPD, BLK), f32, VMEM)]
        result = call(
            functools.partial(far_kernel, hop), "far", [whole(SMEM)] * 4 + [whole(HBM), whole(), whole(), whole(HBM)], outs,
            [
                VMEM((BUCKETS, BLK, BLK), f32),
                VMEM((WIDTH, BPD * BLK), f32),
            ] + ring + [DMA(())],
            limit=ROOM, flops=TPD * 2 * BLK**3, moved=8 << 20,
        )(*lists, tile_vals, got, part, noise)
        if not last:
            packed, squares = result
    tails = [result] + [shift_by(result, "x", shift) for shift in SHIFTS[1:]]
    return call(
        final_kernel, "final", [whole(SMEM)] + [whole()] * (2 + NX), [((WIDTH, BPD * BLK), bf16, VMEM)]
    )(x_only, weights, early, *tails).T


def solution(mesh):
    grid = Mesh(np.array(mesh.devices).reshape(NY, NZ, NC, NX), ("y", "z", "core", "x"))
    row = ("y", "z", "core")
    in_specs = (
        P(row, "x"),
        P(row, None, None),
        P(row, None),
        P(row, None),
        P(row),
        P(row, None, None),
        P(None, row, "x"),
        P(),
    )
    return jax.shard_map(shards, mesh=grid, in_specs=in_specs, out_specs=P(row, "x"), check_vma=False)
```

```python
import functools

import jax
import jax.numpy as jnp
import numpy as np
from jax import lax
from jax.experimental import pallas as pl
from jax.experimental.pallas import tpu as pltpu
from jax.sharding import Mesh, PartitionSpec as P

BLK = 128
BPD = 8
TPD = 160
PAIRS = BPD // 2
HOPS = 2
NY, NZ, NC, NX = 4, 8, 2, 4
WIDTH = 64
GROUP = 4
BUCKETS = 2 * BPD
MAXG = TPD // GROUP + BUCKETS
SLOTS = MAXG * GROUP
SHIFTS = (0, 2, 1, 3)
ZSHIFTS = (0, 4, 3, 5, 2, 6, 1, 7)
HALF = BLK // 2
DEPTH = 10
FULL = 63 << 20
MOST = 66_200_000
ROOM = 63_600_000
EPS = 1e-06
bf16 = jnp.bfloat16
f32 = jnp.float32
VMEM = pltpu.VMEM
SMEM = pltpu.SMEM
HBM = pltpu.HBM
DMA = pltpu.SemaphoreType.DMA


def lane_low(shape):
    return lax.broadcasted_iota(jnp.int32, shape, len(shape) - 1) < WIDTH


def pair_squares(pair_values):
    total = jnp.zeros((BPD, BLK), f32)
    row = lax.broadcasted_iota(jnp.int32, (BPD, BLK), 0)
    half = lax.broadcasted_iota(jnp.int32, (BPD, BLK), 1) // WIDTH
    for p in range(PAIRS):
        v = pair_values[p]
        pick = jnp.where(row == 2 * p + half, 1.0, 0.0).astype(f32)
        total = total + lax.dot_general(
            pick, v * v, (((1,), (1,)), ((), ())),
            precision=lax.Precision.HIGHEST, preferred_element_type=f32,
        )
    return total


def row_scale(total):
    return (1.0 / jnp.sqrt(total + EPS)).T


def pair_scale(columns, p):
    return jnp.where(
        lane_low((BLK, BLK)),
        jnp.broadcast_to(columns[:, 2 * p : 2 * p + 1], (BLK, BLK)),
        jnp.broadcast_to(columns[:, 2 * p + 1 : 2 * p + 2], (BLK, BLK)),
    )


def swap_halves(v):
    return pltpu.roll(v, WIDTH, 1)


def stacked_pair(ref, p):
    first = ref[:, (2 * p) * BLK : (2 * p + 1) * BLK].astype(f32)
    second = ref[:, (2 * p + 1) * BLK : (2 * p + 2) * BLK].astype(f32)
    return jnp.concatenate([first, second], axis=0)


def pack_kernel(feat_ref, out_ref, sq_ref):
    rows = []
    for p in range(PAIRS):
        stacked = stacked_pair(feat_ref, p)
        out_ref[p] = stacked.T.astype(bf16)
        squares = stacked * stacked
        rows.append(jnp.sum(squares[:WIDTH], axis=0, keepdims=True))
        rows.append(jnp.sum(squares[WIDTH:], axis=0, keepdims=True))
    sq_ref[...] = jnp.concatenate(rows, axis=0)


def norm_kernel(hop, raw_ref, sq_ref, *rest):
    columns = row_scale(sq_ref[...])
    before_ref = rest[0] if hop else None
    out_ref, second_ref, own_ref, buf, sem = rest[-5:]
    copies = []
    for p in range(PAIRS):
        v = (raw_ref[p].astype(f32) * pair_scale(columns, p)).astype(bf16)
        buf[p] = v[:HALF]
        second_ref[p] = v[HALF:]
        own_ref[hop, p] = v
    for z in range(NZ):
        copy = pltpu.make_async_copy(buf, out_ref.at[z], sem.at[z])
        copy.start()
        copies.append(copy)
    if hop:
        own_ref[0:hop] = before_ref[...]
    for copy in copies:
        copy.wait()


def pick_kernel(direct, me_ref, idx_ref, *refs):
    z_refs = refs[: NZ if direct else 1]
    out_ref, slots, buf, sem = refs[len(z_refs) :]
    for j in range(NZ):
        z = (me_ref[1] + NZ - ZSHIFTS[j]) % NZ if direct else j
        for p in range(PAIRS):
            v = z_refs[j][p] if direct else z_refs[0][j, p]
            slots[z * BPD + p] = v
            slots[z * BPD + PAIRS + p] = jnp.concatenate([v[:, WIDTH:], v[:, :WIDTH]], axis=1)
    mask = lane_low((HALF, BLK))
    mine = me_ref[0] * NC + me_ref[2]
    copies = []
    for dest in range(NY * NC):
        for z in range(NZ):
            i = dest * NZ + z
            buf[i] = jnp.where(mask, slots[idx_ref[2 * i]], slots[idx_ref[2 * i + 1]])

        @pl.when(mine == dest)
        def _():
            buf[dest * NZ + me_ref[1]] = jnp.zeros((HALF, BLK), bf16)

        copy = pltpu.make_async_copy(
            buf.at[pl.ds(dest * NZ, NZ)], out_ref.at[pl.ds(dest * NZ, NZ)], sem.at[dest]
        )
        copy.start()
        copies.append(copy)
    for copy in copies:
        copy.wait()


def order_kernel(me_ref, rows_ref, srcs_ref, count_ref, tile_ref, slab_ref, into_ref, groups_ref, fill, begin):
    count = count_ref[0]
    empty = (me_ref[0] * NC + me_ref[2]) * NZ + me_ref[1]

    @pl.loop(0, SLOTS // 8)
    def _(i):
        for j in range(8):
            tile_ref[i * 8 + j] = 0
            tile_ref[SLOTS + i * 8 + j] = 0
            slab_ref[i * 8 + j] = PAIRS
            slab_ref[SLOTS + i * 8 + j] = empty

    @pl.loop(0, 2 * MAXG)
    def _(i):
        into_ref[i] = 0

    for b in range(2 * BUCKETS):
        fill[b] = 0

    def bucket_of(t):
        s = srcs_ref[t]
        return jnp.where(s < BPD, 0, BUCKETS) + rows_ref[t] * 2 + s % 2

    @pl.loop(0, count)
    def _(t):
        b = bucket_of(t)
        fill[b] = fill[b] + 1

    for kind in range(2):
        def place(b, group):
            size = (fill[kind * BUCKETS + b] + GROUP - 1) // GROUP
            begin[kind * BUCKETS + b] = (kind * MAXG + group) * GROUP

            @pl.loop(0, size)
            def _(i):
                into_ref[kind * MAXG + group + i] = b

            return group + size

        groups_ref[kind] = lax.fori_loop(0, BUCKETS, place, jnp.int32(0))

    @pl.loop(0, count)
    def _(t):
        b = bucket_of(t)
        at = begin[b]
        begin[b] = at + 1
        s = srcs_ref[t]
        o = (s - BPD) // 2
        y = o // (NZ * NC)
        z = (o // NC) % NZ
        k = o % NC
        tile_ref[at] = t
        slab_ref[at] = jnp.where(s < BPD, s // 2, (y * NC + k) * NZ + z)


def add_groups(kind, tile_ref, slab_ref, into_ref, groups_ref, tiles_ref, srcs, acc, ring, sem):
    steps = (groups_ref[kind] + 1) // 2

    def copies(step):
        slot = step % DEPTH
        first = (kind * MAXG + 2 * step) * GROUP
        return [
            pltpu.make_async_copy(tiles_ref.at[tile_ref[first + j]], ring.at[slot, j], sem.at[slot, j])
            for j in range(2 * GROUP)
        ]

    def begin(step):
        @pl.when(step < steps)
        def _():
            for copy in copies(step):
                copy.start()

    def run(step, carry):
        slot = step % DEPTH
        group = kind * MAXG + 2 * step
        for copy in copies(step):
            copy.wait()
        parts = []
        for h in range(2):
            left = jnp.concatenate([ring[slot, h * GROUP + j] for j in range(GROUP)], axis=1)
            right = jnp.concatenate([src[slab_ref[(group + h) * GROUP + j]] for j in range(GROUP) for src in srcs], axis=0)
            parts.append(jnp.dot(left, right, preferred_element_type=f32))
        for h in range(2):
            acc[into_ref[group + h]] += parts[h]
        begin(step + DEPTH)
        return carry

    return begin, lambda: lax.fori_loop(0, steps, run, 0)


def own_kernel(hop, tile_ref, slab_ref, into_ref, groups_ref, tiles_ref, own_ref, acc_ref, src, ring, sem):
    begin, run = add_groups(0, tile_ref, slab_ref, into_ref, groups_ref, tiles_ref, (src,), acc_ref, ring, sem)
    for step in range(DEPTH):
        begin(step)
    acc_ref[...] = jnp.zeros_like(acc_ref)
    src[0:PAIRS] = own_ref[hop]
    src[PAIRS] = jnp.zeros((BLK, BLK), bf16)
    run()


def far_kernel(hop, tile_ref, slab_ref, into_ref, groups_ref, tiles_ref, first_ref, second_ref, part_ref, noise_ref, *rest):
    last = hop == HOPS - 1
    if last:
        out_ref, acc, noise, ring, sem, load = rest
    else:
        out_ref, sq_ref, acc, noise, ring, sem, load = rest
    begin, run = add_groups(1, tile_ref, slab_ref, into_ref, groups_ref, tiles_ref, (first_ref, second_ref), acc, ring, sem)
    for step in range(DEPTH):
        begin(step)
    noise_copy = pltpu.make_async_copy(noise_ref.at[hop], noise, load)
    noise_copy.start()
    acc[...] = part_ref[...]
    run()
    noise_copy.wait()
    mask = lane_low((BLK, BLK))
    pairs = []
    for p in range(PAIRS):
        u = stacked_pair(noise, p).T + jnp.where(
            mask,
            acc[4 * p] + swap_halves(acc[4 * p + 1]),
            swap_halves(acc[4 * p + 2]) + acc[4 * p + 3],
        )
        pairs.append(u)
        if last:
            out_ref[p * BLK : (p + 1) * BLK] = u.astype(bf16)
        else:
            out_ref[p] = u
    total = pair_squares(pairs)
    if last:
        hi = total.astype(bf16).astype(f32)
        mid = (total - hi).astype(bf16).astype(f32)
        lo = total - hi - mid
        out_ref[PAIRS * BLK : PAIRS * BLK + 16] = jnp.concatenate([hi, mid], axis=0).astype(bf16)
        out_ref[PAIRS * BLK + 16 : PAIRS * BLK + 32] = jnp.concatenate([lo, jnp.zeros_like(lo)], axis=0).astype(bf16)
    else:
        sq_ref[...] = total


def early_kernel(x_ref, w_ref, *refs):
    h_refs, out_ref = refs[:-1], refs[-1]
    for p in range(PAIRS):
        total = jnp.zeros((BLK, BLK), f32)
        for k in range(HOPS):
            for j, shift in enumerate(SHIFTS):
                source = (x_ref[0] + NX - shift) % NX
                total = total + jnp.dot(h_refs[j][k, p], w_ref[k, source], preferred_element_type=f32)
        out_ref[p] = total


def final_kernel(x_ref, w_ref, early_ref, *refs):
    got_refs, out_ref = refs[:-1], refs[-1]
    total = jnp.zeros((BPD, BLK), f32)
    for got_ref in got_refs:
        a = got_ref[PAIRS * BLK : PAIRS * BLK + 16].astype(f32)
        b = got_ref[PAIRS * BLK + 16 : PAIRS * BLK + 32].astype(f32)
        total = total + (a[:BPD] + a[BPD:] + b[:BPD])
    columns = row_scale(total)
    for p in range(PAIRS):
        raw = jnp.zeros((BLK, BLK), f32)
        for j, shift in enumerate(SHIFTS):
            source = (x_ref[0] + NX - shift) % NX
            raw = raw + jnp.dot(got_refs[j][p * BLK : (p + 1) * BLK], w_ref[HOPS, source], preferred_element_type=f32)
        v = (early_ref[p] + raw * pair_scale(columns, p)).T
        out_ref[:, (2 * p) * BLK : (2 * p + 1) * BLK] = v[:WIDTH].astype(bf16)
        out_ref[:, (2 * p + 1) * BLK : (2 * p + 2) * BLK] = v[WIDTH:].astype(bf16)


def whole(space=VMEM):
    return pl.BlockSpec(memory_space=space)


def call(kernel, name, in_specs, outs, scratch=(), limit=24 << 20, flops=1 << 20, moved=1 << 20):
    shapes = [jax.ShapeDtypeStruct(dims, kind) for dims, kind, _ in outs]
    specs = [whole(space) for _, _, space in outs]
    single = len(outs) == 1
    return pl.pallas_call(
        kernel,
        name=name,
        out_shape=shapes[0] if single else shapes,
        in_specs=in_specs,
        out_specs=specs[0] if single else specs,
        scratch_shapes=list(scratch),
        compiler_params=pltpu.CompilerParams(vmem_limit_bytes=limit),
        cost_estimate=pl.CostEstimate(flops=flops, bytes_accessed=moved, transcendentals=0),
    )


def shift_by(value, axis, shift):
    size = lax.axis_size(axis)
    return lax.ppermute(value, axis, [(i, (i + shift) % size) for i in range(size)])


def shards(features, tile_vals, tile_rows, tile_srcs, tile_count, needed, hop_noise, enc_weight):
    me = jnp.stack([lax.axis_index("y"), lax.axis_index("z"), lax.axis_index("core")]).astype(jnp.int32)
    x_index = lax.axis_index("x").astype(jnp.int32)
    x_only = x_index.reshape(1)
    noise = hop_noise.transpose(0, 2, 1)

    packed, squares = call(
        pack_kernel, "pack", [whole()],
        [((PAIRS, BLK, BLK), bf16, VMEM), ((BPD, BLK), f32, VMEM)],
    )(features.T)
    packed, squares, needed, rows, srcs, count, enc_weight, tile_vals = lax.optimization_barrier(
        (packed, squares, needed.reshape(-1), tile_rows.reshape(-1), tile_srcs.reshape(-1), tile_count, enc_weight, tile_vals)
    )

    weights = lax.dynamic_slice_in_dim(enc_weight, x_index * WIDTH, WIDTH, axis=2).reshape(HOPS + 1, NX, WIDTH, WIDTH)
    nothing = jnp.zeros_like(weights)
    weights = jnp.concatenate(
        [jnp.concatenate([weights, nothing], axis=-1), jnp.concatenate([nothing, weights], axis=-1)], axis=-2
    )
    lists = call(
        order_kernel, "order", [whole(SMEM)] * 4,
        [((2 * SLOTS,), jnp.int32, SMEM), ((2 * SLOTS,), jnp.int32, SMEM), ((2 * MAXG,), jnp.int32, SMEM), ((2,), jnp.int32, SMEM)],
        [SMEM((2 * BUCKETS,), jnp.int32), SMEM((2 * BUCKETS,), jnp.int32)],
    )(me, rows, srcs, count)
    table = None
    for hop in range(HOPS):
        last = hop == HOPS - 1
        total = lax.psum(squares, "x")
        before = [owned] if hop else []
        first, second, owned = call(
            functools.partial(norm_kernel, hop), "norm", [whole()] * (2 + hop),
            [
                ((NZ, PAIRS, HALF, BLK), bf16, HBM),
                ((PAIRS, HALF, BLK), bf16, VMEM),
                ((hop + 1, PAIRS, BLK, BLK), bf16, VMEM),
            ],
            [VMEM((PAIRS, HALF, BLK), bf16), DMA((NZ,))],
            limit=MOST,
        )(packed, total, *before)
        if last:
            spread = [owned] + [shift_by(owned, "x", shift) for shift in SHIFTS[1:]]
        along = [lax.all_to_all(first, "z", 0, 0, tiled=True)]
        direct = [second] + [shift_by(second, "z", shift) for shift in ZSHIFTS[1:]]
        if table is None:
            needed, owned = lax.optimization_barrier((needed, owned))
            asked = lax.all_gather(needed, ("y", "core"), axis=0).reshape(NY * NC, NY, NZ, NC, 2)
            asked = lax.dynamic_slice(asked, (0, me[0], 0, me[2], 0), (NY * NC, 1, NZ, 1, 2)).reshape(NY * NC, NZ, 2)
            odd = (asked % 2) ^ jnp.arange(2, dtype=jnp.int32)
            table = (jnp.arange(NZ, dtype=jnp.int32)[:, None] * BPD + asked // 2 + PAIRS * odd).reshape(-1)
        got = []
        at = me
        for inputs in (along, direct):
            picked = call(
                functools.partial(pick_kernel, inputs is direct), "pick", [whole(SMEM)] * 2 + [whole()] * len(inputs),
                [((NY * NC * NZ, HALF, BLK), bf16, HBM)],
                [VMEM((NZ * BPD, HALF, BLK), bf16), VMEM((NY * NC * NZ, HALF, BLK), bf16), DMA((NY * NC,))],
                limit=MOST,
            )(at, table, *inputs)
            picked, at = lax.optimization_barrier((picked, at))
            got.append(lax.all_to_all(picked, ("y", "core"), 0, 0, tiled=True))
        ring = [VMEM((DEPTH, 2 * GROUP, BLK, BLK), bf16), DMA((DEPTH, 2 * GROUP))]
        part = call(
            functools.partial(own_kernel, hop), "own", [whole(SMEM)] * 4 + [whole(HBM), whole()], [((BUCKETS, BLK, BLK), f32, VMEM)],
            [VMEM((PAIRS + 1, BLK, BLK), bf16)] + ring,
            limit=FULL, flops=TPD * 2 * BLK**3, moved=4 << 20,
        )(*lists, tile_vals, owned)
        if last:
            early = call(
                early_kernel, "early", [whole(SMEM)] + [whole()] * (1 + NX), [((PAIRS, BLK, BLK), f32, VMEM)]
            )(x_only, weights, *spread)
            early, part = lax.optimization_barrier((early, part))
        if last:
            outs = [((PAIRS * BLK + 32, BLK), bf16, VMEM)]
        else:
            outs = [((PAIRS, BLK, BLK), f32, VMEM), ((BPD, BLK), f32, VMEM)]
        result = call(
            functools.partial(far_kernel, hop), "far", [whole(SMEM)] * 4 + [whole(HBM), whole(), whole(), whole(), whole(HBM)], outs,
            [
                VMEM((BUCKETS, BLK, BLK), f32),
                VMEM((WIDTH, BPD * BLK), f32),
            ] + ring + [DMA(())],
            limit=ROOM, flops=TPD * 2 * BLK**3, moved=8 << 20,
        )(*lists, tile_vals, *got, part, noise)
        if not last:
            packed, squares = result
    tails = [result] + [shift_by(result, "x", shift) for shift in SHIFTS[1:]]
    return call(
        final_kernel, "final", [whole(SMEM)] + [whole()] * (2 + NX), [((WIDTH, BPD * BLK), bf16, VMEM)]
    )(x_only, weights, early, *tails).T


def solution(mesh):
    grid = Mesh(np.array(mesh.devices).reshape(NY, NZ, NC, NX), ("y", "z", "core", "x"))
    row = ("y", "z", "core")
    in_specs = (
        P(row, "x"),
        P(row, None, None),
        P(row, None),
        P(row, None),
        P(row),
        P(row, None, None),
        P(None, row, "x"),
        P(),
    )
    return jax.shard_map(shards, mesh=grid, in_specs=in_specs, out_specs=P(row, "x"), check_vma=False)
```

```python
import functools

import jax
import jax.numpy as jnp
import numpy as np
from jax import lax
from jax.experimental import pallas as pl
from jax.experimental.pallas import tpu as pltpu
from jax.sharding import Mesh, PartitionSpec as P

BLK = 128
BPD = 8
TPD = 160
PAIRS = BPD // 2
HOPS = 2
NY, NZ, NC, NX = 4, 8, 2, 4
WIDTH = 64
GROUP = 4
STEP = 4
BUCKETS = 2 * BPD
MAXG = TPD // GROUP + BUCKETS
SLOTS = MAXG * GROUP
SHIFTS = (0, 2, 1, 3)
ZSHIFTS = (0, 4, 3, 5, 2, 6, 1, 7)
DEPTH = 4
FULL = 63 << 20
MOST = 65_000_000
TIGHT = 66_200_000
ROOM = 63_600_000
EPS = 1e-06
bf16 = jnp.bfloat16
f32 = jnp.float32
VMEM = pltpu.VMEM
SMEM = pltpu.SMEM
HBM = pltpu.HBM
DMA = pltpu.SemaphoreType.DMA


def lane_low(shape):
    return lax.broadcasted_iota(jnp.int32, shape, len(shape) - 1) < WIDTH


def pair_squares(pair_values):
    total = jnp.zeros((BPD, BLK), f32)
    row = lax.broadcasted_iota(jnp.int32, (BPD, BLK), 0)
    half = lax.broadcasted_iota(jnp.int32, (BPD, BLK), 1) // WIDTH
    for p in range(PAIRS):
        v = pair_values[p]
        pick = jnp.where(row == 2 * p + half, 1.0, 0.0).astype(f32)
        total = total + lax.dot_general(
            pick, v * v, (((1,), (1,)), ((), ())),
            precision=lax.Precision.HIGHEST, preferred_element_type=f32,
        )
    return total


def row_scale(total):
    return (1.0 / jnp.sqrt(total + EPS)).T


def pair_scale(columns, p):
    return jnp.where(
        lane_low((BLK, BLK)),
        jnp.broadcast_to(columns[:, 2 * p : 2 * p + 1], (BLK, BLK)),
        jnp.broadcast_to(columns[:, 2 * p + 1 : 2 * p + 2], (BLK, BLK)),
    )


def swap_halves(v):
    return pltpu.roll(v, WIDTH, 1)


def stacked_pair(ref, p):
    first = ref[:, (2 * p) * BLK : (2 * p + 1) * BLK].astype(f32)
    second = ref[:, (2 * p + 1) * BLK : (2 * p + 2) * BLK].astype(f32)
    return jnp.concatenate([first, second], axis=0)


def pack_kernel(feat_ref, out_ref, sq_ref):
    rows = []
    for p in range(PAIRS):
        stacked = stacked_pair(feat_ref, p)
        out_ref[p] = stacked.T.astype(bf16)
        squares = stacked * stacked
        rows.append(jnp.sum(squares[:WIDTH], axis=0, keepdims=True))
        rows.append(jnp.sum(squares[WIDTH:], axis=0, keepdims=True))
    sq_ref[...] = jnp.concatenate(rows, axis=0)


def norm_kernel(raw_ref, sq_ref, out_ref, own_ref, buf, sem):
    columns = row_scale(sq_ref[...])
    copies = []
    for p in range(PAIRS):
        v = (raw_ref[p].astype(f32) * pair_scale(columns, p)).astype(bf16)
        buf[p] = v
        own_ref[0, p] = v
    for z in range(NZ):
        copy = pltpu.make_async_copy(buf, out_ref.at[z], sem.at[z])
        copy.start()
        copies.append(copy)
    for copy in copies:
        copy.wait()


def pick_kernel(raw, me_ref, idx_ref, z_ref, *refs):
    out_ref, slots, buf, sem = refs[0], *refs[-3:]
    if raw:
        u_ref, before_ref = refs[0], refs[1]
        sum_refs = refs[2 : 2 + NZ]
        out_ref, own_ref = refs[2 + NZ], refs[3 + NZ]
        columns = row_scale(sum_refs[0][...])
        for p in range(PAIRS):
            own_ref[1, p] = (u_ref[p] * pair_scale(columns, p)).astype(bf16)
        own_ref[0] = before_ref[0]
    for j in range(NZ):
        z = (me_ref[1] + NZ - ZSHIFTS[j]) % NZ if raw else j
        if raw:
            columns = row_scale(sum_refs[j][...])
        for p in range(PAIRS):
            v = z_ref[z, p]
            if raw:
                v = (v.astype(f32) * pair_scale(columns, p)).astype(bf16)
            slots[z * BPD + p] = v
            slots[z * BPD + PAIRS + p] = jnp.concatenate([v[:, WIDTH:], v[:, :WIDTH]], axis=1)
    mask = lane_low((BLK, BLK))
    mine = me_ref[0] * NC + me_ref[2]
    copies = []
    for dest in range(NY * NC):
        for z in range(NZ):
            i = dest * NZ + z
            buf[i] = jnp.where(mask, slots[idx_ref[2 * i]], slots[idx_ref[2 * i + 1]])

        @pl.when(mine == dest)
        def _():
            buf[dest * NZ + me_ref[1]] = jnp.zeros((BLK, BLK), bf16)

        copy = pltpu.make_async_copy(
            buf.at[pl.ds(dest * NZ, NZ)], out_ref.at[pl.ds(dest * NZ, NZ)], sem.at[dest]
        )
        copy.start()
        copies.append(copy)
    for copy in copies:
        copy.wait()


def order_kernel(me_ref, rows_ref, srcs_ref, count_ref, tile_ref, slab_ref, into_ref, groups_ref, fill, begin):
    count = count_ref[0]
    empty = (me_ref[0] * NC + me_ref[2]) * NZ + me_ref[1]

    @pl.loop(0, SLOTS // 8)
    def _(i):
        for j in range(8):
            tile_ref[i * 8 + j] = 0
            tile_ref[SLOTS + i * 8 + j] = 0
            slab_ref[i * 8 + j] = PAIRS
            slab_ref[SLOTS + i * 8 + j] = empty

    @pl.loop(0, 2 * MAXG)
    def _(i):
        into_ref[i] = 0

    for b in range(2 * BUCKETS):
        fill[b] = 0

    def bucket_of(t):
        s = srcs_ref[t]
        return jnp.where(s < BPD, 0, BUCKETS) + rows_ref[t] * 2 + s % 2

    @pl.loop(0, count)
    def _(t):
        b = bucket_of(t)
        fill[b] = fill[b] + 1

    for kind in range(2):
        def place(b, group):
            size = (fill[kind * BUCKETS + b] + GROUP - 1) // GROUP
            begin[kind * BUCKETS + b] = (kind * MAXG + group) * GROUP

            @pl.loop(0, size)
            def _(i):
                into_ref[kind * MAXG + group + i] = b

            return group + size

        groups_ref[kind] = lax.fori_loop(0, BUCKETS, place, jnp.int32(0))

    @pl.loop(0, count)
    def _(t):
        b = bucket_of(t)
        at = begin[b]
        begin[b] = at + 1
        s = srcs_ref[t]
        o = (s - BPD) // 2
        y = o // (NZ * NC)
        z = (o // NC) % NZ
        k = o % NC
        tile_ref[at] = t
        slab_ref[at] = jnp.where(s < BPD, s // 2, (y * NC + k) * NZ + z)


def add_groups(kind, tile_ref, slab_ref, into_ref, groups_ref, tiles_ref, src, acc, ring, sem):
    steps = (groups_ref[kind] + STEP - 1) // STEP

    def copies(step):
        slot = step % DEPTH
        first = (kind * MAXG + STEP * step) * GROUP
        return [
            pltpu.make_async_copy(tiles_ref.at[tile_ref[first + j]], ring.at[slot, j], sem.at[slot, j])
            for j in range(STEP * GROUP)
        ]

    def begin(step):
        @pl.when(step < steps)
        def _():
            for copy in copies(step):
                copy.start()

    def run(step, carry):
        slot = step % DEPTH
        group = kind * MAXG + STEP * step
        for copy in copies(step):
            copy.wait()
        parts = []
        for h in range(STEP):
            left = jnp.concatenate([ring[slot, h * GROUP + j] for j in range(GROUP)], axis=1)
            right = jnp.concatenate([src[slab_ref[(group + h) * GROUP + j]] for j in range(GROUP)], axis=0)
            parts.append(jnp.dot(left, right, preferred_element_type=f32))
        for h in range(STEP):
            acc[into_ref[group + h]] += parts[h]
        begin(step + DEPTH)
        return carry

    return begin, lambda: lax.fori_loop(0, steps, run, 0)


def fold(acc, p):
    return jnp.where(
        lane_low((BLK, BLK)),
        acc[4 * p] + swap_halves(acc[4 * p + 1]),
        swap_halves(acc[4 * p + 2]) + acc[4 * p + 3],
    )


def own_kernel(hop, tile_ref, slab_ref, into_ref, groups_ref, tiles_ref, own_ref, noise_ref, part_ref, acc, src, noise, ring, sem, load):
    begin, run = add_groups(0, tile_ref, slab_ref, into_ref, groups_ref, tiles_ref, src, acc, ring, sem)
    for step in range(DEPTH):
        begin(step)
    noise_copy = pltpu.make_async_copy(noise_ref.at[hop], noise, load)
    noise_copy.start()
    acc[...] = jnp.zeros_like(acc)
    src[0:PAIRS] = own_ref[hop]
    src[PAIRS] = jnp.zeros((BLK, BLK), bf16)
    run()
    noise_copy.wait()
    for p in range(PAIRS):
        part_ref[p] = stacked_pair(noise, p).T + fold(acc, p)


def far_kernel(hop, tile_ref, slab_ref, into_ref, groups_ref, tiles_ref, got_ref, part_ref, *rest):
    last = hop == HOPS - 1
    if last:
        out_ref, acc, ring, sem = rest
    else:
        out_ref, u_ref, sq_ref, acc, ring, sem, buf, out_sem = rest
    begin, run = add_groups(1, tile_ref, slab_ref, into_ref, groups_ref, tiles_ref, got_ref, acc, ring, sem)
    for step in range(DEPTH):
        begin(step)
    acc[...] = jnp.zeros_like(acc)
    run()
    pairs = []
    for p in range(PAIRS):
        u = part_ref[p] + fold(acc, p)
        pairs.append(u)
        if last:
            out_ref[p * BLK : (p + 1) * BLK] = u.astype(bf16)
        else:
            buf[p] = u.astype(bf16)
            u_ref[p] = u
    if not last:
        copies = [pltpu.make_async_copy(buf, out_ref.at[z], out_sem.at[z]) for z in range(NZ)]
        for copy in copies:
            copy.start()
    total = pair_squares(pairs)
    if last:
        hi = total.astype(bf16).astype(f32)
        mid = (total - hi).astype(bf16).astype(f32)
        lo = total - hi - mid
        out_ref[PAIRS * BLK : PAIRS * BLK + 16] = jnp.concatenate([hi, mid], axis=0).astype(bf16)
        out_ref[PAIRS * BLK + 16 : PAIRS * BLK + 32] = jnp.concatenate([lo, jnp.zeros_like(lo)], axis=0).astype(bf16)
    else:
        sq_ref[...] = total
        for copy in copies:
            copy.wait()


def early_kernel(x_ref, w_ref, *refs):
    h_refs, out_ref = refs[:-1], refs[-1]
    for p in range(PAIRS):
        total = jnp.zeros((BLK, BLK), f32)
        for k in range(HOPS):
            for j, shift in enumerate(SHIFTS):
                source = (x_ref[0] + NX - shift) % NX
                total = total + jnp.dot(h_refs[j][k, p], w_ref[k, source], preferred_element_type=f32)
        out_ref[p] = total


def final_kernel(x_ref, w_ref, early_ref, *refs):
    got_refs, out_ref = refs[:-1], refs[-1]
    total = jnp.zeros((BPD, BLK), f32)
    for got_ref in got_refs:
        a = got_ref[PAIRS * BLK : PAIRS * BLK + 16].astype(f32)
        b = got_ref[PAIRS * BLK + 16 : PAIRS * BLK + 32].astype(f32)
        total = total + (a[:BPD] + a[BPD:] + b[:BPD])
    columns = row_scale(total)
    for p in range(PAIRS):
        raw = jnp.zeros((BLK, BLK), f32)
        for j, shift in enumerate(SHIFTS):
            source = (x_ref[0] + NX - shift) % NX
            raw = raw + jnp.dot(got_refs[j][p * BLK : (p + 1) * BLK], w_ref[HOPS, source], preferred_element_type=f32)
        v = (early_ref[p] + raw * pair_scale(columns, p)).T
        out_ref[:, (2 * p) * BLK : (2 * p + 1) * BLK] = v[:WIDTH].astype(bf16)
        out_ref[:, (2 * p + 1) * BLK : (2 * p + 2) * BLK] = v[WIDTH:].astype(bf16)


def whole(space=VMEM):
    return pl.BlockSpec(memory_space=space)


def call(kernel, name, in_specs, outs, scratch=(), limit=24 << 20, flops=1 << 20, moved=1 << 20):
    shapes = [jax.ShapeDtypeStruct(dims, kind) for dims, kind, _ in outs]
    specs = [whole(space) for _, _, space in outs]
    single = len(outs) == 1
    return pl.pallas_call(
        kernel,
        name=name,
        out_shape=shapes[0] if single else shapes,
        in_specs=in_specs,
        out_specs=specs[0] if single else specs,
        scratch_shapes=list(scratch),
        compiler_params=pltpu.CompilerParams(vmem_limit_bytes=limit),
        cost_estimate=pl.CostEstimate(flops=flops, bytes_accessed=moved, transcendentals=0),
    )


def shift_by(value, axis, shift):
    size = lax.axis_size(axis)
    return lax.ppermute(value, axis, [(i, (i + shift) % size) for i in range(size)])


def shards(features, tile_vals, tile_rows, tile_srcs, tile_count, needed, hop_noise, enc_weight):
    me = jnp.stack([lax.axis_index("y"), lax.axis_index("z"), lax.axis_index("core")]).astype(jnp.int32)
    x_index = lax.axis_index("x").astype(jnp.int32)
    x_only = x_index.reshape(1)
    noise = hop_noise.transpose(0, 2, 1)

    packed, squares = call(
        pack_kernel, "pack", [whole()],
        [((PAIRS, BLK, BLK), bf16, VMEM), ((BPD, BLK), f32, VMEM)],
    )(features.T)
    packed, squares, needed, rows, srcs, count, enc_weight, tile_vals = lax.optimization_barrier(
        (packed, squares, needed.reshape(-1), tile_rows.reshape(-1), tile_srcs.reshape(-1), tile_count, enc_weight, tile_vals)
    )

    weights = lax.dynamic_slice_in_dim(enc_weight, x_index * WIDTH, WIDTH, axis=2).reshape(HOPS + 1, NX, WIDTH, WIDTH)
    nothing = jnp.zeros_like(weights)
    weights = jnp.concatenate(
        [jnp.concatenate([weights, nothing], axis=-1), jnp.concatenate([nothing, weights], axis=-1)], axis=-2
    )
    lists = call(
        order_kernel, "order", [whole(SMEM)] * 4,
        [((2 * SLOTS,), jnp.int32, SMEM), ((2 * SLOTS,), jnp.int32, SMEM), ((2 * MAXG,), jnp.int32, SMEM), ((2,), jnp.int32, SMEM)],
        [SMEM((2 * BUCKETS,), jnp.int32), SMEM((2 * BUCKETS,), jnp.int32)],
    )(me, rows, srcs, count)
    table = None
    for hop in range(HOPS):
        last = hop == HOPS - 1
        total = lax.psum(squares, "x")
        if not hop:
            packed, owned = call(
                norm_kernel, "norm", [whole()] * 2,
                [((NZ, PAIRS, BLK, BLK), bf16, HBM), ((1, PAIRS, BLK, BLK), bf16, VMEM)],
                [VMEM((PAIRS, BLK, BLK), bf16), DMA((NZ,))],
                limit=TIGHT,
            )(packed, total)
        along = lax.all_to_all(packed, "z", 0, 0, tiled=True)
        if table is None:
            needed, owned = lax.optimization_barrier((needed, owned))
            asked = lax.all_gather(needed, ("y", "core"), axis=0).reshape(NY * NC, NY, NZ, NC, 2)
            asked = lax.dynamic_slice(asked, (0, me[0], 0, me[2], 0), (NY * NC, 1, NZ, 1, 2)).reshape(NY * NC, NZ, 2)
            odd = (asked % 2) ^ jnp.arange(2, dtype=jnp.int32)
            table = (jnp.arange(NZ, dtype=jnp.int32)[:, None] * BPD + asked // 2 + PAIRS * odd).reshape(-1)
        scratch = [VMEM((NZ * BPD, BLK, BLK), bf16), VMEM((NY * NC * NZ, BLK, BLK), bf16), DMA((NY * NC,))]
        outs = [((NY * NC * NZ, BLK, BLK), bf16, HBM)]
        if hop:
            totals = [total] + [shift_by(total, "z", shift) for shift in ZSHIFTS[1:]]
            picked, owned = call(
                functools.partial(pick_kernel, True), "pick", [whole(SMEM)] * 2 + [whole()] * (3 + NZ),
                outs + [((2, PAIRS, BLK, BLK), bf16, VMEM)], scratch, limit=MOST,
            )(me, table, along, values, owned, *totals)
            spread = [owned] + [shift_by(owned, "x", shift) for shift in SHIFTS[1:]]
        else:
            picked = call(
                functools.partial(pick_kernel, False), "pick", [whole(SMEM)] * 2 + [whole()], outs, scratch, limit=MOST
            )(me, table, along)
        got = lax.all_to_all(picked, ("y", "core"), 0, 0, tiled=True)
        ring = [VMEM((DEPTH, STEP * GROUP, BLK, BLK), bf16), DMA((DEPTH, STEP * GROUP))]
        part = call(
            functools.partial(own_kernel, hop), "own", [whole(SMEM)] * 4 + [whole(HBM), whole(), whole(HBM)],
            [((PAIRS, BLK, BLK), f32, VMEM)],
            [VMEM((BUCKETS, BLK, BLK), f32), VMEM((PAIRS + 1, BLK, BLK), bf16), VMEM((WIDTH, BPD * BLK), f32)] + ring + [DMA(())],
            limit=FULL, flops=TPD * 2 * BLK**3, moved=4 << 20,
        )(*lists, tile_vals, owned, noise)
        if last:
            early = call(
                early_kernel, "early", [whole(SMEM)] + [whole()] * (1 + NX), [((PAIRS, BLK, BLK), f32, VMEM)]
            )(x_only, weights, *spread)
            early, part = lax.optimization_barrier((early, part))
        if last:
            outs = [((PAIRS * BLK + 32, BLK), bf16, VMEM)]
            more = []
        else:
            outs = [((NZ, PAIRS, BLK, BLK), bf16, HBM), ((PAIRS, BLK, BLK), f32, VMEM), ((BPD, BLK), f32, VMEM)]
            more = [VMEM((PAIRS, BLK, BLK), bf16), DMA((NZ,))]
        result = call(
            functools.partial(far_kernel, hop), "far", [whole(SMEM)] * 4 + [whole(HBM), whole(), whole()], outs,
            [VMEM((BUCKETS, BLK, BLK), f32)] + ring + more,
            limit=ROOM, flops=TPD * 2 * BLK**3, moved=8 << 20,
        )(*lists, tile_vals, got, part)
        if not last:
            packed, values, squares = result
    tails = [result] + [shift_by(result, "x", shift) for shift in SHIFTS[1:]]
    return call(
        final_kernel, "final", [whole(SMEM)] + [whole()] * (2 + NX), [((WIDTH, BPD * BLK), bf16, VMEM)]
    )(x_only, weights, early, *tails).T


def solution(mesh):
    grid = Mesh(np.array(mesh.devices).reshape(NY, NZ, NC, NX), ("y", "z", "core", "x"))
    row = ("y", "z", "core")
    in_specs = (
        P(row, "x"),
        P(row, None, None),
        P(row, None),
        P(row, None),
        P(row),
        P(row, None, None),
        P(None, row, "x"),
        P(),
    )
    return jax.shard_map(shards, mesh=grid, in_specs=in_specs, out_specs=P(row, "x"), check_vma=False)
```

```python
import functools

import jax
import jax.numpy as jnp
import numpy as np
from jax import lax
from jax.experimental import pallas as pl
from jax.experimental.pallas import tpu as pltpu
from jax.sharding import Mesh, PartitionSpec as P

BLK = 128
BPD = 8
TPD = 160
PAIRS = BPD // 2
HOPS = 2
NY, NZ, NC, NX = 4, 8, 2, 4
WIDTH = 64
GROUP = 4
STEP = 4
BUCKETS = 2 * BPD
MAXG = TPD // GROUP + BUCKETS
SLOTS = MAXG * GROUP
SHIFTS = (0, 2, 1, 3)
N_ROW = NY * NZ * NC
BATCH = 8
DEPTH = 4
FULL = 63 << 20
MOST = 65_000_000
TIGHT = 66_200_000
ROOM = 63_600_000
EPS = 1e-06
bf16 = jnp.bfloat16
f32 = jnp.float32
VMEM = pltpu.VMEM
SMEM = pltpu.SMEM
HBM = pltpu.HBM
DMA = pltpu.SemaphoreType.DMA


def lane_low(shape):
    return lax.broadcasted_iota(jnp.int32, shape, len(shape) - 1) < WIDTH


def pair_squares(pair_values):
    total = jnp.zeros((BPD, BLK), f32)
    row = lax.broadcasted_iota(jnp.int32, (BPD, BLK), 0)
    half = lax.broadcasted_iota(jnp.int32, (BPD, BLK), 1) // WIDTH
    for p in range(PAIRS):
        v = pair_values[p]
        pick = jnp.where(row == 2 * p + half, 1.0, 0.0).astype(f32)
        total = total + lax.dot_general(
            pick, v * v, (((1,), (1,)), ((), ())),
            precision=lax.Precision.HIGHEST, preferred_element_type=f32,
        )
    return total


def row_scale(total):
    return (1.0 / jnp.sqrt(total + EPS)).T


def pair_scale(columns, p):
    return jnp.where(
        lane_low((BLK, BLK)),
        jnp.broadcast_to(columns[:, 2 * p : 2 * p + 1], (BLK, BLK)),
        jnp.broadcast_to(columns[:, 2 * p + 1 : 2 * p + 2], (BLK, BLK)),
    )


def swap_halves(v):
    return pltpu.roll(v, WIDTH, 1)


def stacked_pair(ref, p):
    first = ref[:, (2 * p) * BLK : (2 * p + 1) * BLK].astype(f32)
    second = ref[:, (2 * p + 1) * BLK : (2 * p + 2) * BLK].astype(f32)
    return jnp.concatenate([first, second], axis=0)


def pack_kernel(feat_ref, out_ref, sq_ref):
    rows = []
    for p in range(PAIRS):
        stacked = stacked_pair(feat_ref, p)
        out_ref[p] = stacked.T.astype(bf16)
        squares = stacked * stacked
        rows.append(jnp.sum(squares[:WIDTH], axis=0, keepdims=True))
        rows.append(jnp.sum(squares[WIDTH:], axis=0, keepdims=True))
    sq_ref[...] = jnp.concatenate(rows, axis=0)


def send_kernel(hop, me_ref, idx_ref, raw_ref, *refs):
    sum_refs = refs[:NX]
    out_ref, own_ref, slots, buf, sem = refs[-5:]
    total = sum_refs[0][...]
    for ref in sum_refs[1:]:
        total = total + ref[...]
    columns = row_scale(total)
    if hop:
        own_ref[0:hop] = refs[NX][...]
    for p in range(PAIRS):
        v = (raw_ref[p].astype(f32) * pair_scale(columns, p)).astype(bf16)
        own_ref[hop, p] = v
        slots[p] = v
        slots[PAIRS + p] = jnp.concatenate([v[:, WIDTH:], v[:, :WIDTH]], axis=1)
    mask = lane_low((BLK, BLK))
    mine = (me_ref[0] * NZ + me_ref[1]) * NC + me_ref[2]
    copies = []
    for part in range(N_ROW // BATCH):
        for j in range(BATCH):
            i = part * BATCH + j
            first = idx_ref[i, 0]
            second = idx_ref[i, 1]
            low = slots[(first >> 1) | ((first & 1) << 2)]
            high = slots[((second >> 1) | ((second & 1) << 2)) ^ PAIRS]
            buf[i] = jnp.where(mask, low, high)

        @pl.when(mine // BATCH == part)
        def _():
            buf[mine] = jnp.zeros((BLK, BLK), bf16)

        copy = pltpu.make_async_copy(
            buf.at[pl.ds(part * BATCH, BATCH)], out_ref.at[pl.ds(part * BATCH, BATCH)], sem.at[part]
        )
        copy.start()
        copies.append(copy)
    for copy in copies:
        copy.wait()


def order_kernel(me_ref, rows_ref, srcs_ref, count_ref, tile_ref, slab_ref, into_ref, groups_ref, fill, begin):
    count = count_ref[0]
    empty = (me_ref[0] * NZ + me_ref[1]) * NC + me_ref[2]

    @pl.loop(0, SLOTS // 8)
    def _(i):
        for j in range(8):
            tile_ref[i * 8 + j] = 0
            tile_ref[SLOTS + i * 8 + j] = 0
            slab_ref[i * 8 + j] = PAIRS
            slab_ref[SLOTS + i * 8 + j] = empty

    @pl.loop(0, 2 * MAXG)
    def _(i):
        into_ref[i] = 0

    for b in range(2 * BUCKETS):
        fill[b] = 0

    def bucket_of(t):
        s = srcs_ref[t]
        return jnp.where(s < BPD, 0, BUCKETS) + rows_ref[t] * 2 + (s & 1)

    @pl.loop(0, count)
    def _(t):
        b = bucket_of(t)
        fill[b] = fill[b] + 1

    for kind in range(2):
        def place(b, group):
            size = (fill[kind * BUCKETS + b] + GROUP - 1) // GROUP
            begin[kind * BUCKETS + b] = (kind * MAXG + group) * GROUP

            @pl.loop(0, size)
            def _(i):
                into_ref[kind * MAXG + group + i] = b

            return group + size

        groups_ref[kind] = lax.fori_loop(0, BUCKETS, place, jnp.int32(0))

    @pl.loop(0, count)
    def _(t):
        b = bucket_of(t)
        at = begin[b]
        begin[b] = at + 1
        s = srcs_ref[t]
        tile_ref[at] = t
        slab_ref[at] = jnp.where(s < BPD, s >> 1, (s - BPD) >> 1)


def add_groups(kind, tile_ref, slab_ref, into_ref, groups_ref, tiles_ref, src, acc, ring, sem):
    steps = (groups_ref[kind] + STEP - 1) // STEP

    def copies(step):
        slot = step % DEPTH
        first = (kind * MAXG + STEP * step) * GROUP
        return [
            pltpu.make_async_copy(tiles_ref.at[tile_ref[first + j]], ring.at[slot, j], sem.at[slot, j])
            for j in range(STEP * GROUP)
        ]

    def begin(step):
        @pl.when(step < steps)
        def _():
            for copy in copies(step):
                copy.start()

    def run(step, carry):
        slot = step % DEPTH
        group = kind * MAXG + STEP * step
        for copy in copies(step):
            copy.wait()
        parts = []
        for h in range(STEP):
            left = jnp.concatenate([ring[slot, h * GROUP + j] for j in range(GROUP)], axis=1)
            right = jnp.concatenate([src[slab_ref[(group + h) * GROUP + j]] for j in range(GROUP)], axis=0)
            parts.append(jnp.dot(left, right, preferred_element_type=f32))
        for h in range(STEP):
            acc[into_ref[group + h]] += parts[h]
        begin(step + DEPTH)
        return carry

    return begin, lambda: lax.fori_loop(0, steps, run, 0)


def fold(acc, p):
    return jnp.where(
        lane_low((BLK, BLK)),
        acc[4 * p] + swap_halves(acc[4 * p + 1]),
        swap_halves(acc[4 * p + 2]) + acc[4 * p + 3],
    )


def own_kernel(hop, tile_ref, slab_ref, into_ref, groups_ref, tiles_ref, own_ref, noise_ref, part_ref, acc, src, noise, ring, sem, load):
    begin, run = add_groups(0, tile_ref, slab_ref, into_ref, groups_ref, tiles_ref, src, acc, ring, sem)
    for step in range(DEPTH):
        begin(step)
    noise_copy = pltpu.make_async_copy(noise_ref.at[hop], noise, load)
    noise_copy.start()
    acc[...] = jnp.zeros_like(acc)
    src[0:PAIRS] = own_ref[hop]
    src[PAIRS] = jnp.zeros((BLK, BLK), bf16)
    run()
    noise_copy.wait()
    for p in range(PAIRS):
        part_ref[p] = stacked_pair(noise, p).T + fold(acc, p)


def far_kernel(hop, tile_ref, slab_ref, into_ref, groups_ref, tiles_ref, got_ref, part_ref, *rest):
    last = hop == HOPS - 1
    if last:
        out_ref, acc, ring, sem = rest
    else:
        out_ref, sq_ref, acc, ring, sem = rest
    begin, run = add_groups(1, tile_ref, slab_ref, into_ref, groups_ref, tiles_ref, got_ref, acc, ring, sem)
    for step in range(DEPTH):
        begin(step)
    acc[...] = jnp.zeros_like(acc)
    run()
    pairs = []
    for p in range(PAIRS):
        u = part_ref[p] + fold(acc, p)
        pairs.append(u)
        if last:
            out_ref[p * BLK : (p + 1) * BLK] = u.astype(bf16)
        else:
            out_ref[p] = u
    total = pair_squares(pairs)
    if last:
        hi = total.astype(bf16).astype(f32)
        mid = (total - hi).astype(bf16).astype(f32)
        lo = total - hi - mid
        out_ref[PAIRS * BLK : PAIRS * BLK + 16] = jnp.concatenate([hi, mid], axis=0).astype(bf16)
        out_ref[PAIRS * BLK + 16 : PAIRS * BLK + 32] = jnp.concatenate([lo, jnp.zeros_like(lo)], axis=0).astype(bf16)
    else:
        sq_ref[...] = total


def early_kernel(x_ref, w_ref, *refs):
    h_refs, out_ref = refs[:-1], refs[-1]
    for p in range(PAIRS):
        total = jnp.zeros((BLK, BLK), f32)
        for k in range(HOPS):
            for j, shift in enumerate(SHIFTS):
                source = (x_ref[0] + NX - shift) % NX
                total = total + jnp.dot(h_refs[j][k, p], w_ref[k, source], preferred_element_type=f32)
        out_ref[p] = total


def final_kernel(x_ref, w_ref, early_ref, *refs):
    got_refs, out_ref = refs[:-1], refs[-1]
    total = jnp.zeros((BPD, BLK), f32)
    for got_ref in got_refs:
        a = got_ref[PAIRS * BLK : PAIRS * BLK + 16].astype(f32)
        b = got_ref[PAIRS * BLK + 16 : PAIRS * BLK + 32].astype(f32)
        total = total + (a[:BPD] + a[BPD:] + b[:BPD])
    columns = row_scale(total)
    for p in range(PAIRS):
        raw = jnp.zeros((BLK, BLK), f32)
        for j, shift in enumerate(SHIFTS):
            source = (x_ref[0] + NX - shift) % NX
            raw = raw + jnp.dot(got_refs[j][p * BLK : (p + 1) * BLK], w_ref[HOPS, source], preferred_element_type=f32)
        v = (early_ref[p] + raw * pair_scale(columns, p)).T
        out_ref[:, (2 * p) * BLK : (2 * p + 1) * BLK] = v[:WIDTH].astype(bf16)
        out_ref[:, (2 * p + 1) * BLK : (2 * p + 2) * BLK] = v[WIDTH:].astype(bf16)


def whole(space=VMEM):
    return pl.BlockSpec(memory_space=space)


def call(kernel, name, in_specs, outs, scratch=(), limit=24 << 20, flops=1 << 20, moved=1 << 20):
    shapes = [jax.ShapeDtypeStruct(dims, kind) for dims, kind, _ in outs]
    specs = [whole(space) for _, _, space in outs]
    single = len(outs) == 1
    return pl.pallas_call(
        kernel,
        name=name,
        out_shape=shapes[0] if single else shapes,
        in_specs=in_specs,
        out_specs=specs[0] if single else specs,
        scratch_shapes=list(scratch),
        compiler_params=pltpu.CompilerParams(vmem_limit_bytes=limit),
        cost_estimate=pl.CostEstimate(flops=flops, bytes_accessed=moved, transcendentals=0),
    )


def shift_by(value, axis, shift):
    size = lax.axis_size(axis)
    return lax.ppermute(value, axis, [(i, (i + shift) % size) for i in range(size)])


def shards(features, tile_vals, tile_rows, tile_srcs, tile_count, needed, hop_noise, enc_weight):
    me = jnp.stack([lax.axis_index("y"), lax.axis_index("z"), lax.axis_index("core")]).astype(jnp.int32)
    x_index = lax.axis_index("x").astype(jnp.int32)
    x_only = x_index.reshape(1)
    noise = hop_noise.transpose(0, 2, 1)

    packed, squares = call(
        pack_kernel, "pack", [whole()],
        [((PAIRS, BLK, BLK), bf16, VMEM), ((BPD, BLK), f32, VMEM)],
    )(features.T)
    asked = lax.all_to_all(jnp.pad(needed[0], ((0, 0), (0, BLK - 2))), ("y", "z", "core"), 0, 0, tiled=True)
    packed, squares, rows, srcs, count, enc_weight = lax.optimization_barrier(
        (packed, squares, tile_rows.reshape(-1), tile_srcs.reshape(-1), tile_count, enc_weight)
    )

    weights = lax.dynamic_slice_in_dim(enc_weight, x_index * WIDTH, WIDTH, axis=2).reshape(HOPS + 1, NX, WIDTH, WIDTH)
    nothing = jnp.zeros_like(weights)
    weights = jnp.concatenate(
        [jnp.concatenate([weights, nothing], axis=-1), jnp.concatenate([nothing, weights], axis=-1)], axis=-2
    )
    lists = call(
        order_kernel, "order", [whole(SMEM)] * 4,
        [((2 * SLOTS,), jnp.int32, SMEM), ((2 * SLOTS,), jnp.int32, SMEM), ((2 * MAXG,), jnp.int32, SMEM), ((2,), jnp.int32, SMEM)],
        [SMEM((2 * BUCKETS,), jnp.int32), SMEM((2 * BUCKETS,), jnp.int32)],
    )(me, rows, srcs, count)
    owned = None
    for hop in range(HOPS):
        last = hop == HOPS - 1
        totals = [squares] + [shift_by(squares, "x", shift) for shift in SHIFTS[1:]]
        before = [owned] if hop else []
        picked, owned = call(
            functools.partial(send_kernel, hop), "send", [whole(SMEM)] * 2 + [whole()] * (1 + NX + hop),
            [((N_ROW, BLK, BLK), bf16, HBM), ((hop + 1, PAIRS, BLK, BLK), bf16, VMEM)],
            [VMEM((BPD, BLK, BLK), bf16), VMEM((N_ROW, BLK, BLK), bf16), DMA((N_ROW // BATCH,))],
            limit=MOST,
        )(me, asked, packed, *totals, *before)
        if last:
            spread = [owned] + [shift_by(owned, "x", shift) for shift in SHIFTS[1:]]
        got = lax.all_to_all(picked, ("y", "z", "core"), 0, 0, tiled=True)
        ring = [VMEM((DEPTH, STEP * GROUP, BLK, BLK), bf16), DMA((DEPTH, STEP * GROUP))]
        part = call(
            functools.partial(own_kernel, hop), "own", [whole(SMEM)] * 4 + [whole(HBM), whole(), whole(HBM)],
            [((PAIRS, BLK, BLK), f32, VMEM)],
            [VMEM((BUCKETS, BLK, BLK), f32), VMEM((PAIRS + 1, BLK, BLK), bf16), VMEM((WIDTH, BPD * BLK), f32)] + ring + [DMA(())],
            limit=FULL, flops=TPD * 2 * BLK**3, moved=4 << 20,
        )(*lists, tile_vals, owned, noise)
        if last:
            early = call(
                early_kernel, "early", [whole(SMEM)] + [whole()] * (1 + NX), [((PAIRS, BLK, BLK), f32, VMEM)]
            )(x_only, weights, *spread)
            early, part = lax.optimization_barrier((early, part))
        if last:
            outs = [((PAIRS * BLK + 32, BLK), bf16, VMEM)]
            more = []
        else:
            outs = [((PAIRS, BLK, BLK), f32, VMEM), ((BPD, BLK), f32, VMEM)]
            more = []
        result = call(
            functools.partial(far_kernel, hop), "far", [whole(SMEM)] * 4 + [whole(HBM), whole(), whole()], outs,
            [VMEM((BUCKETS, BLK, BLK), f32)] + ring + more,
            limit=ROOM, flops=TPD * 2 * BLK**3, moved=8 << 20,
        )(*lists, tile_vals, got, part)
        if not last:
            packed, squares = result
    tails = [result] + [shift_by(result, "x", shift) for shift in SHIFTS[1:]]
    return call(
        final_kernel, "final", [whole(SMEM)] + [whole()] * (2 + NX), [((WIDTH, BPD * BLK), bf16, VMEM)],
    )(x_only, weights, early, *tails).T


def solution(mesh):
    grid = Mesh(np.array(mesh.devices).reshape(NY, NZ, NC, NX), ("y", "z", "core", "x"))
    row = ("y", "z", "core")
    in_specs = (
        P(row, "x"),
        P(row, None, None),
        P(row, None),
        P(row, None),
        P(row),
        P(row, None, None),
        P(None, row, "x"),
        P(),
    )
    return jax.shard_map(shards, mesh=grid, in_specs=in_specs, out_specs=P(row, "x"), check_vma=False)
```

```python
import functools

import jax
import jax.numpy as jnp
import numpy as np
from jax import lax
from jax.experimental import pallas as pl
from jax.experimental.pallas import tpu as pltpu
from jax.sharding import Mesh, PartitionSpec as P

BLK = 128
BPD = 8
TPD = 160
PAIRS = BPD // 2
HOPS = 2
NY, NZ, NC, NX = 4, 8, 2, 4
WIDTH = 64
GROUP = 4
STEP = 4
BUCKETS = 2 * BPD
MAXG = TPD // GROUP + BUCKETS
SLOTS = MAXG * GROUP
SHIFTS = (0, 2, 1, 3)
N_ROW = NY * NZ * NC
N_YC = NY * NC
SIDE = 48
ZSHIFTS = (0, 4, 3, 5, 2, 6, 1, 7)
YSHIFTS = (0, 4, 3, 5, 2, 6, 1, 7)
BATCH = 8
DEPTH = 4
FULL = 63 << 20
MOST = 65_000_000
TIGHT = 66_200_000
ROOM = 63_600_000
EPS = 1e-06
bf16 = jnp.bfloat16
f32 = jnp.float32
VMEM = pltpu.VMEM
SMEM = pltpu.SMEM
HBM = pltpu.HBM
DMA = pltpu.SemaphoreType.DMA


def lane_low(shape):
    return lax.broadcasted_iota(jnp.int32, shape, len(shape) - 1) < WIDTH


def pair_squares(pair_values):
    total = jnp.zeros((BPD, BLK), f32)
    row = lax.broadcasted_iota(jnp.int32, (BPD, BLK), 0)
    half = lax.broadcasted_iota(jnp.int32, (BPD, BLK), 1) // WIDTH
    for p in range(PAIRS):
        v = pair_values[p]
        pick = jnp.where(row == 2 * p + half, 1.0, 0.0).astype(f32)
        total = total + lax.dot_general(
            pick, v * v, (((1,), (1,)), ((), ())),
            precision=lax.Precision.HIGHEST, preferred_element_type=f32,
        )
    return total


def row_scale(total):
    return (1.0 / jnp.sqrt(total + EPS)).T


def pair_scale(columns, p):
    return jnp.where(
        lane_low((BLK, BLK)),
        jnp.broadcast_to(columns[:, 2 * p : 2 * p + 1], (BLK, BLK)),
        jnp.broadcast_to(columns[:, 2 * p + 1 : 2 * p + 2], (BLK, BLK)),
    )


def swap_halves(v):
    return pltpu.roll(v, WIDTH, 1)


def stacked_pair(ref, p):
    first = ref[:, (2 * p) * BLK : (2 * p + 1) * BLK].astype(f32)
    second = ref[:, (2 * p + 1) * BLK : (2 * p + 2) * BLK].astype(f32)
    return jnp.concatenate([first, second], axis=0)


def pack_kernel(feat_ref, out_ref, sq_ref):
    rows = []
    for p in range(PAIRS):
        stacked = stacked_pair(feat_ref, p)
        out_ref[p] = stacked.T.astype(bf16)
        squares = stacked * stacked
        rows.append(jnp.sum(squares[:WIDTH], axis=0, keepdims=True))
        rows.append(jnp.sum(squares[WIDTH:], axis=0, keepdims=True))
    sq_ref[...] = jnp.concatenate(rows, axis=0)


def send_kernel(hop, me_ref, idx_ref, raw_ref, *refs):
    sum_refs = refs[:NX]
    out_ref, own_ref, slots, buf, sem = refs[-5:]
    rows = buf.shape[1]
    total = sum_refs[0][...]
    for ref in sum_refs[1:]:
        total = total + ref[...]
    columns = row_scale(total)
    if hop:
        own_ref[0:hop] = refs[NX][...]
        side_ref = refs[NX + 1]
    for p in range(PAIRS):
        v = (raw_ref[p].astype(f32) * pair_scale(columns, p)).astype(bf16)
        own_ref[hop, p] = v
        if hop:
            side_ref[p] = v[rows:]
        v = v[:rows]
        slots[p] = v
        slots[PAIRS + p] = jnp.concatenate([v[:, WIDTH:], v[:, :WIDTH]], axis=1)
    mask = lane_low((rows, BLK))
    mine = (me_ref[0] * NZ + me_ref[1]) * NC + me_ref[2]
    copies = []
    for part in range(N_ROW // BATCH):
        for j in range(BATCH):
            i = part * BATCH + j
            first = idx_ref[i, 0]
            second = idx_ref[i, 1]
            low = slots[(first >> 1) | ((first & 1) << 2)]
            high = slots[((second >> 1) | ((second & 1) << 2)) ^ PAIRS]
            buf[i] = jnp.where(mask, low, high)

        @pl.when(mine // BATCH == part)
        def _():
            buf[mine] = jnp.zeros((rows, BLK), bf16)

        copy = pltpu.make_async_copy(
            buf.at[pl.ds(part * BATCH, BATCH)], out_ref.at[pl.ds(part * BATCH, BATCH)], sem.at[part]
        )
        copy.start()
        copies.append(copy)
    for copy in copies:
        copy.wait()


def pick_kernel(me_ref, table_ref, *refs):
    z_refs, out_refs, slots = refs[:NZ], refs[NZ : NZ + N_YC], refs[-1]
    for j in range(NZ):
        z = (me_ref[1] + NZ - ZSHIFTS[j]) % NZ
        for p in range(PAIRS):
            v = z_refs[j][p]
            slots[z * BPD + p] = v
            slots[z * BPD + PAIRS + p] = jnp.concatenate([v[:, WIDTH:], v[:, :WIDTH]], axis=1)
    mask = lane_low((SIDE, BLK))
    mine = me_ref[0] * NC + me_ref[2]
    for j in range(N_YC):
        dest = (mine + YSHIFTS[j]) % N_YC
        for z in range(NZ):
            at = (dest * NZ + z) * 2
            out_refs[j][z] = jnp.where(mask, slots[table_ref[at]], slots[table_ref[at + 1]])
    out_refs[0][me_ref[1]] = jnp.zeros((SIDE, BLK), bf16)


def order_kernel(me_ref, rows_ref, srcs_ref, count_ref, tile_ref, slab_ref, into_ref, groups_ref, fill, begin):
    count = count_ref[0]
    empty = (me_ref[0] * NZ + me_ref[1]) * NC + me_ref[2]

    @pl.loop(0, SLOTS // 8)
    def _(i):
        for j in range(8):
            tile_ref[i * 8 + j] = 0
            tile_ref[SLOTS + i * 8 + j] = 0
            slab_ref[i * 8 + j] = PAIRS
            slab_ref[SLOTS + i * 8 + j] = empty

    @pl.loop(0, 2 * MAXG)
    def _(i):
        into_ref[i] = 0

    for b in range(2 * BUCKETS):
        fill[b] = 0

    def bucket_of(t):
        s = srcs_ref[t]
        return jnp.where(s < BPD, 0, BUCKETS) + rows_ref[t] * 2 + (s & 1)

    @pl.loop(0, count)
    def _(t):
        b = bucket_of(t)
        fill[b] = fill[b] + 1

    for kind in range(2):
        def place(b, group):
            size = (fill[kind * BUCKETS + b] + GROUP - 1) // GROUP
            begin[kind * BUCKETS + b] = (kind * MAXG + group) * GROUP

            @pl.loop(0, size)
            def _(i):
                into_ref[kind * MAXG + group + i] = b

            return group + size

        groups_ref[kind] = lax.fori_loop(0, BUCKETS, place, jnp.int32(0))

    @pl.loop(0, count)
    def _(t):
        b = bucket_of(t)
        at = begin[b]
        begin[b] = at + 1
        s = srcs_ref[t]
        tile_ref[at] = t
        slab_ref[at] = jnp.where(s < BPD, s >> 1, (s - BPD) >> 1)


def add_groups(kind, tile_ref, slab_ref, into_ref, groups_ref, tiles_ref, source, acc, ring, sem):
    steps = (groups_ref[kind] + STEP - 1) // STEP

    def copies(step):
        slot = step % DEPTH
        first = (kind * MAXG + STEP * step) * GROUP
        return [
            pltpu.make_async_copy(tiles_ref.at[tile_ref[first + j]], ring.at[slot, j], sem.at[slot, j])
            for j in range(STEP * GROUP)
        ]

    def begin(step):
        @pl.when(step < steps)
        def _():
            for copy in copies(step):
                copy.start()

    def run(step, carry):
        slot = step % DEPTH
        group = kind * MAXG + STEP * step
        for copy in copies(step):
            copy.wait()
        parts = []
        for h in range(STEP):
            left = jnp.concatenate([ring[slot, h * GROUP + j] for j in range(GROUP)], axis=1)
            right = jnp.concatenate(
                [piece for j in range(GROUP) for piece in source(slab_ref[(group + h) * GROUP + j])], axis=0
            )
            parts.append(jnp.dot(left, right, preferred_element_type=f32))
        for h in range(STEP):
            acc[into_ref[group + h]] += parts[h]
        begin(step + DEPTH)
        return carry

    return begin, lambda: lax.fori_loop(0, steps, run, 0)


def fold(acc, p):
    return jnp.where(
        lane_low((BLK, BLK)),
        acc[4 * p] + swap_halves(acc[4 * p + 1]),
        swap_halves(acc[4 * p + 2]) + acc[4 * p + 3],
    )


def own_kernel(hop, tile_ref, slab_ref, into_ref, groups_ref, tiles_ref, own_ref, noise_ref, part_ref, acc, src, noise, ring, sem, load):
    begin, run = add_groups(0, tile_ref, slab_ref, into_ref, groups_ref, tiles_ref, lambda i: [src[i]], acc, ring, sem)
    for step in range(DEPTH):
        begin(step)
    noise_copy = pltpu.make_async_copy(noise_ref.at[hop], noise, load)
    noise_copy.start()
    acc[...] = jnp.zeros_like(acc)
    src[0:PAIRS] = own_ref[hop]
    src[PAIRS] = jnp.zeros((BLK, BLK), bf16)
    run()
    noise_copy.wait()
    for p in range(PAIRS):
        part_ref[p] = stacked_pair(noise, p).T + fold(acc, p)


def far_kernel(hop, me_ref, tile_ref, slab_ref, into_ref, groups_ref, tiles_ref, got_ref, part_ref, *rest):
    last = hop == HOPS - 1
    if last:
        side_refs = rest[:N_YC]
        out_ref, acc, ring, sem, side, load = rest[N_YC:]
        mine = me_ref[0] * NC + me_ref[2]
        loads = []
        for j in range(N_YC):
            at = (mine + N_YC - YSHIFTS[j]) % N_YC
            loads.append(pltpu.make_async_copy(side_refs[j], side.at[pl.ds(at * NZ, NZ)], load.at[j]))
            loads[-1].start()

        def source(i):
            return [got_ref[i], side[((i >> 4) * NC + (i & 1)) * NZ + ((i >> 1) & (NZ - 1))]]
    else:
        out_ref, sq_ref, acc, ring, sem = rest
        loads = []

        def source(i):
            return [got_ref[i]]

    begin, run = add_groups(1, tile_ref, slab_ref, into_ref, groups_ref, tiles_ref, source, acc, ring, sem)
    for step in range(DEPTH):
        begin(step)
    for copy in loads:
        copy.wait()
    acc[...] = jnp.zeros_like(acc)
    run()
    pairs = []
    for p in range(PAIRS):
        u = part_ref[p] + fold(acc, p)
        pairs.append(u)
        if last:
            out_ref[p * BLK : (p + 1) * BLK] = u.astype(bf16)
        else:
            out_ref[p] = u
    total = pair_squares(pairs)
    if last:
        hi = total.astype(bf16).astype(f32)
        mid = (total - hi).astype(bf16).astype(f32)
        lo = total - hi - mid
        out_ref[PAIRS * BLK : PAIRS * BLK + 16] = jnp.concatenate([hi, mid], axis=0).astype(bf16)
        out_ref[PAIRS * BLK + 16 : PAIRS * BLK + 32] = jnp.concatenate([lo, jnp.zeros_like(lo)], axis=0).astype(bf16)
    else:
        sq_ref[...] = total


def early_kernel(x_ref, w_ref, *refs):
    h_refs, out_ref = refs[:-1], refs[-1]
    for p in range(PAIRS):
        total = jnp.zeros((BLK, BLK), f32)
        for k in range(HOPS):
            for j, shift in enumerate(SHIFTS):
                source = (x_ref[0] + NX - shift) % NX
                total = total + jnp.dot(h_refs[j][k, p], w_ref[k, source], preferred_element_type=f32)
        out_ref[p] = total


def final_kernel(x_ref, w_ref, early_ref, *refs):
    got_refs, out_ref = refs[:-1], refs[-1]
    total = jnp.zeros((BPD, BLK), f32)
    for got_ref in got_refs:
        a = got_ref[PAIRS * BLK : PAIRS * BLK + 16].astype(f32)
        b = got_ref[PAIRS * BLK + 16 : PAIRS * BLK + 32].astype(f32)
        total = total + (a[:BPD] + a[BPD:] + b[:BPD])
    columns = row_scale(total)
    for p in range(PAIRS):
        raw = jnp.zeros((BLK, BLK), f32)
        for j, shift in enumerate(SHIFTS):
            source = (x_ref[0] + NX - shift) % NX
            raw = raw + jnp.dot(got_refs[j][p * BLK : (p + 1) * BLK], w_ref[HOPS, source], preferred_element_type=f32)
        v = (early_ref[p] + raw * pair_scale(columns, p)).T
        out_ref[:, (2 * p) * BLK : (2 * p + 1) * BLK] = v[:WIDTH].astype(bf16)
        out_ref[:, (2 * p + 1) * BLK : (2 * p + 2) * BLK] = v[WIDTH:].astype(bf16)


def whole(space=VMEM):
    return pl.BlockSpec(memory_space=space)


def call(kernel, name, in_specs, outs, scratch=(), limit=24 << 20, flops=1 << 20, moved=1 << 20):
    shapes = [jax.ShapeDtypeStruct(dims, kind) for dims, kind, _ in outs]
    specs = [whole(space) for _, _, space in outs]
    single = len(outs) == 1
    return pl.pallas_call(
        kernel,
        name=name,
        out_shape=shapes[0] if single else shapes,
        in_specs=in_specs,
        out_specs=specs[0] if single else specs,
        scratch_shapes=list(scratch),
        compiler_params=pltpu.CompilerParams(vmem_limit_bytes=limit),
        cost_estimate=pl.CostEstimate(flops=flops, bytes_accessed=moved, transcendentals=0),
    )


def shift_by(value, axis, shift):
    size = N_YC if axis == ("y", "core") else lax.axis_size(axis)
    return lax.ppermute(value, axis, [(i, (i + shift) % size) for i in range(size)])


def shards(features, tile_vals, tile_rows, tile_srcs, tile_count, needed, hop_noise, enc_weight):
    me = jnp.stack([lax.axis_index("y"), lax.axis_index("z"), lax.axis_index("core")]).astype(jnp.int32)
    x_index = lax.axis_index("x").astype(jnp.int32)
    x_only = x_index.reshape(1)
    noise = hop_noise.transpose(0, 2, 1)

    packed, squares = call(
        pack_kernel, "pack", [whole()],
        [((PAIRS, BLK, BLK), bf16, VMEM), ((BPD, BLK), f32, VMEM)],
    )(features.T)
    asked = lax.all_to_all(jnp.pad(needed[0], ((0, 0), (0, BLK - 2))), ("y", "z", "core"), 0, 0, tiled=True)
    packed, squares, rows, srcs, count, enc_weight = lax.optimization_barrier(
        (packed, squares, tile_rows.reshape(-1), tile_srcs.reshape(-1), tile_count, enc_weight)
    )

    weights = lax.dynamic_slice_in_dim(enc_weight, x_index * WIDTH, WIDTH, axis=2).reshape(HOPS + 1, NX, WIDTH, WIDTH)
    nothing = jnp.zeros_like(weights)
    weights = jnp.concatenate(
        [jnp.concatenate([weights, nothing], axis=-1), jnp.concatenate([nothing, weights], axis=-1)], axis=-2
    )
    lists = call(
        order_kernel, "order", [whole(SMEM)] * 4,
        [((2 * SLOTS,), jnp.int32, SMEM), ((2 * SLOTS,), jnp.int32, SMEM), ((2 * MAXG,), jnp.int32, SMEM), ((2,), jnp.int32, SMEM)],
        [SMEM((2 * BUCKETS,), jnp.int32), SMEM((2 * BUCKETS,), jnp.int32)],
    )(me, rows, srcs, count)
    owned = None
    for hop in range(HOPS):
        last = hop == HOPS - 1
        totals = [squares] + [shift_by(squares, "x", shift) for shift in SHIFTS[1:]]
        before = [owned] if hop else []
        rows_sent = BLK - SIDE if last else BLK
        outs = [((N_ROW, rows_sent, BLK), bf16, HBM), ((hop + 1, PAIRS, BLK, BLK), bf16, VMEM)]
        if last:
            outs = [((PAIRS, SIDE, BLK), bf16, VMEM)] + outs
        *sides, picked, owned = call(
            functools.partial(send_kernel, hop), "send", [whole(SMEM)] * 2 + [whole()] * (1 + NX + hop), outs,
            [VMEM((BPD, rows_sent, BLK), bf16), VMEM((N_ROW, rows_sent, BLK), bf16), DMA((N_ROW // BATCH,))],
            limit=MOST,
        )(me, asked, packed, *totals, *before)
        got = lax.all_to_all(picked, ("y", "z", "core"), 0, 0, tiled=True)
        if last:
            along = sides + [shift_by(sides[0], "z", shift) for shift in ZSHIFTS[1:]]
            sides = call(
                pick_kernel, "pick", [whole(SMEM)] * 2 + [whole()] * NZ,
                [((NZ, SIDE, BLK), bf16, VMEM)] * N_YC,
                [VMEM((NZ * BPD, SIDE, BLK), bf16)],
            )(me, table, *along)
            sides = [sides[0]] + [shift_by(side, ("y", "core"), shift) for side, shift in zip(sides[1:], YSHIFTS[1:])]
            owned, first = lax.optimization_barrier((owned, sides[0]))
            sides = [first] + sides[1:]
            spread = [owned] + [shift_by(owned, "x", shift) for shift in SHIFTS[1:]]
        else:
            wide, owned = lax.optimization_barrier((needed.reshape(-1), owned))
            table = lax.all_gather(wide, ("y", "core"), axis=0).reshape(N_YC, NY, NZ, NC, 2)
            table = lax.dynamic_slice(table, (0, me[0], 0, me[2], 0), (N_YC, 1, NZ, 1, 2)).reshape(N_YC, NZ, 2)
            odd = (table % 2) ^ jnp.arange(2, dtype=jnp.int32)
            table = (jnp.arange(NZ, dtype=jnp.int32)[:, None] * BPD + table // 2 + PAIRS * odd).reshape(-1)
        ring = [VMEM((DEPTH, STEP * GROUP, BLK, BLK), bf16), DMA((DEPTH, STEP * GROUP))]
        part = call(
            functools.partial(own_kernel, hop), "own", [whole(SMEM)] * 4 + [whole(HBM), whole(), whole(HBM)],
            [((PAIRS, BLK, BLK), f32, VMEM)],
            [VMEM((BUCKETS, BLK, BLK), f32), VMEM((PAIRS + 1, BLK, BLK), bf16), VMEM((WIDTH, BPD * BLK), f32)] + ring + [DMA(())],
            limit=FULL, flops=TPD * 2 * BLK**3, moved=4 << 20,
        )(*lists, tile_vals, owned, noise)
        if not last:
            part, table = lax.optimization_barrier((part, table))
        if last:
            early = call(
                early_kernel, "early", [whole(SMEM)] + [whole()] * (1 + NX), [((PAIRS, BLK, BLK), f32, VMEM)]
            )(x_only, weights, *spread)
            early, part = lax.optimization_barrier((early, part))
        if last:
            outs = [((PAIRS * BLK + 32, BLK), bf16, VMEM)]
            more = [VMEM((N_YC * NZ, SIDE, BLK), bf16), DMA((N_YC,))]
        else:
            outs = [((PAIRS, BLK, BLK), f32, VMEM), ((BPD, BLK), f32, VMEM)]
            more = []
        result = call(
            functools.partial(far_kernel, hop), "far", [whole(SMEM)] * 5 + [whole(HBM), whole(), whole()] + [whole(HBM)] * len(sides), outs,
            [VMEM((BUCKETS, BLK, BLK), f32)] + ring + more,
            limit=ROOM, flops=TPD * 2 * BLK**3, moved=8 << 20,
        )(me, *lists, tile_vals, got, part, *sides)
        if not last:
            packed, squares = result
    tails = [result] + [shift_by(result, "x", shift) for shift in SHIFTS[1:]]
    return call(
        final_kernel, "final", [whole(SMEM)] + [whole()] * (2 + NX), [((WIDTH, BPD * BLK), bf16, VMEM)],
    )(x_only, weights, early, *tails).T


def solution(mesh):
    grid = Mesh(np.array(mesh.devices).reshape(NY, NZ, NC, NX), ("y", "z", "core", "x"))
    row = ("y", "z", "core")
    in_specs = (
        P(row, "x"),
        P(row, None, None),
        P(row, None),
        P(row, None),
        P(row),
        P(row, None, None),
        P(None, row, "x"),
        P(),
    )
    return jax.shard_map(shards, mesh=grid, in_specs=in_specs, out_specs=P(row, "x"), check_vma=False)
```

```python
import functools

import jax
import jax.numpy as jnp
import numpy as np
from jax import lax
from jax.experimental import pallas as pl
from jax.experimental.pallas import tpu as pltpu
from jax.sharding import Mesh, PartitionSpec as P

BLK = 128
BPD = 8
TPD = 160
PAIRS = BPD // 2
HOPS = 2
NY, NZ, NC, NX = 4, 8, 2, 4
WIDTH = 64
GROUP = 4
STEP = 4
BUCKETS = 2 * BPD
MAXG = TPD // GROUP + BUCKETS
SLOTS = MAXG * GROUP
SHIFTS = (0, 2, 1, 3)
N_ROW = NY * NZ * NC
BATCH = 8
DEPTH = 4
FULL = 63 << 20
MOST = 65_000_000
TIGHT = 66_200_000
ROOM = 63_600_000
EPS = 1e-06
bf16 = jnp.bfloat16
f32 = jnp.float32
VMEM = pltpu.VMEM
SMEM = pltpu.SMEM
HBM = pltpu.HBM
DMA = pltpu.SemaphoreType.DMA


def lane_low(shape):
    return lax.broadcasted_iota(jnp.int32, shape, len(shape) - 1) < WIDTH


def pair_squares(pair_values):
    total = jnp.zeros((BPD, BLK), f32)
    row = lax.broadcasted_iota(jnp.int32, (BPD, BLK), 0)
    half = lax.broadcasted_iota(jnp.int32, (BPD, BLK), 1) // WIDTH
    for p in range(PAIRS):
        v = pair_values[p]
        pick = jnp.where(row == 2 * p + half, 1.0, 0.0).astype(f32)
        total = total + lax.dot_general(
            pick, v * v, (((1,), (1,)), ((), ())),
            precision=lax.Precision.HIGHEST, preferred_element_type=f32,
        )
    return total


def row_scale(total):
    return (1.0 / jnp.sqrt(total + EPS)).T


def pair_scale(columns, p):
    return jnp.where(
        lane_low((BLK, BLK)),
        jnp.broadcast_to(columns[:, 2 * p : 2 * p + 1], (BLK, BLK)),
        jnp.broadcast_to(columns[:, 2 * p + 1 : 2 * p + 2], (BLK, BLK)),
    )


def swap_halves(v):
    return pltpu.roll(v, WIDTH, 1)


def stacked_pair(ref, p):
    first = ref[:, (2 * p) * BLK : (2 * p + 1) * BLK].astype(f32)
    second = ref[:, (2 * p + 1) * BLK : (2 * p + 2) * BLK].astype(f32)
    return jnp.concatenate([first, second], axis=0)


def pack_kernel(feat_ref, out_ref, sq_ref):
    rows = []
    for p in range(PAIRS):
        stacked = stacked_pair(feat_ref, p)
        out_ref[p] = stacked.T.astype(bf16)
        squares = stacked * stacked
        rows.append(jnp.sum(squares[:WIDTH], axis=0, keepdims=True))
        rows.append(jnp.sum(squares[WIDTH:], axis=0, keepdims=True))
    sq_ref[...] = jnp.concatenate(rows, axis=0)


def total_of(refs):
    total = refs[0][...]
    for ref in refs[1:]:
        total = total + ref[...]
    return total


def swapped(v):
    return jnp.concatenate([v[:, WIDTH:], v[:, :WIDTH]], axis=1)


def norm_kernel(raw_ref, *refs):
    out_ref, own_ref, buf, sem = refs[NX:]
    columns = row_scale(total_of(refs[:NX]))
    copies = []
    for p in range(PAIRS):
        v = (raw_ref[p].astype(f32) * pair_scale(columns, p)).astype(bf16)
        buf[p] = v
        own_ref[0, p] = v
    for z in range(NZ):
        copy = pltpu.make_async_copy(buf, out_ref.at[z], sem.at[z])
        copy.start()
        copies.append(copy)
    for copy in copies:
        copy.wait()


def write_slabs(me_ref, idx_ref, slots, out_ref, buf, sem):
    mask = lane_low((BLK, BLK))
    mine = (me_ref[0] * NC + me_ref[2]) * NZ + me_ref[1]
    copies = []
    for part in range(N_ROW // BATCH):
        for j in range(BATCH):
            i = part * BATCH + j
            buf[i] = jnp.where(mask, slots[idx_ref[2 * i]], slots[idx_ref[2 * i + 1]])

        @pl.when(mine // BATCH == part)
        def _():
            buf[mine] = jnp.zeros((BLK, BLK), bf16)

        copy = pltpu.make_async_copy(
            buf.at[pl.ds(part * BATCH, BATCH)], out_ref.at[pl.ds(part * BATCH, BATCH)], sem.at[part]
        )
        copy.start()
        copies.append(copy)
    for copy in copies:
        copy.wait()


def pick_kernel(me_ref, idx_ref, z_ref, out_ref, slots, buf, sem):
    for z in range(NZ):
        for p in range(PAIRS):
            v = z_ref[z, p]
            slots[z * BPD + p] = v
            slots[z * BPD + PAIRS + p] = swapped(v)
    write_slabs(me_ref, idx_ref, slots, out_ref, buf, sem)


def send_kernel(me_ref, idx_ref, raw_ref, *refs):
    before_ref, out_ref, own_ref, slots, buf, sem = refs[NX:]
    columns = row_scale(total_of(refs[:NX]))
    own_ref[0] = before_ref[0]
    for p in range(PAIRS):
        v = (raw_ref[p] * pair_scale(columns, p)).astype(bf16)
        own_ref[1, p] = v
        slots[p] = v
        slots[PAIRS + p] = swapped(v)
    write_slabs(me_ref, idx_ref, slots, out_ref, buf, sem)


def order_kernel(me_ref, rows_ref, srcs_ref, count_ref, tile_ref, slab_ref, into_ref, groups_ref, fill, begin):
    count = count_ref[0]
    empty = (me_ref[0] * NC + me_ref[2]) * NZ + me_ref[1]

    @pl.loop(0, SLOTS // 8)
    def _(i):
        for j in range(8):
            tile_ref[i * 8 + j] = 0
            tile_ref[SLOTS + i * 8 + j] = 0
            slab_ref[i * 8 + j] = PAIRS
            slab_ref[SLOTS + i * 8 + j] = empty

    @pl.loop(0, 2 * MAXG)
    def _(i):
        into_ref[i] = 0

    for b in range(2 * BUCKETS):
        fill[b] = 0

    def bucket_of(t):
        s = srcs_ref[t]
        return jnp.where(s < BPD, 0, BUCKETS) + rows_ref[t] * 2 + (s & 1)

    @pl.loop(0, count)
    def _(t):
        b = bucket_of(t)
        fill[b] = fill[b] + 1

    for kind in range(2):
        def place(b, group):
            size = (fill[kind * BUCKETS + b] + GROUP - 1) // GROUP
            begin[kind * BUCKETS + b] = (kind * MAXG + group) * GROUP

            @pl.loop(0, size)
            def _(i):
                into_ref[kind * MAXG + group + i] = b

            return group + size

        groups_ref[kind] = lax.fori_loop(0, BUCKETS, place, jnp.int32(0))

    @pl.loop(0, count)
    def _(t):
        b = bucket_of(t)
        at = begin[b]
        begin[b] = at + 1
        s = srcs_ref[t]
        tile_ref[at] = t
        o = (s - BPD) >> 1
        far_slab = (((o >> 4) * NC) + (o & 1)) * NZ + ((o >> 1) & (NZ - 1))
        slab_ref[at] = jnp.where(s < BPD, s >> 1, far_slab)


def add_groups(kind, tile_ref, slab_ref, into_ref, groups_ref, tiles_ref, src, acc, ring, sem):
    steps = (groups_ref[kind] + STEP - 1) // STEP

    def copies(step):
        slot = step % DEPTH
        first = (kind * MAXG + STEP * step) * GROUP
        return [
            pltpu.make_async_copy(tiles_ref.at[tile_ref[first + j]], ring.at[slot, j], sem.at[slot, j])
            for j in range(STEP * GROUP)
        ]

    def begin(step):
        @pl.when(step < steps)
        def _():
            for copy in copies(step):
                copy.start()

    def run(step, carry):
        slot = step % DEPTH
        group = kind * MAXG + STEP * step
        for copy in copies(step):
            copy.wait()
        parts = []
        for h in range(STEP):
            left = jnp.concatenate([ring[slot, h * GROUP + j] for j in range(GROUP)], axis=1)
            right = jnp.concatenate([src[slab_ref[(group + h) * GROUP + j]] for j in range(GROUP)], axis=0)
            parts.append(jnp.dot(left, right, preferred_element_type=f32))
        for h in range(STEP):
            acc[into_ref[group + h]] += parts[h]
        begin(step + DEPTH)
        return carry

    return begin, lambda: lax.fori_loop(0, steps, run, 0)


def fold(acc, p):
    return jnp.where(
        lane_low((BLK, BLK)),
        acc[4 * p] + swap_halves(acc[4 * p + 1]),
        swap_halves(acc[4 * p + 2]) + acc[4 * p + 3],
    )


def own_kernel(hop, tile_ref, slab_ref, into_ref, groups_ref, tiles_ref, own_ref, noise_ref, part_ref, acc, src, noise, ring, sem, load):
    begin, run = add_groups(0, tile_ref, slab_ref, into_ref, groups_ref, tiles_ref, src, acc, ring, sem)
    for step in range(DEPTH):
        begin(step)
    noise_copy = pltpu.make_async_copy(noise_ref.at[hop], noise, load)
    noise_copy.start()
    acc[...] = jnp.zeros_like(acc)
    src[0:PAIRS] = own_ref[hop]
    src[PAIRS] = jnp.zeros((BLK, BLK), bf16)
    run()
    noise_copy.wait()
    for p in range(PAIRS):
        part_ref[p] = stacked_pair(noise, p).T + fold(acc, p)


def far_kernel(hop, tile_ref, slab_ref, into_ref, groups_ref, tiles_ref, got_ref, part_ref, *rest):
    last = hop == HOPS - 1
    if last:
        out_ref, acc, ring, sem = rest
    else:
        out_ref, sq_ref, acc, ring, sem = rest
    begin, run = add_groups(1, tile_ref, slab_ref, into_ref, groups_ref, tiles_ref, got_ref, acc, ring, sem)
    for step in range(DEPTH):
        begin(step)
    acc[...] = jnp.zeros_like(acc)
    run()
    pairs = []
    for p in range(PAIRS):
        u = part_ref[p] + fold(acc, p)
        pairs.append(u)
        if last:
            out_ref[p * BLK : (p + 1) * BLK] = u.astype(bf16)
        else:
            out_ref[p] = u
    total = pair_squares(pairs)
    if last:
        hi = total.astype(bf16).astype(f32)
        mid = (total - hi).astype(bf16).astype(f32)
        lo = total - hi - mid
        out_ref[PAIRS * BLK : PAIRS * BLK + 16] = jnp.concatenate([hi, mid], axis=0).astype(bf16)
        out_ref[PAIRS * BLK + 16 : PAIRS * BLK + 32] = jnp.concatenate([lo, jnp.zeros_like(lo)], axis=0).astype(bf16)
    else:
        sq_ref[...] = total


def early_kernel(x_ref, w_ref, *refs):
    h_refs, out_ref = refs[:-1], refs[-1]
    for p in range(PAIRS):
        total = jnp.zeros((BLK, BLK), f32)
        for k in range(HOPS):
            for j, shift in enumerate(SHIFTS):
                source = (x_ref[0] + NX - shift) % NX
                total = total + jnp.dot(h_refs[j][k, p], w_ref[k, source], preferred_element_type=f32)
        out_ref[p] = total


def final_kernel(x_ref, w_ref, early_ref, *refs):
    got_refs, out_ref = refs[:-1], refs[-1]
    total = jnp.zeros((BPD, BLK), f32)
    for got_ref in got_refs:
        a = got_ref[PAIRS * BLK : PAIRS * BLK + 16].astype(f32)
        b = got_ref[PAIRS * BLK + 16 : PAIRS * BLK + 32].astype(f32)
        total = total + (a[:BPD] + a[BPD:] + b[:BPD])
    columns = row_scale(total)
    for p in range(PAIRS):
        raw = jnp.zeros((BLK, BLK), f32)
        for j, shift in enumerate(SHIFTS):
            source = (x_ref[0] + NX - shift) % NX
            raw = raw + jnp.dot(got_refs[j][p * BLK : (p + 1) * BLK], w_ref[HOPS, source], preferred_element_type=f32)
        v = (early_ref[p] + raw * pair_scale(columns, p)).T
        out_ref[:, (2 * p) * BLK : (2 * p + 1) * BLK] = v[:WIDTH].astype(bf16)
        out_ref[:, (2 * p + 1) * BLK : (2 * p + 2) * BLK] = v[WIDTH:].astype(bf16)


def whole(space=VMEM):
    return pl.BlockSpec(memory_space=space)


def call(kernel, name, in_specs, outs, scratch=(), limit=24 << 20, flops=1 << 20, moved=1 << 20):
    shapes = [jax.ShapeDtypeStruct(dims, kind) for dims, kind, _ in outs]
    specs = [whole(space) for _, _, space in outs]
    single = len(outs) == 1
    return pl.pallas_call(
        kernel,
        name=name,
        out_shape=shapes[0] if single else shapes,
        in_specs=in_specs,
        out_specs=specs[0] if single else specs,
        scratch_shapes=list(scratch),
        compiler_params=pltpu.CompilerParams(vmem_limit_bytes=limit),
        cost_estimate=pl.CostEstimate(flops=flops, bytes_accessed=moved, transcendentals=0),
    )


def shift_by(value, axis, shift):
    size = lax.axis_size(axis)
    return lax.ppermute(value, axis, [(i, (i + shift) % size) for i in range(size)])


def slot_table(asked, start, base):
    mine = lax.dynamic_slice(asked, (0, *start, 0), (asked.shape[0], 1, base.shape[0], 1, 2)).reshape(asked.shape[0], base.shape[0], 2)
    odd = (mine & 1) ^ jnp.arange(2, dtype=jnp.int32)
    return (base[:, None] + (mine >> 1) + PAIRS * odd).reshape(-1)


def shards(features, tile_vals, tile_rows, tile_srcs, tile_count, needed, hop_noise, enc_weight):
    me = jnp.stack([lax.axis_index("y"), lax.axis_index("z"), lax.axis_index("core")]).astype(jnp.int32)
    x_index = lax.axis_index("x").astype(jnp.int32)
    x_only = x_index.reshape(1)
    noise = hop_noise.transpose(0, 2, 1)

    packed, squares = call(
        pack_kernel, "pack", [whole()],
        [((PAIRS, BLK, BLK), bf16, VMEM), ((BPD, BLK), f32, VMEM)],
    )(features.T)
    packed, squares, rows, srcs, count, enc_weight, needed = lax.optimization_barrier(
        (packed, squares, tile_rows.reshape(-1), tile_srcs.reshape(-1), tile_count, enc_weight, needed.reshape(-1))
    )

    weights = lax.dynamic_slice_in_dim(enc_weight, x_index * WIDTH, WIDTH, axis=2).reshape(HOPS + 1, NX, WIDTH, WIDTH)
    nothing = jnp.zeros_like(weights)
    weights = jnp.concatenate(
        [jnp.concatenate([weights, nothing], axis=-1), jnp.concatenate([nothing, weights], axis=-1)], axis=-2
    )
    lists = call(
        order_kernel, "order", [whole(SMEM)] * 4,
        [((2 * SLOTS,), jnp.int32, SMEM), ((2 * SLOTS,), jnp.int32, SMEM), ((2 * MAXG,), jnp.int32, SMEM), ((2,), jnp.int32, SMEM)],
        [SMEM((2 * BUCKETS,), jnp.int32), SMEM((2 * BUCKETS,), jnp.int32)],
    )(me, rows, srcs, count)
    owned = None
    for hop in range(HOPS):
        last = hop == HOPS - 1
        totals = [squares] + [shift_by(squares, "x", shift) for shift in SHIFTS[1:]]
        wide = [((N_ROW, BLK, BLK), bf16, HBM)]
        if last:
            picked, owned = call(
                send_kernel, "send", [whole(SMEM)] * 2 + [whole()] * (2 + NX), wide + [((2, PAIRS, BLK, BLK), bf16, VMEM)],
                [VMEM((BPD, BLK, BLK), bf16), VMEM((N_ROW, BLK, BLK), bf16), DMA((N_ROW // BATCH,))],
                limit=MOST,
            )(me, table, packed, *totals, owned)
            spread = [owned] + [shift_by(owned, "x", shift) for shift in SHIFTS[1:]]
            got = lax.all_to_all(picked, ("y", "core", "z"), 0, 0, tiled=True)
        else:
            packed, owned = call(
                norm_kernel, "norm", [whole()] * (1 + NX),
                [((NZ, PAIRS, BLK, BLK), bf16, HBM), ((1, PAIRS, BLK, BLK), bf16, VMEM)],
                [VMEM((PAIRS, BLK, BLK), bf16), DMA((NZ,))],
                limit=TIGHT,
            )(packed, *totals)
            along = lax.all_to_all(packed, "z", 0, 0, tiled=True)
            needed, owned = lax.optimization_barrier((needed, owned))
            asked = lax.all_gather(needed, ("y", "core"), axis=0)
            table = slot_table(asked.reshape(NY * NC, NY, NZ, NC, 2), (me[0], 0, me[2]), jnp.arange(NZ, dtype=jnp.int32) * BPD)
            at, table, asked, *lists = lax.optimization_barrier((me, table, asked, *lists))
            picked = call(
                pick_kernel, "pick", [whole(SMEM)] * 2 + [whole()], wide,
                [VMEM((NZ * BPD, BLK, BLK), bf16), VMEM((N_ROW, BLK, BLK), bf16), DMA((N_ROW // BATCH,))],
                limit=MOST,
            )(at, table, along)
            picked, asked = lax.optimization_barrier((picked, asked))
            got = lax.all_to_all(picked, ("y", "core"), 0, 0, tiled=True)
            everyone = lax.all_gather(asked, "z", axis=1).reshape(NY * NC * NZ, NY, NZ, NC, 2)
            table = slot_table(everyone, (me[0], me[1], me[2]), jnp.zeros((1,), jnp.int32))
        ring = [VMEM((DEPTH, STEP * GROUP, BLK, BLK), bf16), DMA((DEPTH, STEP * GROUP))]
        part = call(
            functools.partial(own_kernel, hop), "own", [whole(SMEM)] * 4 + [whole(HBM), whole(), whole(HBM)],
            [((PAIRS, BLK, BLK), f32, VMEM)],
            [VMEM((BUCKETS, BLK, BLK), f32), VMEM((PAIRS + 1, BLK, BLK), bf16), VMEM((WIDTH, BPD * BLK), f32)] + ring + [DMA(())],
            limit=FULL, flops=TPD * 2 * BLK**3, moved=4 << 20,
        )(*lists, tile_vals, owned, noise)
        if not last:
            part, table = lax.optimization_barrier((part, table))
        if last:
            early = call(
                early_kernel, "early", [whole(SMEM)] + [whole()] * (1 + NX), [((PAIRS, BLK, BLK), f32, VMEM)]
            )(x_only, weights, *spread)
            early, part = lax.optimization_barrier((early, part))
        if last:
            outs = [((PAIRS * BLK + 32, BLK), bf16, VMEM)]
            more = []
        else:
            outs = [((PAIRS, BLK, BLK), f32, VMEM), ((BPD, BLK), f32, VMEM)]
            more = []
        result = call(
            functools.partial(far_kernel, hop), "far", [whole(SMEM)] * 4 + [whole(HBM), whole(), whole()], outs,
            [VMEM((BUCKETS, BLK, BLK), f32)] + ring + more,
            limit=ROOM, flops=TPD * 2 * BLK**3, moved=8 << 20,
        )(*lists, tile_vals, got, part)
        if not last:
            packed, squares = result
    tails = [result] + [shift_by(result, "x", shift) for shift in SHIFTS[1:]]
    return call(
        final_kernel, "final", [whole(SMEM)] + [whole()] * (2 + NX), [((WIDTH, BPD * BLK), bf16, VMEM)],
    )(x_only, weights, early, *tails).T


def solution(mesh):
    grid = Mesh(np.array(mesh.devices).reshape(NY, NZ, NC, NX), ("y", "z", "core", "x"))
    row = ("y", "z", "core")
    in_specs = (
        P(row, "x"),
        P(row, None, None),
        P(row, None),
        P(row, None),
        P(row),
        P(row, None, None),
        P(None, row, "x"),
        P(),
    )
    return jax.shard_map(shards, mesh=grid, in_specs=in_specs, out_specs=P(row, "x"), check_vma=False)
```

```python
import functools

import jax
import jax.numpy as jnp
import numpy as np
from jax import lax
from jax.experimental import pallas as pl
from jax.experimental.pallas import tpu as pltpu
from jax.sharding import Mesh, PartitionSpec as P

BLK = 128
BPD = 8
TPD = 160
PAIRS = BPD // 2
HOPS = 2
NY, NZ, NC, NX = 4, 8, 2, 4
WIDTH = 64
GROUP = 4
STEP = 4
BUCKETS = 2 * BPD
MAXG = TPD // GROUP + BUCKETS
SLOTS = MAXG * GROUP
SHIFTS = (0, 2, 1, 3)
N_ROW = NY * NZ * NC
ZSHIFTS = (0, 4, 3, 5, 2, 6, 1, 7)
DEPTH = 4
FULL = 63 << 20
MOST = 65_000_000
TIGHT = 66_200_000
ROOM = 63_600_000
EPS = 1e-06
bf16 = jnp.bfloat16
f32 = jnp.float32
VMEM = pltpu.VMEM
SMEM = pltpu.SMEM
HBM = pltpu.HBM
DMA = pltpu.SemaphoreType.DMA


def lane_low(shape):
    return lax.broadcasted_iota(jnp.int32, shape, len(shape) - 1) < WIDTH


def pair_squares(pair_values):
    total = jnp.zeros((BPD, BLK), f32)
    row = lax.broadcasted_iota(jnp.int32, (BPD, BLK), 0)
    half = lax.broadcasted_iota(jnp.int32, (BPD, BLK), 1) // WIDTH
    for p in range(PAIRS):
        v = pair_values[p]
        pick = jnp.where(row == 2 * p + half, 1.0, 0.0).astype(f32)
        total = total + lax.dot_general(
            pick, v * v, (((1,), (1,)), ((), ())),
            precision=lax.Precision.HIGHEST, preferred_element_type=f32,
        )
    return total


def row_scale(total):
    return (1.0 / jnp.sqrt(total + EPS)).T


def pair_scale(columns, p):
    return jnp.where(
        lane_low((BLK, BLK)),
        jnp.broadcast_to(columns[:, 2 * p : 2 * p + 1], (BLK, BLK)),
        jnp.broadcast_to(columns[:, 2 * p + 1 : 2 * p + 2], (BLK, BLK)),
    )


def swap_halves(v):
    return pltpu.roll(v, WIDTH, 1)


def stacked_pair(ref, p):
    first = ref[:, (2 * p) * BLK : (2 * p + 1) * BLK].astype(f32)
    second = ref[:, (2 * p + 1) * BLK : (2 * p + 2) * BLK].astype(f32)
    return jnp.concatenate([first, second], axis=0)


def pack_kernel(feat_ref, out_ref, sq_ref):
    rows = []
    for p in range(PAIRS):
        stacked = stacked_pair(feat_ref, p)
        out_ref[p] = stacked.T.astype(bf16)
        squares = stacked * stacked
        rows.append(jnp.sum(squares[:WIDTH], axis=0, keepdims=True))
        rows.append(jnp.sum(squares[WIDTH:], axis=0, keepdims=True))
    sq_ref[...] = jnp.concatenate(rows, axis=0)


def total_of(refs):
    total = refs[0][...]
    for ref in refs[1:]:
        total = total + ref[...]
    return total


def swapped(v):
    return jnp.concatenate([v[:, WIDTH:], v[:, :WIDTH]], axis=1)


def norm_kernel(raw_ref, *refs):
    out_ref, own_ref, buf, sem = refs[NX:]
    columns = row_scale(total_of(refs[:NX]))
    copies = []
    for p in range(PAIRS):
        v = (raw_ref[p].astype(f32) * pair_scale(columns, p)).astype(bf16)
        buf[p] = v
        own_ref[0, p] = v
    for z in range(NZ):
        copy = pltpu.make_async_copy(buf, out_ref.at[z], sem.at[z])
        copy.start()
        copies.append(copy)
    for copy in copies:
        copy.wait()


def write_slabs(me_ref, slab_of, out_ref, buf, sem):
    mine = me_ref[0] * NC + me_ref[2]
    copies = []
    for dest in range(NY * NC):
        for j in range(NZ):
            z, slab = slab_of(dest, j)
            buf[dest * NZ + z] = slab

        @pl.when(mine == dest)
        def _():
            buf[dest * NZ + me_ref[1]] = jnp.zeros((BLK, BLK), bf16)

        copy = pltpu.make_async_copy(
            buf.at[pl.ds(dest * NZ, NZ)], out_ref.at[pl.ds(dest * NZ, NZ)], sem.at[dest]
        )
        copy.start()
        copies.append(copy)
    for copy in copies:
        copy.wait()


def pick_kernel(me_ref, idx_ref, z_ref, out_ref, slots, buf, sem):
    for z in range(NZ):
        for p in range(PAIRS):
            v = z_ref[z, p]
            slots[z * BPD + p] = v
            slots[z * BPD + PAIRS + p] = swapped(v)
    mask = lane_low((BLK, BLK))

    def slab_of(dest, j):
        i = 2 * (dest * NZ + j)
        return j, jnp.where(mask, slots[idx_ref[i]], slots[idx_ref[i + 1]])

    write_slabs(me_ref, slab_of, out_ref, buf, sem)


def send_kernel(me_ref, *refs):
    asked_refs, raw_ref, refs = refs[:NZ], refs[NZ], refs[NZ + 1 :]
    before_ref, out_ref, own_ref, slots, buf, sem = refs[NX:]
    columns = row_scale(total_of(refs[:NX]))
    own_ref[0] = before_ref[0]
    for p in range(PAIRS):
        v = (raw_ref[p] * pair_scale(columns, p)).astype(bf16)
        own_ref[1, p] = v
        slots[p] = v
        slots[PAIRS + p] = swapped(v)
    mask = lane_low((BLK, BLK))
    at = ((me_ref[0] * NZ + me_ref[1]) * NC + me_ref[2]) * 2

    def slab_of(dest, j):
        z = (me_ref[1] + NZ - ZSHIFTS[j]) & (NZ - 1)
        first = asked_refs[j][dest, at]
        second = asked_refs[j][dest, at + 1]
        low = (first >> 1) | ((first & 1) << 2)
        high = ((second >> 1) | ((second & 1) << 2)) ^ PAIRS
        return z, jnp.where(mask, slots[low], slots[high])

    write_slabs(me_ref, slab_of, out_ref, buf, sem)


def order_kernel(me_ref, rows_ref, srcs_ref, count_ref, tile_ref, slab_ref, into_ref, groups_ref, fill, begin):
    count = count_ref[0]
    empty = (me_ref[0] * NC + me_ref[2]) * NZ + me_ref[1]

    @pl.loop(0, SLOTS // 8)
    def _(i):
        for j in range(8):
            tile_ref[i * 8 + j] = 0
            tile_ref[SLOTS + i * 8 + j] = 0
            slab_ref[i * 8 + j] = PAIRS
            slab_ref[SLOTS + i * 8 + j] = empty

    @pl.loop(0, 2 * MAXG)
    def _(i):
        into_ref[i] = 0

    for b in range(2 * BUCKETS):
        fill[b] = 0

    def bucket_of(t):
        s = srcs_ref[t]
        return jnp.where(s < BPD, 0, BUCKETS) + rows_ref[t] * 2 + (s & 1)

    @pl.loop(0, count)
    def _(t):
        b = bucket_of(t)
        fill[b] = fill[b] + 1

    for kind in range(2):
        def place(b, group):
            size = (fill[kind * BUCKETS + b] + GROUP - 1) // GROUP
            begin[kind * BUCKETS + b] = (kind * MAXG + group) * GROUP

            @pl.loop(0, size)
            def _(i):
                into_ref[kind * MAXG + group + i] = b

            return group + size

        groups_ref[kind] = lax.fori_loop(0, BUCKETS, place, jnp.int32(0))

    @pl.loop(0, count)
    def _(t):
        b = bucket_of(t)
        at = begin[b]
        begin[b] = at + 1
        s = srcs_ref[t]
        tile_ref[at] = t
        o = (s - BPD) >> 1
        far_slab = (((o >> 4) * NC) + (o & 1)) * NZ + ((o >> 1) & (NZ - 1))
        slab_ref[at] = jnp.where(s < BPD, s >> 1, far_slab)


def add_groups(kind, tile_ref, slab_ref, into_ref, groups_ref, tiles_ref, src, acc, ring, sem):
    steps = (groups_ref[kind] + STEP - 1) // STEP

    def copies(step):
        slot = step % DEPTH
        first = (kind * MAXG + STEP * step) * GROUP
        return [
            pltpu.make_async_copy(tiles_ref.at[tile_ref[first + j]], ring.at[slot, j], sem.at[slot, j])
            for j in range(STEP * GROUP)
        ]

    def begin(step):
        @pl.when(step < steps)
        def _():
            for copy in copies(step):
                copy.start()

    def run(step, carry):
        slot = step % DEPTH
        group = kind * MAXG + STEP * step
        for copy in copies(step):
            copy.wait()
        parts = []
        for h in range(STEP):
            left = jnp.concatenate([ring[slot, h * GROUP + j] for j in range(GROUP)], axis=1)
            right = jnp.concatenate([src[slab_ref[(group + h) * GROUP + j]] for j in range(GROUP)], axis=0)
            parts.append(jnp.dot(left, right, preferred_element_type=f32))
        for h in range(STEP):
            acc[into_ref[group + h]] += parts[h]
        begin(step + DEPTH)
        return carry

    return begin, lambda: lax.fori_loop(0, steps, run, 0)


def fold(acc, p):
    return jnp.where(
        lane_low((BLK, BLK)),
        acc[4 * p] + swap_halves(acc[4 * p + 1]),
        swap_halves(acc[4 * p + 2]) + acc[4 * p + 3],
    )


def own_kernel(hop, tile_ref, slab_ref, into_ref, groups_ref, tiles_ref, own_ref, noise_ref, part_ref, acc, src, noise, ring, sem, load):
    begin, run = add_groups(0, tile_ref, slab_ref, into_ref, groups_ref, tiles_ref, src, acc, ring, sem)
    for step in range(DEPTH):
        begin(step)
    noise_copy = pltpu.make_async_copy(noise_ref.at[hop], noise, load)
    noise_copy.start()
    acc[...] = jnp.zeros_like(acc)
    src[0:PAIRS] = own_ref[hop]
    src[PAIRS] = jnp.zeros((BLK, BLK), bf16)
    run()
    noise_copy.wait()
    for p in range(PAIRS):
        part_ref[p] = stacked_pair(noise, p).T + fold(acc, p)


def far_kernel(hop, tile_ref, slab_ref, into_ref, groups_ref, tiles_ref, got_ref, part_ref, *rest):
    last = hop == HOPS - 1
    if last:
        out_ref, acc, ring, sem = rest
    else:
        out_ref, sq_ref, acc, ring, sem = rest
    begin, run = add_groups(1, tile_ref, slab_ref, into_ref, groups_ref, tiles_ref, got_ref, acc, ring, sem)
    for step in range(DEPTH):
        begin(step)
    acc[...] = jnp.zeros_like(acc)
    run()
    pairs = []
    for p in range(PAIRS):
        u = part_ref[p] + fold(acc, p)
        pairs.append(u)
        if last:
            out_ref[p * BLK : (p + 1) * BLK] = u.astype(bf16)
        else:
            out_ref[p] = u
    total = pair_squares(pairs)
    if last:
        hi = total.astype(bf16).astype(f32)
        mid = (total - hi).astype(bf16).astype(f32)
        lo = total - hi - mid
        out_ref[PAIRS * BLK : PAIRS * BLK + 16] = jnp.concatenate([hi, mid], axis=0).astype(bf16)
        out_ref[PAIRS * BLK + 16 : PAIRS * BLK + 32] = jnp.concatenate([lo, jnp.zeros_like(lo)], axis=0).astype(bf16)
    else:
        sq_ref[...] = total


def early_kernel(x_ref, w_ref, *refs):
    h_refs, out_ref = refs[:-1], refs[-1]
    for p in range(PAIRS):
        total = jnp.zeros((BLK, BLK), f32)
        for k in range(HOPS):
            for j, shift in enumerate(SHIFTS):
                source = (x_ref[0] + NX - shift) % NX
                total = total + jnp.dot(h_refs[j][k, p], w_ref[k, source], preferred_element_type=f32)
        out_ref[p] = total


def final_kernel(x_ref, w_ref, early_ref, *refs):
    got_refs, out_ref = refs[:-1], refs[-1]
    total = jnp.zeros((BPD, BLK), f32)
    for got_ref in got_refs:
        a = got_ref[PAIRS * BLK : PAIRS * BLK + 16].astype(f32)
        b = got_ref[PAIRS * BLK + 16 : PAIRS * BLK + 32].astype(f32)
        total = total + (a[:BPD] + a[BPD:] + b[:BPD])
    columns = row_scale(total)
    for p in range(PAIRS):
        raw = jnp.zeros((BLK, BLK), f32)
        for j, shift in enumerate(SHIFTS):
            source = (x_ref[0] + NX - shift) % NX
            raw = raw + jnp.dot(got_refs[j][p * BLK : (p + 1) * BLK], w_ref[HOPS, source], preferred_element_type=f32)
        v = (early_ref[p] + raw * pair_scale(columns, p)).T
        out_ref[:, (2 * p) * BLK : (2 * p + 1) * BLK] = v[:WIDTH].astype(bf16)
        out_ref[:, (2 * p + 1) * BLK : (2 * p + 2) * BLK] = v[WIDTH:].astype(bf16)


def whole(space=VMEM):
    return pl.BlockSpec(memory_space=space)


def call(kernel, name, in_specs, outs, scratch=(), limit=24 << 20, flops=1 << 20, moved=1 << 20):
    shapes = [jax.ShapeDtypeStruct(dims, kind) for dims, kind, _ in outs]
    specs = [whole(space) for _, _, space in outs]
    single = len(outs) == 1
    return pl.pallas_call(
        kernel,
        name=name,
        out_shape=shapes[0] if single else shapes,
        in_specs=in_specs,
        out_specs=specs[0] if single else specs,
        scratch_shapes=list(scratch),
        compiler_params=pltpu.CompilerParams(vmem_limit_bytes=limit),
        cost_estimate=pl.CostEstimate(flops=flops, bytes_accessed=moved, transcendentals=0),
    )


def shift_by(value, axis, shift):
    size = lax.axis_size(axis)
    return lax.ppermute(value, axis, [(i, (i + shift) % size) for i in range(size)])


def slot_table(asked, start, base):
    mine = lax.dynamic_slice(asked, (0, *start, 0), (asked.shape[0], 1, base.shape[0], 1, 2)).reshape(asked.shape[0], base.shape[0], 2)
    odd = (mine & 1) ^ jnp.arange(2, dtype=jnp.int32)
    return (base[:, None] + (mine >> 1) + PAIRS * odd).reshape(-1)


def shards(features, tile_vals, tile_rows, tile_srcs, tile_count, needed, hop_noise, enc_weight):
    me = jnp.stack([lax.axis_index("y"), lax.axis_index("z"), lax.axis_index("core")]).astype(jnp.int32)
    x_index = lax.axis_index("x").astype(jnp.int32)
    x_only = x_index.reshape(1)
    noise = hop_noise.transpose(0, 2, 1)

    packed, squares = call(
        pack_kernel, "pack", [whole()],
        [((PAIRS, BLK, BLK), bf16, VMEM), ((BPD, BLK), f32, VMEM)],
    )(features.T)
    packed, squares, rows, srcs, count, enc_weight, needed = lax.optimization_barrier(
        (packed, squares, tile_rows.reshape(-1), tile_srcs.reshape(-1), tile_count, enc_weight, needed)
    )

    weights = lax.dynamic_slice_in_dim(enc_weight, x_index * WIDTH, WIDTH, axis=2).reshape(HOPS + 1, NX, WIDTH, WIDTH)
    nothing = jnp.zeros_like(weights)
    weights = jnp.concatenate(
        [jnp.concatenate([weights, nothing], axis=-1), jnp.concatenate([nothing, weights], axis=-1)], axis=-2
    )
    lists = call(
        order_kernel, "order", [whole(SMEM)] * 4,
        [((2 * SLOTS,), jnp.int32, SMEM), ((2 * SLOTS,), jnp.int32, SMEM), ((2 * MAXG,), jnp.int32, SMEM), ((2,), jnp.int32, SMEM)],
        [SMEM((2 * BUCKETS,), jnp.int32), SMEM((2 * BUCKETS,), jnp.int32)],
    )(me, rows, srcs, count)
    owned = None
    for hop in range(HOPS):
        last = hop == HOPS - 1
        totals = [squares] + [shift_by(squares, "x", shift) for shift in SHIFTS[1:]]
        wide = [((N_ROW, BLK, BLK), bf16, HBM)]
        if last:
            picked, owned = call(
                send_kernel, "send", [whole(SMEM)] * (1 + NZ) + [whole()] * (2 + NX), wide + [((2, PAIRS, BLK, BLK), bf16, VMEM)],
                [VMEM((BPD, BLK, BLK), bf16), VMEM((N_ROW, BLK, BLK), bf16), DMA((NY * NC,))],
                limit=MOST,
            )(me, *tables, packed, *totals, owned)
            spread = [owned] + [shift_by(owned, "x", shift) for shift in SHIFTS[1:]]
            got = lax.all_to_all(picked, ("y", "core", "z"), 0, 0, tiled=True)
        else:
            packed, owned = call(
                norm_kernel, "norm", [whole()] * (1 + NX),
                [((NZ, PAIRS, BLK, BLK), bf16, HBM), ((1, PAIRS, BLK, BLK), bf16, VMEM)],
                [VMEM((PAIRS, BLK, BLK), bf16), DMA((NZ,))],
                limit=TIGHT,
            )(packed, *totals)
            along = lax.all_to_all(packed, "z", 0, 0, tiled=True)
            needed, owned = lax.optimization_barrier((needed, owned))
            asked = lax.all_gather(needed.reshape(-1), ("y", "core"), axis=0)
            table = slot_table(asked.reshape(NY * NC, NY, NZ, NC, 2), (me[0], 0, me[2]), jnp.arange(NZ, dtype=jnp.int32) * BPD)
            at, table, asked, *lists = lax.optimization_barrier((me, table, asked, *lists))
            picked = call(
                pick_kernel, "pick", [whole(SMEM)] * 2 + [whole()], wide,
                [VMEM((NZ * BPD, BLK, BLK), bf16), VMEM((N_ROW, BLK, BLK), bf16), DMA((NY * NC,))],
                limit=MOST,
            )(at, table, along)
            picked, asked = lax.optimization_barrier((picked, asked))
            got = lax.all_to_all(picked, ("y", "core"), 0, 0, tiled=True)
            tables = [asked] + [shift_by(asked, "z", shift) for shift in ZSHIFTS[1:]]
        ring = [VMEM((DEPTH, STEP * GROUP, BLK, BLK), bf16), DMA((DEPTH, STEP * GROUP))]
        part = call(
            functools.partial(own_kernel, hop), "own", [whole(SMEM)] * 4 + [whole(HBM), whole(), whole(HBM)],
            [((PAIRS, BLK, BLK), f32, VMEM)],
            [VMEM((BUCKETS, BLK, BLK), f32), VMEM((PAIRS + 1, BLK, BLK), bf16), VMEM((WIDTH, BPD * BLK), f32)] + ring + [DMA(())],
            limit=FULL, flops=TPD * 2 * BLK**3, moved=4 << 20,
        )(*lists, tile_vals, owned, noise)
        if not last:
            part, *tables = lax.optimization_barrier((part, *tables))
        if last:
            early = call(
                early_kernel, "early", [whole(SMEM)] + [whole()] * (1 + NX), [((PAIRS, BLK, BLK), f32, VMEM)]
            )(x_only, weights, *spread)
            early, part = lax.optimization_barrier((early, part))
        if last:
            outs = [((PAIRS * BLK + 32, BLK), bf16, VMEM)]
            more = []
        else:
            outs = [((PAIRS, BLK, BLK), f32, VMEM), ((BPD, BLK), f32, VMEM)]
            more = []
        result = call(
            functools.partial(far_kernel, hop), "far", [whole(SMEM)] * 4 + [whole(HBM), whole(), whole()], outs,
            [VMEM((BUCKETS, BLK, BLK), f32)] + ring + more,
            limit=ROOM, flops=TPD * 2 * BLK**3, moved=8 << 20,
        )(*lists, tile_vals, got, part)
        if not last:
            packed, squares = result
    tails = [result] + [shift_by(result, "x", shift) for shift in SHIFTS[1:]]
    return call(
        final_kernel, "final", [whole(SMEM)] + [whole()] * (2 + NX), [((WIDTH, BPD * BLK), bf16, VMEM)],
    )(x_only, weights, early, *tails).T


def solution(mesh):
    grid = Mesh(np.array(mesh.devices).reshape(NY, NZ, NC, NX), ("y", "z", "core", "x"))
    row = ("y", "z", "core")
    in_specs = (
        P(row, "x"),
        P(row, None, None),
        P(row, None),
        P(row, None),
        P(row),
        P(row, None, None),
        P(None, row, "x"),
        P(),
    )
    return jax.shard_map(shards, mesh=grid, in_specs=in_specs, out_specs=P(row, "x"), check_vma=False)
```

```python
import functools

import jax
import jax.numpy as jnp
import numpy as np
from jax import lax
from jax.experimental import pallas as pl
from jax.experimental.pallas import tpu as pltpu
from jax.sharding import Mesh, PartitionSpec as P

BLK = 128
BPD = 8
TPD = 160
PAIRS = BPD // 2
HOPS = 2
NY, NZ, NC, NX = 4, 8, 2, 4
WIDTH = 64
GROUP = 4
STEP = 4
BUCKETS = 2 * BPD
MAXG = TPD // GROUP + BUCKETS
SLOTS = MAXG * GROUP
SHIFTS = (0, 2, 1, 3)
N_ROW = NY * NZ * NC
ZSHIFTS = (0, 4, 3, 5, 2, 6, 1, 7)
DEPTH = 4
FULL = 63 << 20
MOST = 65_000_000
NORM = 24 << 20
ROOM = 63_600_000
EPS = 1e-06
bf16 = jnp.bfloat16
f32 = jnp.float32
VMEM = pltpu.VMEM
SMEM = pltpu.SMEM
HBM = pltpu.HBM
DMA = pltpu.SemaphoreType.DMA


def lane_low(shape):
    return lax.broadcasted_iota(jnp.int32, shape, len(shape) - 1) < WIDTH


def pair_squares(pair_values):
    total = jnp.zeros((BPD, BLK), f32)
    row = lax.broadcasted_iota(jnp.int32, (BPD, BLK), 0)
    half = lax.broadcasted_iota(jnp.int32, (BPD, BLK), 1) // WIDTH
    for p in range(PAIRS):
        v = pair_values[p]
        pick = jnp.where(row == 2 * p + half, 1.0, 0.0).astype(f32)
        total = total + lax.dot_general(
            pick, v * v, (((1,), (1,)), ((), ())),
            precision=lax.Precision.HIGHEST, preferred_element_type=f32,
        )
    return total


def row_scale(total):
    return (1.0 / jnp.sqrt(total + EPS)).T


def pair_scale(columns, p):
    return jnp.where(
        lane_low((BLK, BLK)),
        jnp.broadcast_to(columns[:, 2 * p : 2 * p + 1], (BLK, BLK)),
        jnp.broadcast_to(columns[:, 2 * p + 1 : 2 * p + 2], (BLK, BLK)),
    )


def swap_halves(v):
    return pltpu.roll(v, WIDTH, 1)


def stacked_pair(ref, p):
    first = ref[:, (2 * p) * BLK : (2 * p + 1) * BLK].astype(f32)
    second = ref[:, (2 * p + 1) * BLK : (2 * p + 2) * BLK].astype(f32)
    return jnp.concatenate([first, second], axis=0)


def pack_kernel(feat_ref, out_ref, sq_ref):
    rows = []
    for p in range(PAIRS):
        stacked = stacked_pair(feat_ref, p)
        out_ref[p] = stacked.T.astype(bf16)
        squares = stacked * stacked
        rows.append(jnp.sum(squares[:WIDTH], axis=0, keepdims=True))
        rows.append(jnp.sum(squares[WIDTH:], axis=0, keepdims=True))
    sq_ref[...] = jnp.concatenate(rows, axis=0)


def total_of(refs):
    total = refs[0][...]
    for ref in refs[1:]:
        total = total + ref[...]
    return total


def swapped(v):
    return jnp.concatenate([v[:, WIDTH:], v[:, :WIDTH]], axis=1)


def norm_kernel(raw_ref, *refs):
    out_ref, own_ref, buf, sem = refs[NX:]
    columns = row_scale(total_of(refs[:NX]))
    copies = []
    for p in range(PAIRS):
        v = (raw_ref[p].astype(f32) * pair_scale(columns, p)).astype(bf16)
        buf[p] = v
    for z in range(NZ):
        copy = pltpu.make_async_copy(buf, out_ref.at[z], sem.at[z])
        copy.start()
        copies.append(copy)
    copies.append(pltpu.make_async_copy(buf, own_ref.at[0], sem.at[NZ]))
    copies[-1].start()
    for copy in copies:
        copy.wait()


def write_slabs(me_ref, slab_of, out_ref, buf, sem):
    mine = me_ref[0] * NC + me_ref[2]
    copies = []
    for dest in range(NY * NC):
        for j in range(NZ):
            z, slab = slab_of(dest, j)
            buf[dest * NZ + z] = slab

        @pl.when(mine == dest)
        def _():
            buf[dest * NZ + me_ref[1]] = jnp.zeros((BLK, BLK), bf16)

        copy = pltpu.make_async_copy(
            buf.at[pl.ds(dest * NZ, NZ)], out_ref.at[pl.ds(dest * NZ, NZ)], sem.at[dest]
        )
        copy.start()
        copies.append(copy)
    for copy in copies:
        copy.wait()


def pick_kernel(me_ref, idx_ref, z_ref, out_ref, slots, buf, sem):
    for z in range(NZ):
        for p in range(PAIRS):
            v = z_ref[z, p]
            slots[z * BPD + p] = v
            slots[z * BPD + PAIRS + p] = swapped(v)
    mask = lane_low((BLK, BLK))

    def slab_of(dest, j):
        i = 2 * (dest * NZ + j)
        return j, jnp.where(mask, slots[idx_ref[i]], slots[idx_ref[i + 1]])

    write_slabs(me_ref, slab_of, out_ref, buf, sem)


def send_kernel(me_ref, *refs):
    asked_refs, raw_ref, refs = refs[:NZ], refs[NZ], refs[NZ + 1 :]
    before_ref, out_ref, own_ref, slots, buf, sem = refs[NX:]
    columns = row_scale(total_of(refs[:NX]))
    own_ref[0] = before_ref[0]
    for p in range(PAIRS):
        v = (raw_ref[p] * pair_scale(columns, p)).astype(bf16)
        own_ref[1, p] = v
        slots[p] = v
        slots[PAIRS + p] = swapped(v)
    mask = lane_low((BLK, BLK))
    at = ((me_ref[0] * NZ + me_ref[1]) * NC + me_ref[2]) * 2

    def slab_of(dest, j):
        z = (me_ref[1] + NZ - ZSHIFTS[j]) & (NZ - 1)
        first = asked_refs[j][dest, at]
        second = asked_refs[j][dest, at + 1]
        low = (first >> 1) | ((first & 1) << 2)
        high = ((second >> 1) | ((second & 1) << 2)) ^ PAIRS
        return z, jnp.where(mask, slots[low], slots[high])

    write_slabs(me_ref, slab_of, out_ref, buf, sem)


class Part:
    def __init__(self, ref, start):
        self.ref, self.start = ref, start

    def __getitem__(self, i):
        return self.ref[self.start + i]

    def __setitem__(self, i, value):
        self.ref[self.start + i] = value


def parts_of(ref):
    return [Part(ref, start) for start in (0, 2 * SLOTS, 4 * SLOTS, 4 * SLOTS + 2 * MAXG)]


def order_kernel(me_ref, rows_ref, srcs_ref, count_ref, lists_ref, fill, begin):
    tile_ref, slab_ref, into_ref, groups_ref = parts_of(lists_ref)
    count = count_ref[0]
    empty = (me_ref[0] * NC + me_ref[2]) * NZ + me_ref[1]

    @pl.loop(0, SLOTS // 8)
    def _(i):
        for j in range(8):
            tile_ref[i * 8 + j] = 0
            tile_ref[SLOTS + i * 8 + j] = 0
            slab_ref[i * 8 + j] = PAIRS
            slab_ref[SLOTS + i * 8 + j] = empty

    @pl.loop(0, 2 * MAXG)
    def _(i):
        into_ref[i] = 0

    for b in range(2 * BUCKETS):
        fill[b] = 0

    def bucket_of(t):
        s = srcs_ref[t]
        return jnp.where(s < BPD, 0, BUCKETS) + rows_ref[t] * 2 + (s & 1)

    @pl.loop(0, count)
    def _(t):
        b = bucket_of(t)
        fill[b] = fill[b] + 1

    for kind in range(2):
        def place(b, group):
            size = (fill[kind * BUCKETS + b] + GROUP - 1) // GROUP
            begin[kind * BUCKETS + b] = (kind * MAXG + group) * GROUP

            @pl.loop(0, size)
            def _(i):
                into_ref[kind * MAXG + group + i] = b

            return group + size

        groups_ref[kind] = lax.fori_loop(0, BUCKETS, place, jnp.int32(0))

    @pl.loop(0, count)
    def _(t):
        b = bucket_of(t)
        at = begin[b]
        begin[b] = at + 1
        s = srcs_ref[t]
        tile_ref[at] = t
        o = (s - BPD) >> 1
        far_slab = (((o >> 4) * NC) + (o & 1)) * NZ + ((o >> 1) & (NZ - 1))
        slab_ref[at] = jnp.where(s < BPD, s >> 1, far_slab)


def add_groups(kind, tile_ref, slab_ref, into_ref, groups_ref, tiles_ref, src, acc, ring, sem):
    steps = (groups_ref[kind] + STEP - 1) // STEP

    def copies(step):
        slot = step % DEPTH
        first = (kind * MAXG + STEP * step) * GROUP
        return [
            pltpu.make_async_copy(tiles_ref.at[tile_ref[first + j]], ring.at[slot, j], sem.at[slot, j])
            for j in range(STEP * GROUP)
        ]

    def begin(step):
        @pl.when(step < steps)
        def _():
            for copy in copies(step):
                copy.start()

    def run(step, carry):
        slot = step % DEPTH
        group = kind * MAXG + STEP * step
        for copy in copies(step):
            copy.wait()
        parts = []
        for h in range(STEP):
            left = jnp.concatenate([ring[slot, h * GROUP + j] for j in range(GROUP)], axis=1)
            right = jnp.concatenate([src[slab_ref[(group + h) * GROUP + j]] for j in range(GROUP)], axis=0)
            parts.append(jnp.dot(left, right, preferred_element_type=f32))
        for h in range(STEP):
            acc[into_ref[group + h]] += parts[h]
        begin(step + DEPTH)
        return carry

    return begin, lambda: lax.fori_loop(0, steps, run, 0)


def fold(acc, p):
    return jnp.where(
        lane_low((BLK, BLK)),
        acc[4 * p] + swap_halves(acc[4 * p + 1]),
        swap_halves(acc[4 * p + 2]) + acc[4 * p + 3],
    )


def own_kernel(hop, lists_ref, tiles_ref, own_ref, noise_ref, part_ref, acc, src, noise, ring, sem, load):
    begin, run = add_groups(0, *parts_of(lists_ref), tiles_ref, src, acc, ring, sem)
    for step in range(DEPTH):
        begin(step)
    noise_copy = pltpu.make_async_copy(noise_ref.at[hop], noise, load)
    noise_copy.start()
    acc[...] = jnp.zeros_like(acc)
    src[0:PAIRS] = own_ref[hop]
    src[PAIRS] = jnp.zeros((BLK, BLK), bf16)
    run()
    noise_copy.wait()
    for p in range(PAIRS):
        part_ref[p] = stacked_pair(noise, p).T + fold(acc, p)


def far_kernel(hop, lists_ref, tiles_ref, got_ref, part_ref, *rest):
    last = hop == HOPS - 1
    if last:
        out_ref, acc, src, load, ring, sem = rest
    else:
        out_ref, sq_ref, acc, src, load, ring, sem = rest
    begin, run = add_groups(1, *parts_of(lists_ref), tiles_ref, src, acc, ring, sem)
    begin(0)
    got_copy = pltpu.make_async_copy(got_ref, src, load)
    got_copy.start()
    for step in range(1, DEPTH):
        begin(step)
    acc[...] = jnp.zeros_like(acc)
    got_copy.wait()
    run()
    pairs = []
    for p in range(PAIRS):
        u = part_ref[p] + fold(acc, p)
        pairs.append(u)
        if last:
            out_ref[p * BLK : (p + 1) * BLK] = u.astype(bf16)
        else:
            out_ref[p] = u
    total = pair_squares(pairs)
    if last:
        hi = total.astype(bf16).astype(f32)
        mid = (total - hi).astype(bf16).astype(f32)
        lo = total - hi - mid
        out_ref[PAIRS * BLK : PAIRS * BLK + 16] = jnp.concatenate([hi, mid], axis=0).astype(bf16)
        out_ref[PAIRS * BLK + 16 : PAIRS * BLK + 32] = jnp.concatenate([lo, jnp.zeros_like(lo)], axis=0).astype(bf16)
    else:
        sq_ref[...] = total


def early_kernel(x_ref, w_ref, *refs):
    h_refs, out_ref = refs[:-1], refs[-1]
    for p in range(PAIRS):
        total = jnp.zeros((BLK, BLK), f32)
        for k in range(HOPS):
            for j, shift in enumerate(SHIFTS):
                source = (x_ref[0] + NX - shift) % NX
                total = total + jnp.dot(h_refs[j][k, p], w_ref[k, source], preferred_element_type=f32)
        out_ref[p] = total


def final_kernel(x_ref, w_ref, early_ref, *refs):
    got_refs, out_ref = refs[:-1], refs[-1]
    total = jnp.zeros((BPD, BLK), f32)
    for got_ref in got_refs:
        a = got_ref[PAIRS * BLK : PAIRS * BLK + 16].astype(f32)
        b = got_ref[PAIRS * BLK + 16 : PAIRS * BLK + 32].astype(f32)
        total = total + (a[:BPD] + a[BPD:] + b[:BPD])
    columns = row_scale(total)
    for p in range(PAIRS):
        raw = jnp.zeros((BLK, BLK), f32)
        for j, shift in enumerate(SHIFTS):
            source = (x_ref[0] + NX - shift) % NX
            raw = raw + jnp.dot(got_refs[j][p * BLK : (p + 1) * BLK], w_ref[HOPS, source], preferred_element_type=f32)
        v = (early_ref[p] + raw * pair_scale(columns, p)).T
        out_ref[:, (2 * p) * BLK : (2 * p + 1) * BLK] = v[:WIDTH].astype(bf16)
        out_ref[:, (2 * p + 1) * BLK : (2 * p + 2) * BLK] = v[WIDTH:].astype(bf16)


def whole(space=VMEM):
    return pl.BlockSpec(memory_space=space)


def call(kernel, name, in_specs, outs, scratch=(), limit=24 << 20, flops=1 << 20, moved=1 << 20):
    shapes = [jax.ShapeDtypeStruct(dims, kind) for dims, kind, _ in outs]
    specs = [whole(space) for _, _, space in outs]
    single = len(outs) == 1
    return pl.pallas_call(
        kernel,
        name=name,
        out_shape=shapes[0] if single else shapes,
        in_specs=in_specs,
        out_specs=specs[0] if single else specs,
        scratch_shapes=list(scratch),
        compiler_params=pltpu.CompilerParams(vmem_limit_bytes=limit),
        cost_estimate=pl.CostEstimate(flops=flops, bytes_accessed=moved, transcendentals=0),
    )


def shift_by(value, axis, shift):
    size = lax.axis_size(axis)
    return lax.ppermute(value, axis, [(i, (i + shift) % size) for i in range(size)])


def slot_table(asked, start, base):
    mine = lax.dynamic_slice(asked, (0, *start, 0), (asked.shape[0], 1, base.shape[0], 1, 2)).reshape(asked.shape[0], base.shape[0], 2)
    odd = (mine & 1) ^ jnp.arange(2, dtype=jnp.int32)
    return (base[:, None] + (mine >> 1) + PAIRS * odd).reshape(-1)


def shards(features, tile_vals, tile_rows, tile_srcs, tile_count, needed, hop_noise, enc_weight):
    me = jnp.stack([lax.axis_index("y"), lax.axis_index("z"), lax.axis_index("core")]).astype(jnp.int32)
    x_index = lax.axis_index("x").astype(jnp.int32)
    x_only = x_index.reshape(1)
    noise = hop_noise.transpose(0, 2, 1)

    packed, squares = call(
        pack_kernel, "pack", [whole()],
        [((PAIRS, BLK, BLK), bf16, VMEM), ((BPD, BLK), f32, VMEM)],
    )(features.T)
    packed, squares, rows, srcs, count, enc_weight, needed = lax.optimization_barrier(
        (packed, squares, tile_rows.reshape(-1), tile_srcs.reshape(-1), tile_count, enc_weight, needed)
    )

    weights = lax.dynamic_slice_in_dim(enc_weight, x_index * WIDTH, WIDTH, axis=2).reshape(HOPS + 1, NX, WIDTH, WIDTH)
    nothing = jnp.zeros_like(weights)
    weights = jnp.concatenate(
        [jnp.concatenate([weights, nothing], axis=-1), jnp.concatenate([nothing, weights], axis=-1)], axis=-2
    )
    lists = call(
        order_kernel, "order", [whole(SMEM)] * 4,
        [((4 * SLOTS + 2 * MAXG + 16,), jnp.int32, SMEM)],
        [SMEM((2 * BUCKETS,), jnp.int32), SMEM((2 * BUCKETS,), jnp.int32)],
    )(me, rows, srcs, count)
    owned = None
    for hop in range(HOPS):
        last = hop == HOPS - 1
        totals = [squares] + [shift_by(squares, "x", shift) for shift in SHIFTS[1:]]
        wide = [((N_ROW, BLK, BLK), bf16, HBM)]
        if last:
            picked, owned = call(
                send_kernel, "send", [whole(SMEM)] * (1 + NZ) + [whole()] * (2 + NX), wide + [((2, PAIRS, BLK, BLK), bf16, VMEM)],
                [VMEM((BPD, BLK, BLK), bf16), VMEM((N_ROW, BLK, BLK), bf16), DMA((NY * NC,))],
                limit=MOST,
            )(me, *tables, packed, *totals, owned)
            spread = [owned] + [shift_by(owned, "x", shift) for shift in SHIFTS[1:]]
            got = lax.all_to_all(picked, ("y", "core", "z"), 0, 0, tiled=True)
        else:
            packed, owned = call(
                norm_kernel, "norm", [whole()] * (1 + NX),
                [((NZ, PAIRS, BLK, BLK), bf16, HBM), ((1, PAIRS, BLK, BLK), bf16, HBM)],
                [VMEM((PAIRS, BLK, BLK), bf16), DMA((NZ + 1,))],
                limit=NORM,
            )(packed, *totals)
            along = lax.all_to_all(packed, "z", 0, 0, tiled=True)
            needed, owned = lax.optimization_barrier((needed, owned))
            asked = lax.all_gather(needed.reshape(-1), ("y", "core"), axis=0)
            table = slot_table(asked.reshape(NY * NC, NY, NZ, NC, 2), (me[0], 0, me[2]), jnp.arange(NZ, dtype=jnp.int32) * BPD)
            at, table, asked, lists = lax.optimization_barrier((me, table, asked, lists))
            picked = call(
                pick_kernel, "pick", [whole(SMEM)] * 2 + [whole()], wide,
                [VMEM((NZ * BPD, BLK, BLK), bf16), VMEM((N_ROW, BLK, BLK), bf16), DMA((NY * NC,))],
                limit=MOST,
            )(at, table, along)
            picked, asked = lax.optimization_barrier((picked, asked))
            got = lax.all_to_all(picked, ("y", "core"), 0, 0, tiled=True)
            tables = [asked] + [shift_by(asked, "z", shift) for shift in ZSHIFTS[1:]]
        ring = [VMEM((DEPTH, STEP * GROUP, BLK, BLK), bf16), DMA((DEPTH, STEP * GROUP))]
        part = call(
            functools.partial(own_kernel, hop), "own", [whole(SMEM)] + [whole(HBM), whole(), whole(HBM)],
            [((PAIRS, BLK, BLK), f32, VMEM)],
            [VMEM((BUCKETS, BLK, BLK), f32), VMEM((PAIRS + 1, BLK, BLK), bf16), VMEM((WIDTH, BPD * BLK), f32)] + ring + [DMA(())],
            limit=FULL, flops=TPD * 2 * BLK**3, moved=4 << 20,
        )(lists, tile_vals, owned, noise)
        if not last:
            part, *tables = lax.optimization_barrier((part, *tables))
        if last:
            early = call(
                early_kernel, "early", [whole(SMEM)] + [whole()] * (1 + NX), [((PAIRS, BLK, BLK), f32, VMEM)]
            )(x_only, weights, *spread)
            early, part = lax.optimization_barrier((early, part))
        if last:
            outs = [((PAIRS * BLK + 32, BLK), bf16, VMEM)]
            more = []
        else:
            outs = [((PAIRS, BLK, BLK), f32, VMEM), ((BPD, BLK), f32, VMEM)]
            more = []
        result = call(
            functools.partial(far_kernel, hop), "far", [whole(SMEM)] + [whole(HBM), whole(HBM), whole()], outs,
            [VMEM((BUCKETS, BLK, BLK), f32), VMEM((N_ROW, BLK, BLK), bf16), DMA(())] + ring + more,
            limit=ROOM, flops=TPD * 2 * BLK**3, moved=8 << 20,
        )(lists, tile_vals, got, part)
        if not last:
            packed, squares = result
    tails = [result] + [shift_by(result, "x", shift) for shift in SHIFTS[1:]]
    return call(
        final_kernel, "final", [whole(SMEM)] + [whole()] * (2 + NX), [((WIDTH, BPD * BLK), bf16, VMEM)],
    )(x_only, weights, early, *tails).T


def solution(mesh):
    grid = Mesh(np.array(mesh.devices).reshape(NY, NZ, NC, NX), ("y", "z", "core", "x"))
    row = ("y", "z", "core")
    in_specs = (
        P(row, "x"),
        P(row, None, None),
        P(row, None),
        P(row, None),
        P(row),
        P(row, None, None),
        P(None, row, "x"),
        P(),
    )
    return jax.shard_map(shards, mesh=grid, in_specs=in_specs, out_specs=P(row, "x"), check_vma=False)
```

```python
import functools

import jax
import jax.numpy as jnp
import numpy as np
from jax import lax
from jax.experimental import pallas as pl
from jax.experimental.pallas import tpu as pltpu
from jax.sharding import Mesh, PartitionSpec as P

BLK = 128
BPD = 8
TPD = 160
PAIRS = BPD // 2
HOPS = 2
NY, NZ, NC, NX = 4, 8, 2, 4
WIDTH = 64
GROUP = 4
STEP = 4
BUCKETS = 2 * BPD
MAXG = TPD // GROUP + BUCKETS
SLOTS = MAXG * GROUP
SHIFTS = (0, 2, 1, 3)
N_ROW = NY * NZ * NC
ZSHIFTS = (0, 4, 3, 5, 2, 6, 1, 7)
DEPTH = 4
FULL = 63 << 20
MOST = 65_000_000
NORM = 24 << 20
ROOM = 63_600_000
EPS = 1e-06
bf16 = jnp.bfloat16
f32 = jnp.float32
VMEM = pltpu.VMEM
SMEM = pltpu.SMEM
HBM = pltpu.HBM
DMA = pltpu.SemaphoreType.DMA


def lane_low(shape):
    return lax.broadcasted_iota(jnp.int32, shape, len(shape) - 1) < WIDTH


def pair_squares(pair_values):
    total = jnp.zeros((BPD, BLK), f32)
    row = lax.broadcasted_iota(jnp.int32, (BPD, BLK), 0)
    half = lax.broadcasted_iota(jnp.int32, (BPD, BLK), 1) // WIDTH
    for p in range(PAIRS):
        v = pair_values[p]
        pick = jnp.where(row == 2 * p + half, 1.0, 0.0).astype(f32)
        total = total + lax.dot_general(
            pick, v * v, (((1,), (1,)), ((), ())),
            precision=lax.Precision.HIGHEST, preferred_element_type=f32,
        )
    return total


def row_scale(total):
    return (1.0 / jnp.sqrt(total + EPS)).T


def pair_scale(columns, p):
    return jnp.where(
        lane_low((BLK, BLK)),
        jnp.broadcast_to(columns[:, 2 * p : 2 * p + 1], (BLK, BLK)),
        jnp.broadcast_to(columns[:, 2 * p + 1 : 2 * p + 2], (BLK, BLK)),
    )


def swap_halves(v):
    return pltpu.roll(v, WIDTH, 1)


def stacked_pair(ref, p):
    first = ref[:, (2 * p) * BLK : (2 * p + 1) * BLK].astype(f32)
    second = ref[:, (2 * p + 1) * BLK : (2 * p + 2) * BLK].astype(f32)
    return jnp.concatenate([first, second], axis=0)


def pack_kernel(feat_ref, out_ref, sq_ref):
    rows = []
    for p in range(PAIRS):
        stacked = stacked_pair(feat_ref, p)
        out_ref[p] = stacked.T.astype(bf16)
        squares = stacked * stacked
        rows.append(jnp.sum(squares[:WIDTH], axis=0, keepdims=True))
        rows.append(jnp.sum(squares[WIDTH:], axis=0, keepdims=True))
    sq_ref[...] = jnp.concatenate(rows, axis=0)


def total_of(refs):
    total = refs[0][...]
    for ref in refs[1:]:
        total = total + ref[...]
    return total


def swapped(v):
    return jnp.concatenate([v[:, WIDTH:], v[:, :WIDTH]], axis=1)


def norm_kernel(raw_ref, *refs):
    out_ref, own_ref, buf, sem = refs[NX:]
    columns = row_scale(total_of(refs[:NX]))
    copies = []
    for p in range(PAIRS):
        v = (raw_ref[p].astype(f32) * pair_scale(columns, p)).astype(bf16)
        buf[p] = v
    for z in range(NZ):
        copy = pltpu.make_async_copy(buf, out_ref.at[z], sem.at[z])
        copy.start()
        copies.append(copy)
    copies.append(pltpu.make_async_copy(buf, own_ref.at[0], sem.at[NZ]))
    copies[-1].start()
    for copy in copies:
        copy.wait()


def write_slabs(me_ref, slab_of, out_ref, buf, sem):
    mine = me_ref[0] * NC + me_ref[2]
    copies = []
    for dest in range(NY * NC):
        for j in range(NZ):
            z, slab = slab_of(dest, j)
            buf[dest * NZ + z] = slab

        @pl.when(mine == dest)
        def _():
            buf[dest * NZ + me_ref[1]] = jnp.zeros((BLK, BLK), bf16)

        copy = pltpu.make_async_copy(
            buf.at[pl.ds(dest * NZ, NZ)], out_ref.at[pl.ds(dest * NZ, NZ)], sem.at[dest]
        )
        copy.start()
        copies.append(copy)
    for copy in copies:
        copy.wait()


def pick_kernel(me_ref, idx_ref, z_ref, out_ref, slots, buf, sem):
    for z in range(NZ):
        for p in range(PAIRS):
            v = z_ref[z, p]
            slots[z * BPD + p] = v
            slots[z * BPD + PAIRS + p] = swapped(v)
    mask = lane_low((BLK, BLK))

    def slab_of(dest, j):
        i = 2 * (dest * NZ + j)
        return j, jnp.where(mask, slots[idx_ref[i]], slots[idx_ref[i + 1]])

    write_slabs(me_ref, slab_of, out_ref, buf, sem)


def send_kernel(me_ref, *refs):
    asked_refs, raw_ref, refs = refs[:NZ], refs[NZ], refs[NZ + 1 :]
    before_ref, out_ref, own_ref, slots, buf, sem = refs[NX:]
    columns = row_scale(total_of(refs[:NX]))
    own_ref[0] = before_ref[0]
    for p in range(PAIRS):
        v = (raw_ref[p] * pair_scale(columns, p)).astype(bf16)
        own_ref[1, p] = v
        slots[p] = v
        slots[PAIRS + p] = swapped(v)
    mask = lane_low((BLK, BLK))
    at = ((me_ref[0] * NZ + me_ref[1]) * NC + me_ref[2]) * 2

    def slab_of(dest, j):
        z = (me_ref[1] + NZ - ZSHIFTS[j]) & (NZ - 1)
        first = asked_refs[j][dest, at]
        second = asked_refs[j][dest, at + 1]
        low = (first >> 1) | ((first & 1) << 2)
        high = ((second >> 1) | ((second & 1) << 2)) ^ PAIRS
        return z, jnp.where(mask, slots[low], slots[high])

    write_slabs(me_ref, slab_of, out_ref, buf, sem)


class Part:
    def __init__(self, ref, start):
        self.ref, self.start = ref, start

    def __getitem__(self, i):
        return self.ref[self.start + i]

    def __setitem__(self, i, value):
        self.ref[self.start + i] = value


def parts_of(ref):
    return [Part(ref, start) for start in (0, 2 * SLOTS, 4 * SLOTS, 4 * SLOTS + 2 * MAXG)]


def order_kernel(me_ref, rows_ref, srcs_ref, count_ref, lists_ref, fill, begin):
    tile_ref, slab_ref, into_ref, groups_ref = parts_of(lists_ref)
    count = count_ref[0]
    empty = (me_ref[0] * NC + me_ref[2]) * NZ + me_ref[1]

    @pl.loop(0, SLOTS // 8)
    def _(i):
        for j in range(8):
            tile_ref[i * 8 + j] = 0
            tile_ref[SLOTS + i * 8 + j] = 0
            slab_ref[i * 8 + j] = PAIRS
            slab_ref[SLOTS + i * 8 + j] = empty

    @pl.loop(0, 2 * MAXG)
    def _(i):
        into_ref[i] = 0

    for b in range(2 * BUCKETS):
        fill[b] = 0

    def bucket_of(t):
        s = srcs_ref[t]
        return jnp.where(s < BPD, 0, BUCKETS) + rows_ref[t] * 2 + (s & 1)

    @pl.loop(0, count)
    def _(t):
        b = bucket_of(t)
        fill[b] = fill[b] + 1

    for kind in range(2):
        def place(b, group):
            size = (fill[kind * BUCKETS + b] + GROUP - 1) // GROUP
            begin[kind * BUCKETS + b] = (kind * MAXG + group) * GROUP

            @pl.loop(0, size)
            def _(i):
                into_ref[kind * MAXG + group + i] = b

            return group + size

        groups_ref[kind] = lax.fori_loop(0, BUCKETS, place, jnp.int32(0))

    @pl.loop(0, count)
    def _(t):
        b = bucket_of(t)
        at = begin[b]
        begin[b] = at + 1
        s = srcs_ref[t]
        tile_ref[at] = t
        o = (s - BPD) >> 1
        far_slab = (((o >> 4) * NC) + (o & 1)) * NZ + ((o >> 1) & (NZ - 1))
        slab_ref[at] = jnp.where(s < BPD, s >> 1, far_slab)


def add_groups(kind, tile_ref, slab_ref, into_ref, groups_ref, tiles_ref, src, acc, ring, sem):
    steps = (groups_ref[kind] + STEP - 1) // STEP

    def copies(step):
        slot = step % DEPTH
        first = (kind * MAXG + STEP * step) * GROUP
        return [
            pltpu.make_async_copy(tiles_ref.at[tile_ref[first + j]], ring.at[slot, j], sem.at[slot, j])
            for j in range(STEP * GROUP)
        ]

    def begin(step):
        @pl.when(step < steps)
        def _():
            for copy in copies(step):
                copy.start()

    def run(step, carry):
        slot = step % DEPTH
        group = kind * MAXG + STEP * step
        for copy in copies(step):
            copy.wait()
        parts = []
        for h in range(STEP):
            left = jnp.concatenate([ring[slot, h * GROUP + j] for j in range(GROUP)], axis=1)
            right = jnp.concatenate([src[slab_ref[(group + h) * GROUP + j]] for j in range(GROUP)], axis=0)
            parts.append(jnp.dot(left, right, preferred_element_type=f32))
        for h in range(STEP):
            acc[into_ref[group + h]] += parts[h]
        begin(step + DEPTH)
        return carry

    return begin, lambda: lax.fori_loop(0, steps, run, 0)


def fold(acc, p):
    return jnp.where(
        lane_low((BLK, BLK)),
        acc[4 * p] + swap_halves(acc[4 * p + 1]),
        swap_halves(acc[4 * p + 2]) + acc[4 * p + 3],
    )


def own_kernel(hop, lists_ref, tiles_ref, own_ref, noise_ref, part_ref, acc, src, noise, ring, sem, load):
    begin, run = add_groups(0, *parts_of(lists_ref), tiles_ref, src, acc, ring, sem)
    for step in range(DEPTH):
        begin(step)
    noise_copy = pltpu.make_async_copy(noise_ref.at[hop], noise, load)
    noise_copy.start()
    acc[...] = jnp.zeros_like(acc)
    src[0:PAIRS] = own_ref[hop]
    src[PAIRS] = jnp.zeros((BLK, BLK), bf16)
    run()
    noise_copy.wait()
    for p in range(PAIRS):
        part_ref[p] = stacked_pair(noise, p).T + fold(acc, p)


def far_kernel(hop, lists_ref, tiles_ref, got_ref, part_ref, *rest):
    last = hop == HOPS - 1
    if last:
        out_ref, acc, ring, sem = rest
    else:
        out_ref, sq_ref, acc, ring, sem = rest
    begin, run = add_groups(1, *parts_of(lists_ref), tiles_ref, got_ref, acc, ring, sem)
    for step in range(DEPTH):
        begin(step)
    acc[...] = jnp.zeros_like(acc)
    run()
    pairs = []
    for p in range(PAIRS):
        u = part_ref[p] + fold(acc, p)
        pairs.append(u)
        if last:
            out_ref[p * BLK : (p + 1) * BLK] = u.astype(bf16)
        else:
            out_ref[p] = u
    total = pair_squares(pairs)
    if last:
        hi = total.astype(bf16).astype(f32)
        mid = (total - hi).astype(bf16).astype(f32)
        lo = total - hi - mid
        out_ref[PAIRS * BLK : PAIRS * BLK + 16] = jnp.concatenate([hi, mid], axis=0).astype(bf16)
        out_ref[PAIRS * BLK + 16 : PAIRS * BLK + 32] = jnp.concatenate([lo, jnp.zeros_like(lo)], axis=0).astype(bf16)
    else:
        sq_ref[...] = total


def early_kernel(x_ref, w_ref, *refs):
    h_refs, out_ref = refs[:-1], refs[-1]
    for p in range(PAIRS):
        total = jnp.zeros((BLK, BLK), f32)
        for k in range(HOPS):
            for j, shift in enumerate(SHIFTS):
                source = (x_ref[0] + NX - shift) % NX
                total = total + jnp.dot(h_refs[j][k, p], w_ref[k, source], preferred_element_type=f32)
        out_ref[p] = total


def final_kernel(x_ref, w_ref, early_ref, *refs):
    got_refs, out_ref = refs[:-1], refs[-1]
    total = jnp.zeros((BPD, BLK), f32)
    for got_ref in got_refs:
        a = got_ref[PAIRS * BLK : PAIRS * BLK + 16].astype(f32)
        b = got_ref[PAIRS * BLK + 16 : PAIRS * BLK + 32].astype(f32)
        total = total + (a[:BPD] + a[BPD:] + b[:BPD])
    columns = row_scale(total)
    for p in range(PAIRS):
        raw = jnp.zeros((BLK, BLK), f32)
        for j, shift in enumerate(SHIFTS):
            source = (x_ref[0] + NX - shift) % NX
            raw = raw + jnp.dot(got_refs[j][p * BLK : (p + 1) * BLK], w_ref[HOPS, source], preferred_element_type=f32)
        v = (early_ref[p] + raw * pair_scale(columns, p)).T
        out_ref[:, (2 * p) * BLK : (2 * p + 1) * BLK] = v[:WIDTH].astype(bf16)
        out_ref[:, (2 * p + 1) * BLK : (2 * p + 2) * BLK] = v[WIDTH:].astype(bf16)


def whole(space=VMEM):
    return pl.BlockSpec(memory_space=space)


def call(kernel, name, in_specs, outs, scratch=(), limit=24 << 20, flops=1 << 20, moved=1 << 20):
    shapes = [jax.ShapeDtypeStruct(dims, kind) for dims, kind, _ in outs]
    specs = [whole(space) for _, _, space in outs]
    single = len(outs) == 1
    return pl.pallas_call(
        kernel,
        name=name,
        out_shape=shapes[0] if single else shapes,
        in_specs=in_specs,
        out_specs=specs[0] if single else specs,
        scratch_shapes=list(scratch),
        compiler_params=pltpu.CompilerParams(vmem_limit_bytes=limit),
        cost_estimate=pl.CostEstimate(flops=flops, bytes_accessed=moved, transcendentals=0),
    )


def shift_by(value, axis, shift):
    size = lax.axis_size(axis)
    return lax.ppermute(value, axis, [(i, (i + shift) % size) for i in range(size)])


def slot_table(asked, start, base):
    mine = lax.dynamic_slice(asked, (0, *start, 0), (asked.shape[0], 1, base.shape[0], 1, 2)).reshape(asked.shape[0], base.shape[0], 2)
    odd = (mine & 1) ^ jnp.arange(2, dtype=jnp.int32)
    return (base[:, None] + (mine >> 1) + PAIRS * odd).reshape(-1)


def shards(features, tile_vals, tile_rows, tile_srcs, tile_count, needed, hop_noise, enc_weight):
    me = jnp.stack([lax.axis_index("y"), lax.axis_index("z"), lax.axis_index("core")]).astype(jnp.int32)
    x_index = lax.axis_index("x").astype(jnp.int32)
    x_only = x_index.reshape(1)
    noise = hop_noise.transpose(0, 2, 1)

    packed, squares = call(
        pack_kernel, "pack", [whole()],
        [((PAIRS, BLK, BLK), bf16, VMEM), ((BPD, BLK), f32, VMEM)],
    )(features.T)
    packed, squares, rows, srcs, count, enc_weight, needed = lax.optimization_barrier(
        (packed, squares, tile_rows.reshape(-1), tile_srcs.reshape(-1), tile_count, enc_weight, needed)
    )

    weights = lax.dynamic_slice_in_dim(enc_weight, x_index * WIDTH, WIDTH, axis=2).reshape(HOPS + 1, NX, WIDTH, WIDTH)
    nothing = jnp.zeros_like(weights)
    weights = jnp.concatenate(
        [jnp.concatenate([weights, nothing], axis=-1), jnp.concatenate([nothing, weights], axis=-1)], axis=-2
    )
    lists = call(
        order_kernel, "order", [whole(SMEM)] * 4,
        [((4 * SLOTS + 2 * MAXG + 16,), jnp.int32, SMEM)],
        [SMEM((2 * BUCKETS,), jnp.int32), SMEM((2 * BUCKETS,), jnp.int32)],
    )(me, rows, srcs, count)
    owned = None
    for hop in range(HOPS):
        last = hop == HOPS - 1
        totals = [squares] + [shift_by(squares, "x", shift) for shift in SHIFTS[1:]]
        wide = [((N_ROW, BLK, BLK), bf16, HBM)]
        if last:
            picked, owned = call(
                send_kernel, "send", [whole(SMEM)] * (1 + NZ) + [whole()] * (2 + NX), wide + [((2, PAIRS, BLK, BLK), bf16, VMEM)],
                [VMEM((BPD, BLK, BLK), bf16), VMEM((N_ROW, BLK, BLK), bf16), DMA((NY * NC,))],
                limit=NORM,
            )(me, *tables, packed, *totals, owned)
            spread = [owned] + [shift_by(owned, "x", shift) for shift in SHIFTS[1:]]
            got = lax.all_to_all(picked, ("y", "core", "z"), 0, 0, tiled=True)
        else:
            packed, owned = call(
                norm_kernel, "norm", [whole()] * (1 + NX),
                [((NZ, PAIRS, BLK, BLK), bf16, HBM), ((1, PAIRS, BLK, BLK), bf16, HBM)],
                [VMEM((PAIRS, BLK, BLK), bf16), DMA((NZ + 1,))],
                limit=NORM,
            )(packed, *totals)
            along = lax.all_to_all(packed, "z", 0, 0, tiled=True)
            needed, owned = lax.optimization_barrier((needed, owned))
            asked = lax.all_gather(needed.reshape(-1), ("y", "core"), axis=0)
            table = slot_table(asked.reshape(NY * NC, NY, NZ, NC, 2), (me[0], 0, me[2]), jnp.arange(NZ, dtype=jnp.int32) * BPD)
            at, table, asked, lists = lax.optimization_barrier((me, table, asked, lists))
            picked = call(
                pick_kernel, "pick", [whole(SMEM)] * 2 + [whole()], wide,
                [VMEM((NZ * BPD, BLK, BLK), bf16), VMEM((N_ROW, BLK, BLK), bf16), DMA((NY * NC,))],
                limit=NORM,
            )(at, table, along)
            picked, asked = lax.optimization_barrier((picked, asked))
            got = lax.all_to_all(picked, ("y", "core"), 0, 0, tiled=True)
            tables = [asked] + [shift_by(asked, "z", shift) for shift in ZSHIFTS[1:]]
        ring = [VMEM((DEPTH, STEP * GROUP, BLK, BLK), bf16), DMA((DEPTH, STEP * GROUP))]
        part = call(
            functools.partial(own_kernel, hop), "own", [whole(SMEM)] + [whole(HBM), whole(), whole(HBM)],
            [((PAIRS, BLK, BLK), f32, VMEM)],
            [VMEM((BUCKETS, BLK, BLK), f32), VMEM((PAIRS + 1, BLK, BLK), bf16), VMEM((WIDTH, BPD * BLK), f32)] + ring + [DMA(())],
            limit=FULL, flops=TPD * 2 * BLK**3, moved=4 << 20,
        )(lists, tile_vals, owned, noise)
        if not last:
            part, *tables = lax.optimization_barrier((part, *tables))
        if last:
            early = call(
                early_kernel, "early", [whole(SMEM)] + [whole()] * (1 + NX), [((PAIRS, BLK, BLK), f32, VMEM)]
            )(x_only, weights, *spread)
            early, part = lax.optimization_barrier((early, part))
        if last:
            outs = [((PAIRS * BLK + 32, BLK), bf16, VMEM)]
            more = []
        else:
            outs = [((PAIRS, BLK, BLK), f32, VMEM), ((BPD, BLK), f32, VMEM)]
            more = []
        result = call(
            functools.partial(far_kernel, hop), "far", [whole(SMEM)] + [whole(HBM), whole(), whole()], outs,
            [VMEM((BUCKETS, BLK, BLK), f32)] + ring + more,
            limit=ROOM, flops=TPD * 2 * BLK**3, moved=8 << 20,
        )(lists, tile_vals, got, part)
        if not last:
            packed, squares = result
    tails = [result] + [shift_by(result, "x", shift) for shift in SHIFTS[1:]]
    return call(
        final_kernel, "final", [whole(SMEM)] + [whole()] * (2 + NX), [((WIDTH, BPD * BLK), bf16, VMEM)],
    )(x_only, weights, early, *tails).T


def solution(mesh):
    grid = Mesh(np.array(mesh.devices).reshape(NY, NZ, NC, NX), ("y", "z", "core", "x"))
    row = ("y", "z", "core")
    in_specs = (
        P(row, "x"),
        P(row, None, None),
        P(row, None),
        P(row, None),
        P(row),
        P(row, None, None),
        P(None, row, "x"),
        P(),
    )
    return jax.shard_map(shards, mesh=grid, in_specs=in_specs, out_specs=P(row, "x"), check_vma=False)
```
